32 devices in a mesh: rows: 8 (over z, y), heads: 4 (over x, core).
Axes of the slice: x: 2, y: 2, z: 4, core: 2. Of those that a mesh axis runs over, the one named last changes fastest.
Arguments:
- frames: bfloat16 [24, 800, 640], P('rows'), may hold values from -6 to 6
- segment_ids: int32 [24, 800], P('rows'), may hold values from -1 to 3, as said below
- cotangent: bfloat16 [24, 800, 640], P('rows'), may hold values from -6 to 6
- query_weight: bfloat16 [640, 768], P(None, 'heads'), may hold values from -0.25 to 0.25
- query_bias: float32 [768], P('heads'), may hold values from -3 to 3
- key_weight: bfloat16 [640, 768], P(None, 'heads'), may hold values from -0.25 to 0.25
- value_weight: bfloat16 [640, 768], P(None, 'heads'), may hold values from -0.25 to 0.25
- value_bias: float32 [768], P('heads'), may hold values from -3 to 3
- output_weight: bfloat16 [768, 640], P('heads'), may hold values from -2 to 2
- output_bias: float32 [640], replicated, may hold values from -3 to 3
- first_gain: float32 [640], replicated, may hold values from 0.1 to 1.9
- first_shift: float32 [640], replicated, may hold values from -3 to 3
- inner_weight: bfloat16 [640, 3072], P(None, 'heads'), may hold values from -0.25 to 0.25
- inner_bias: float32 [3072], P('heads'), may hold values from -3 to 3
- outer_weight: bfloat16 [3072, 640], P('heads'), may hold values from -0.1875 to 0.1875
- outer_bias: float32 [640], replicated, may hold values from -3 to 3
- second_gain: float32 [640], replicated, may hold values from 0.1 to 1.9
- second_shift: float32 [640], replicated, may hold values from -3 to 3
Outputs:
- layer_out: bfloat16 [24, 800, 640], P('rows')
- frames_grad: bfloat16 [24, 800, 640], P('rows')
- query_grad: float32 [640, 768], P(None, 'heads')
- querybias_grad: float32 [768], P('heads')
- key_grad: float32 [640, 768], P(None, 'heads')
- value_grad: float32 [640, 768], P(None, 'heads')
- valuebias_grad: float32 [768], P('heads')
- output_grad: float32 [768, 640], P('heads')
- outputbias_grad: float32 [640], replicated
- firstgain_grad: float32 [640], replicated
- firstshift_grad: float32 [640], replicated
- inner_grad: float32 [640, 3072], P(None, 'heads')
- innerbias_grad: float32 [3072], P('heads')
- outer_grad: float32 [3072, 640], P('heads')
- outerbias_grad: float32 [640], replicated
- secondgain_grad: float32 [640], replicated
- secondshift_grad: float32 [640], replicated
The draws below stay inside these ranges and needn't reach their ends.
Inputs may be any that keep to these rules, and one draw needn't show every extreme that they name: `segment_ids`: along each row the ids run 0, 1, 2, 3 in order, each segment nonempty, and the row ends with 1 to 200 pad frames of id -1.
All inputs are finite; a program needn't handle non-finite values.
Results may differ from the reference program's by a relative error of at most 0.024.
Values may be sent and summed in bfloat16 or wider, within the bound.
No kernel may reach another device: no remote copies, remote signals or barrier semaphores. Data moves between devices by JAX's collectives and lax.ppermute only.
A program may use at most 192 MiB of HBM per device.

```python
import jax
import jax.numpy as jnp
from jax import lax

D = 640
HEAD_SLOTS = 12
HEADS_LIVE = 10
HEAD_DIM = 64
FF_SLOTS = 3072
FF_LIVE = 2240
LEN = 800
ROWS = 24
N_HEADS = 4


def draw_segment_ids(key, part):
    border_key, padding_key = jax.random.split(key)
    stride = LEN // 8
    starts = jnp.arange(3, dtype=jnp.int32) * stride
    borders = starts[None, :] + jax.random.randint(border_key, (ROWS, 3), 1, stride + 1, dtype=jnp.int32)
    padding = jax.random.randint(padding_key, (ROWS, 1), 1, LEN // 4 + 1, dtype=jnp.int32)
    places = jnp.arange(LEN, dtype=jnp.int32)
    labels = jnp.sum((places[None, :, None] >= borders[:, None, :]).astype(jnp.int32), axis=-1)
    return jnp.where(places[None, :] >= LEN - padding, -1, labels).astype(jnp.int32)


def steps_of(stream_key, shape, shards, low, largest):
    loudness = 1.0
    for dim, blocks in shards:
        steps = jax.random.uniform(jax.random.fold_in(jax.random.fold_in(stream_key, 6), dim), (blocks,), jnp.float32, low / len(shards), largest / len(shards))
        loudness = loudness * jnp.repeat(jnp.exp(steps), shape[dim] // blocks).reshape((-1,) + (1,) * (len(shape) - 1 - dim))
    return loudness


def centred(own_key, shape, deviation, bound, cuts=(), kind=jnp.bfloat16):
    result = deviation * jax.random.normal(own_key, shape, jnp.float32)
    if cuts:
        result = result * steps_of(own_key, shape, cuts, -0.22, 0.18)
    return jnp.clip(result, -bound, bound).astype(kind)


def setup_inputs(seed: int = 0) -> dict:
    splits = jax.random.split(jax.random.key(seed), 19)
    return {
        "frames": centred(splits[0], (ROWS, LEN, D), 1.0, 6.0, ((0, 8),)),
        "segment_ids": draw_segment_ids(jax.random.fold_in(splits[18], 71), 0),
        "cotangent": centred(splits[2], (ROWS, LEN, D), 1.0, 6.0, ((0, 8),)),
        "query_weight": centred(splits[3], (D, HEAD_SLOTS * HEAD_DIM), D ** -0.5, 0.25, ((1, 4),)),
        "query_bias": centred(splits[4], (HEAD_SLOTS * HEAD_DIM,), 0.5, 3.0, ((0, 4),), jnp.float32),
        "key_weight": centred(splits[5], (D, HEAD_SLOTS * HEAD_DIM), D ** -0.5, 0.25, ((1, 4),)),
        "value_weight": centred(splits[6], (D, HEAD_SLOTS * HEAD_DIM), D ** -0.5, 0.25, ((1, 4),)),
        "value_bias": centred(splits[7], (HEAD_SLOTS * HEAD_DIM,), 0.5, 3.0, ((0, 4),), jnp.float32),
        "output_weight": centred(splits[8], (HEAD_SLOTS * HEAD_DIM, D), HEADS_LIVE ** -0.5, 2.0, ((0, 4),)),
        "output_bias": centred(splits[9], (D,), 0.5, 3.0, (), jnp.float32),
        "first_gain": jnp.clip(1.0 + 0.18 * jax.random.normal(splits[10], (D,), jnp.float32), 0.1, 1.9),
        "first_shift": centred(splits[11], (D,), 0.5, 3.0, (), jnp.float32),
        "inner_weight": centred(splits[12], (D, FF_SLOTS), D ** -0.5, 0.25, ((1, 4),)),
        "inner_bias": centred(splits[13], (FF_SLOTS,), 0.5, 3.0, ((0, 4),), jnp.float32),
        "outer_weight": centred(splits[14], (FF_SLOTS, D), (FF_LIVE // 2) ** -0.5, 0.1875, ((0, 4),)),
        "outer_bias": centred(splits[15], (D,), 0.5, 3.0, (), jnp.float32),
        "second_gain": jnp.clip(1.0 + 0.18 * jax.random.normal(splits[16], (D,), jnp.float32), 0.1, 1.9),
        "second_shift": centred(splits[17], (D,), 0.5, 3.0, (), jnp.float32),
    }


@jax.custom_vjp
def low(v):
    return lax.optimization_barrier(v.astype(jnp.bfloat16)).astype(jnp.float32)

@jax.custom_vjp
def low_back(v):
    return v

def low_keep(v):
    return (low(v), None)

def low_pass(kept, grad):
    return (grad,)

def back_keep(v):
    return (v, None)

def back_low(kept, grad):
    return (low(grad),)
low.defvjp(low_keep, low_pass)
low_back.defvjp(back_keep, back_low)
precise = lax.Precision.HIGHEST
norm_eps = 1e-05

def live_masks():
    per_group = HEAD_SLOTS // N_HEADS
    cells_group = FF_SLOTS // N_HEADS
    slots = jnp.arange(HEAD_SLOTS, dtype=jnp.int32)
    counts = HEADS_LIVE // N_HEADS + (slots // per_group < HEADS_LIVE % N_HEADS).astype(jnp.int32)
    head_live = (slots % per_group < counts).astype(jnp.float32)
    cells = jnp.arange(FF_SLOTS, dtype=jnp.int32)
    owned = HEADS_LIVE // N_HEADS + (cells // cells_group < HEADS_LIVE % N_HEADS).astype(jnp.int32)
    hidden_live = (cells % cells_group < owned * (FF_LIVE // HEADS_LIVE)).astype(jnp.float32)
    return (head_live, hidden_live)

def layer_norm(value, gain, shift):
    centre = value - lax.optimization_barrier(jnp.mean(value, axis=-1, keepdims=True))
    spread_sq = lax.optimization_barrier(jnp.mean(centre * centre, axis=-1, keepdims=True))
    return centre * lax.rsqrt(spread_sq + norm_eps) * gain + shift

def one_row(params, row_frames, row_ids):
    query_weight, query_bias, key_weight, value_weight, value_bias, output_weight, output_bias, first_gain, first_shift, inner_weight, inner_bias, outer_weight, outer_bias, second_gain, second_shift = params
    head_live, hidden_live = live_masks()
    output_weight = output_weight * jnp.repeat(head_live, HEAD_DIM)[:, None]
    outer_weight = outer_weight * hidden_live[:, None]
    head_shape = (LEN, HEAD_SLOTS, HEAD_DIM)
    queries = low(low_back(jnp.dot(row_frames, query_weight, precision=precise) + query_bias)).reshape(head_shape)
    keys_all = low(low_back(jnp.dot(row_frames, key_weight, precision=precise))).reshape(head_shape)
    values_all = low(low_back(jnp.dot(row_frames, value_weight, precision=precise) + value_bias)).reshape(head_shape)
    scores = low_back(jnp.einsum('qhd,khd->hqk', queries, keys_all, precision=precise) * HEAD_DIM ** (-0.5))
    allowed = (row_ids[:, None] == row_ids[None, :])[None]
    scores = jnp.where(allowed, scores, -1e+30)
    probs = low(jax.nn.softmax(scores, axis=-1))
    context = low(low_back(jnp.einsum('hqk,khd->qhd', probs, values_all, precision=precise)))
    context = context.reshape(LEN, HEAD_SLOTS * HEAD_DIM)
    parts = jnp.einsum('tgk,gkd->gtd', context.reshape(LEN, N_HEADS, -1), output_weight.reshape(N_HEADS, -1, D), precision=precise)
    attended = low_back(lax.optimization_barrier(jnp.sum(low(parts), axis=0))) + output_bias
    normed = layer_norm(row_frames + attended, first_gain, first_shift)
    inner_pre = low_back(jnp.dot(low(normed), inner_weight, precision=precise) + inner_bias)
    active = low(jax.nn.gelu(inner_pre, approximate=False))
    parts_two = jnp.einsum('tgc,gcd->gtd', active.reshape(LEN, N_HEADS, -1), outer_weight.reshape(N_HEADS, -1, D), precision=precise)
    mixed = low_back(lax.optimization_barrier(jnp.sum(low(parts_two), axis=0))) + outer_bias
    live_rows = (row_ids >= 0).astype(jnp.float32)[:, None]
    return layer_norm(normed + mixed, second_gain, second_shift) * live_rows

def forward(params, frames_in, segment_ids):

    def step(carried, row_pair):
        return (carried, jax.checkpoint(one_row)(params, row_pair[0], row_pair[1]))
    unused, stacked = lax.scan(step, jnp.float32(0.0), (frames_in, segment_ids))
    return stacked

def reference(frames, segment_ids, cotangent, query_weight, query_bias, key_weight, value_weight, value_bias, output_weight, output_bias, first_gain, first_shift, inner_weight, inner_bias, outer_weight, outer_bias, second_gain, second_shift):
    params = tuple((member.astype(jnp.float32) for member in (query_weight, query_bias, key_weight, value_weight, value_bias, output_weight, output_bias, first_gain, first_shift, inner_weight, inner_bias, outer_weight, outer_bias, second_gain, second_shift)))

    def run(params_in, frames_in):
        return forward(params_in, frames_in, segment_ids)
    layer_out, pullback = jax.vjp(run, params, frames.astype(jnp.float32))
    grads, frames_grad = pullback(cotangent.astype(jnp.float32))
    return (layer_out.astype(jnp.bfloat16), frames_grad.astype(jnp.bfloat16), grads[0], grads[1], grads[2], grads[3], grads[4], grads[5], grads[6], grads[7], grads[8], grads[9], grads[10], grads[11], grads[12], grads[13], grads[14])
```

```python
import math

import jax
import jax.numpy as jnp
from jax import lax
from jax.experimental import pallas as pl
from jax.experimental.pallas import tpu as pltpu
from jax.sharding import PartitionSpec as P

HEADS_LIVE = 10
HEAD_DIM = 64
FF_LIVE = 2240
PAD_HEAD = 128
SEGMENTS = 5
MASK_STEP = -(2.0**30)
norm_eps = 1e-05
f32 = jnp.float32
bf16 = jnp.bfloat16


def dot(a, b, ca, cb):
    return lax.dot_general(a, b, (((ca,), (cb,)), ((), ())), preferred_element_type=f32)


def three_parts(value):
    high = value.astype(bf16).astype(f32)
    middle = (value - high).astype(bf16).astype(f32)
    return high, middle, value - high - middle


def feature_rows(base, value):
    high, middle, low = three_parts(-value)
    row = lax.broadcasted_iota(jnp.int32, base.shape, 0)
    base = jnp.where(row == SEGMENTS, high, base)
    base = jnp.where(row == SEGMENTS + 1, middle, base)
    return jnp.where(row == SEGMENTS + 2, low, base).astype(bf16)


def attend_kernel(
    place, block_ref, row_ref, qkv_ref, out_ref, qbias_ref, vbias_ref, keyf_ref, queryf_ref,
    sum_ref, total_ref, query_ref, key_ref, value_ref, context_ref,
):
    step = pl.program_id(0)
    per_row, live = place[1], place[2]
    row_now = (place[0] + step) // per_row
    row_before = (place[0] + step - 1) // per_row
    length = row_ref.shape[1]
    width = qbias_ref.shape[0]
    heads = width // HEAD_DIM

    @pl.when(jnp.logical_or(step == 0, row_now != row_before))
    def _():
        frames = row_ref[0]
        keys = dot(frames, qkv_ref[width : 2 * width], 1, 1).astype(bf16)
        values = (dot(frames, qkv_ref[2 * width : 3 * width], 1, 1) + vbias_ref[...]).astype(bf16)
        features = keyf_ref[0]
        for head in range(heads):
            cut = slice(head * HEAD_DIM, (head + 1) * HEAD_DIM)
            key_ref[0, head * length : (head + 1) * length] = jnp.concatenate(
                [keys[:, cut], features], axis=1
            )
            value_ref[0, head * length : (head + 1) * length] = jnp.concatenate(
                [values[:, cut], features], axis=1
            )

    queries = (dot(qkv_ref[0:width], block_ref[0], 1, 1) + qbias_ref[...]).astype(bf16)
    queries = queries * jnp.asarray(HEAD_DIM**-0.5, bf16)
    for head in range(heads):
        query_ref[0, head * PAD_HEAD : head * PAD_HEAD + HEAD_DIM] = queries[
            head * HEAD_DIM : (head + 1) * HEAD_DIM
        ]
        query_ref[0, head * PAD_HEAD + HEAD_DIM : (head + 1) * PAD_HEAD] = queryf_ref[0]
    context_ref[...] = jnp.zeros_like(context_ref)

    def one_head(head, carry):
        keys = key_ref[0, pl.ds(pl.multiple_of(head * length, 16), length)]
        values = value_ref[0, pl.ds(pl.multiple_of(head * length, 16), length)]
        start = pl.multiple_of(head * PAD_HEAD, PAD_HEAD)
        scores = dot(keys, query_ref[0, pl.ds(start, PAD_HEAD)], 1, 0)
        highest = jnp.max(scores, axis=0, keepdims=True)
        probs = jnp.exp(scores - highest).astype(bf16)
        mixed = dot(values, probs, 0, 0)
        total = mixed[HEAD_DIM + SEGMENTS : HEAD_DIM + SEGMENTS + 1]
        context = mixed[0:HEAD_DIM] / total
        context_ref[0, pl.ds(pl.multiple_of(head * HEAD_DIM, HEAD_DIM), HEAD_DIM)] = context.astype(bf16)
        base = queryf_ref[0, 0:16].astype(f32)
        query_ref[0, pl.ds(start + HEAD_DIM, 16)] = feature_rows(base, highest + jnp.log(total))
        return carry

    lax.fori_loop(0, live, one_head, 0)
    total_ref[0] = sum_ref[0] + dot(context_ref[0], out_ref[...], 0, 0)


def attend_back_kernel(
    place, block_ref, row_ref, qkv_ref, out_ref, query_ref, key_ref, value_ref, context_ref,
    grad_ref, blocksum_ref, rowsum_ref,
    gradw_ref, qbias_ref, vbias_ref, blockout_ref, rowout_ref,
    weight_acc, dkey, dvalue, picked, dcontext, dquery,
):
    step = pl.program_id(0)
    steps = pl.num_programs(0)
    per_row, live = place[1], place[2]
    row_now = (place[0] + step) // per_row
    row_before = (place[0] + step - 1) // per_row
    row_after = (place[0] + step + 1) // per_row
    length = row_ref.shape[1]
    width = qbias_ref.shape[0]
    heads = width // HEAD_DIM

    @pl.when(step == 0)
    def _():
        weight_acc[...] = jnp.zeros_like(weight_acc)
        qbias_ref[...] = jnp.zeros_like(qbias_ref)
        vbias_ref[...] = jnp.zeros_like(vbias_ref)
        picked[...] = jnp.zeros_like(picked)

    @pl.when(jnp.logical_or(step == 0, row_now != row_before))
    def _():
        dkey[...] = jnp.zeros_like(dkey)
        dvalue[...] = jnp.zeros_like(dvalue)

    dcontext[...] = dot(out_ref[...], grad_ref[0], 1, 1).astype(bf16)
    dquery[...] = jnp.zeros_like(dquery)

    def one_head(head, carry):
        own = pl.ds(pl.multiple_of(head * HEAD_DIM, HEAD_DIM), HEAD_DIM)
        keys = key_ref[0, pl.ds(pl.multiple_of(head * length, 16), length)]
        values = value_ref[0, pl.ds(pl.multiple_of(head * length, 16), length)]
        queries = query_ref[0, pl.ds(pl.multiple_of(head * PAD_HEAD, PAD_HEAD), PAD_HEAD)]
        grad = dcontext[own]
        inner = jnp.sum(grad.astype(f32) * context_ref[0, own].astype(f32), axis=0, keepdims=True)
        extra = feature_rows(jnp.zeros((PAD_HEAD - HEAD_DIM, grad.shape[1]), f32), inner)
        probs = jnp.exp(dot(keys, queries, 1, 0))
        dprobs = dot(values, jnp.concatenate([grad, extra], axis=0), 1, 0)
        dscores = (probs * dprobs).astype(bf16)
        picked[0, pl.ds(pl.multiple_of(head * width + head * HEAD_DIM, HEAD_DIM), HEAD_DIM)] = grad
        picked[1, pl.ds(pl.multiple_of(head * width + head * HEAD_DIM, HEAD_DIM), HEAD_DIM)] = queries[0:HEAD_DIM]
        place_head = pl.ds(pl.multiple_of(head * width, HEAD_DIM), width)
        dvalue[...] += dot(probs.astype(bf16), picked[0, place_head], 1, 1)
        dkey[...] += dot(dscores, picked[1, place_head], 1, 1)
        dquery[own] = (dot(keys, dscores, 0, 0)[0:HEAD_DIM] * HEAD_DIM**-0.5).astype(bf16)
        return carry

    lax.fori_loop(0, live, one_head, 0)
    weight_acc[0:width] += dot(dquery[...], block_ref[0], 1, 0)
    weight_acc[3 * width :] += dot(context_ref[0], grad_ref[0], 1, 0)
    blockout_ref[0] = blocksum_ref[0] + dot(dquery[...], qkv_ref[0:width], 0, 0)
    qbias_ref[...] += jnp.sum(dquery[...].astype(f32), axis=1, keepdims=True)

    @pl.when(jnp.logical_or(step == steps - 1, row_now != row_after))
    def _():
        keys_low = dkey[...].astype(bf16)
        values_low = dvalue[...].astype(bf16)
        weight_acc[width : 2 * width] += dot(keys_low, row_ref[0], 0, 0)
        weight_acc[2 * width : 3 * width] += dot(values_low, row_ref[0], 0, 0)
        rowout_ref[0] = (
            rowsum_ref[0]
            + dot(keys_low, qkv_ref[width : 2 * width], 1, 0)
            + dot(values_low, qkv_ref[2 * width : 3 * width], 1, 0)
        )
        vbias_ref[...] += jnp.sum(values_low.astype(f32), axis=0, keepdims=True)

    @pl.when(step == steps - 1)
    def _():
        gradw_ref[...] = weight_acc[...].astype(bf16)


def whole(shape):
    return pl.BlockSpec(shape, lambda b, place: (0,) * len(shape))


def attend(place, blocks, rows, qkv, out, qbias, vbias, keyf, queryf, partial):
    steps, size, depth = partial.shape
    count, length, _ = rows.shape
    width = qbias.shape[0]
    heads = width // HEAD_DIM
    window = min(2, count)
    row_of = lambda b, place: ((place[0] + b) // place[1], 0, 0)
    rel_row = lambda b, place: ((place[0] + b) // place[1] - place[0] // place[1], 0, 0)
    block_of = lambda b, place: (place[0] + b, 0, 0)
    local = lambda b, place: (b, 0, 0)
    spec = pltpu.PrefetchScalarGridSpec(
        num_scalar_prefetch=1,
        grid=(steps,),
        in_specs=[
            pl.BlockSpec((1, size, depth), block_of),
            pl.BlockSpec((1, length, depth), row_of),
            whole(qkv.shape),
            whole(out.shape),
            whole(qbias.shape),
            whole(vbias.shape),
            pl.BlockSpec((1,) + keyf.shape[1:], row_of),
            pl.BlockSpec((1,) + queryf.shape[1:], block_of),
            pl.BlockSpec((1, size, depth), local),
        ],
        out_specs=[
            pl.BlockSpec((1, size, depth), local),
            pl.BlockSpec((1, heads * PAD_HEAD, size), local),
            pl.BlockSpec((1, heads * length, PAD_HEAD), rel_row),
            pl.BlockSpec((1, heads * length, PAD_HEAD), rel_row),
            pl.BlockSpec((1, width, size), local),
        ],
    )
    return pl.pallas_call(
        attend_kernel,
        grid_spec=spec,
        out_shape=[
            jax.ShapeDtypeStruct(partial.shape, f32),
            jax.ShapeDtypeStruct((steps, heads * PAD_HEAD, size), bf16),
            jax.ShapeDtypeStruct((window, heads * length, PAD_HEAD), bf16),
            jax.ShapeDtypeStruct((window, heads * length, PAD_HEAD), bf16),
            jax.ShapeDtypeStruct((steps, width, size), bf16),
        ],
        cost_estimate=pl.CostEstimate(
            flops=8 * steps * size * length * width, bytes_accessed=2**23, transcendentals=0
        ),
        name="attend",
    )(place, blocks, rows, qkv, out, qbias, vbias, keyf, queryf, partial)


def attend_back(place, blocks, rows, qkv, out, saved, grad, blocksum, rowsum):
    query, key, value, context = saved
    steps, size, depth = blocksum.shape
    count, length, _ = rows.shape
    width = out.shape[0]
    heads = width // HEAD_DIM
    row_of = lambda b, place: ((place[0] + b) // place[1], 0, 0)
    rel_row = lambda b, place: ((place[0] + b) // place[1] - place[0] // place[1], 0, 0)
    block_of = lambda b, place: (place[0] + b, 0, 0)
    local = lambda b, place: (b, 0, 0)
    spec = pltpu.PrefetchScalarGridSpec(
        num_scalar_prefetch=1,
        grid=(steps,),
        in_specs=[
            pl.BlockSpec((1, size, depth), block_of),
            pl.BlockSpec((1, length, depth), row_of),
            whole(qkv.shape),
            whole(out.shape),
            pl.BlockSpec((1,) + query.shape[1:], local),
            pl.BlockSpec((1,) + key.shape[1:], rel_row),
            pl.BlockSpec((1,) + value.shape[1:], rel_row),
            pl.BlockSpec((1,) + context.shape[1:], local),
            pl.BlockSpec((1, size, depth), local),
            pl.BlockSpec((1, size, depth), local),
            pl.BlockSpec((1, length, depth), rel_row),
        ],
        out_specs=[
            whole((4 * width, depth)),
            whole((width, 1)),
            whole((1, width)),
            pl.BlockSpec((1, size, depth), local),
            pl.BlockSpec((1, length, depth), rel_row),
        ],
        scratch_shapes=[
            pltpu.VMEM((4 * width, depth), f32),
            pltpu.VMEM((length, width), f32),
            pltpu.VMEM((length, width), f32),
            pltpu.VMEM((2, heads * width, size), bf16),
            pltpu.VMEM((width, size), bf16),
            pltpu.VMEM((width, size), bf16),
        ],
    )
    return pl.pallas_call(
        attend_back_kernel,
        grid_spec=spec,
        out_shape=[
            jax.ShapeDtypeStruct((4 * width, depth), bf16),
            jax.ShapeDtypeStruct((width, 1), f32),
            jax.ShapeDtypeStruct((1, width), f32),
            jax.ShapeDtypeStruct(blocksum.shape, f32),
            jax.ShapeDtypeStruct(rowsum.shape, f32),
        ],
        input_output_aliases={11: 4},
        cost_estimate=pl.CostEstimate(
            flops=20 * steps * size * length * width, bytes_accessed=2**23, transcendentals=0
        ),
        name="attend_back",
    )(place, blocks, rows, qkv, out, query, key, value, context, grad, blocksum, rowsum)


def swap(value, axis, distance):
    size = lax.axis_size(axis)
    return lax.ppermute(value, axis, [(i, i ^ distance) for i in range(size)])


def add_low(a, b):
    return (a.astype(f32) + b.astype(f32)).astype(bf16)


def sum_slots(parts):
    parts = list(parts)
    distance = 1
    while distance < len(parts):
        for slot in range(0, len(parts), 2 * distance):
            arrived = swap(parts[slot + distance], "heads", distance)
            parts[slot] = add_low(parts[slot], arrived) if arrived.dtype == bf16 else parts[slot] + arrived
        distance *= 2
    return parts[0]


def sum_rows(value):
    size = lax.axis_size("rows")
    here = lax.axis_index("rows")
    taken = []
    distance = 1
    while distance < size:
        half = value.shape[0] // 2
        if value.shape[0] % 2 == 0 and half % 8 == 0 and value.dtype == bf16:
            upper = (here // distance) % 2 == 1
            low_part, high_part = value[:half], value[half:]
            sent = swap(jnp.where(upper, low_part, high_part), "rows", distance)
            value = add_low(jnp.where(upper, high_part, low_part), sent)
            taken.append(distance)
        else:
            arrived = swap(value, "rows", distance)
            value = add_low(value, arrived) if value.dtype == bf16 else value + arrived
        distance *= 2
    for distance in reversed(taken):
        upper = (here // distance) % 2 == 1
        arrived = swap(value, "rows", distance)
        value = jnp.concatenate(
            [jnp.where(upper, arrived, value), jnp.where(upper, value, arrived)], axis=0
        )
    return value


def sum_heads(value):
    distance = 1
    while distance < lax.axis_size("heads"):
        value = value + swap(value, "heads", distance)
        distance *= 2
    return value


def gather_slots(value):
    slots = [value]
    distance = 1
    group = lax.axis_size("heads")
    slots = {0: value}
    distance = group // 2
    while distance >= 1:
        for slot in list(slots):
            slots[slot ^ distance] = swap(slots[slot], "heads", distance)
        distance //= 2
    return [slots[j] for j in range(group)]


def gather_frames(own, full_shape):
    position = lax.axis_index("heads")
    size = own.shape[0]
    result = jnp.zeros((full_shape[0] * full_shape[1], full_shape[2]), own.dtype)
    for slot, piece in enumerate(gather_slots(own)):
        result = lax.dynamic_update_slice(result, piece, ((position ^ slot) * size, 0))
    return result.reshape(full_shape)


def layer_stats(value):
    centre = value - jnp.mean(value, axis=-1, keepdims=True)
    inverse = lax.rsqrt(jnp.mean(centre * centre, axis=-1, keepdims=True) + norm_eps)
    return (centre * inverse, inverse)


def norm_back(grad_out, normal, inverse, gain):
    scaled = grad_out * gain
    return inverse * (
        scaled
        - jnp.mean(scaled, axis=-1, keepdims=True)
        - normal * jnp.mean(scaled * normal, axis=-1, keepdims=True)
    )


def exact_gelu(value):
    return jax.nn.gelu(value, approximate=False)


def per_device(
    frames, segment_ids, cotangent, query_weight, query_bias, key_weight, value_weight, value_bias,
    output_weight, output_bias, first_gain, first_shift, inner_weight, inner_bias, outer_weight,
    outer_bias, second_gain, second_shift,
):
    group = lax.axis_size("heads")
    position = lax.axis_index("heads")
    row_count, row_length, depth = frames.shape
    own_len = row_count * row_length // group
    size = math.gcd(row_length, own_len)
    steps = own_len // size
    per_row = row_length // size
    width = query_weight.shape[1]
    heads_here = width // HEAD_DIM
    per_head = FF_LIVE // HEADS_LIVE
    hidden_slots = inner_weight.shape[1]
    hidden_cap = min(hidden_slots, (HEADS_LIVE + group - 1) // group * per_head)

    def live_of(index):
        return HEADS_LIVE // group + (index < HEADS_LIVE % group).astype(jnp.int32)

    live_heads = live_of(position)
    head_mask = (jnp.arange(width, dtype=jnp.int32) // HEAD_DIM < live_heads)[:, None]
    hidden_mask = (jnp.arange(hidden_cap, dtype=jnp.int32) < live_heads * per_head)[:, None]
    qkv_own = jnp.concatenate([query_weight.T, key_weight.T, value_weight.T], axis=0)
    out_own = jnp.where(head_mask, output_weight, 0)
    up_own = inner_weight.T[:hidden_cap]
    down_own = jnp.where(hidden_mask, outer_weight[:hidden_cap], 0)
    bias_own = jnp.concatenate([query_bias, value_bias, inner_bias[:hidden_cap]])[None]

    qkv = gather_slots(qkv_own)
    out = gather_slots(out_own)
    bias = gather_slots(bias_own)
    up = gather_slots(up_own)
    down = gather_slots(down_own)

    blocks = frames.reshape(row_count * per_row, size, depth)
    kinds = jnp.arange(-1, SEGMENTS - 1, dtype=jnp.int32)
    same = segment_ids[:, :, None] == kinds
    keyf = jnp.concatenate(
        [
            same.astype(bf16),
            jnp.ones((row_count, row_length, 3), bf16),
            jnp.zeros((row_count, row_length, HEAD_DIM - SEGMENTS - 3), bf16),
        ],
        axis=2,
    )
    ids_blocks = segment_ids.reshape(row_count * per_row, 1, size)
    queryf = jnp.where(ids_blocks == kinds[:, None], 0.0, MASK_STEP).astype(bf16)
    queryf = jnp.pad(queryf, ((0, 0), (0, HEAD_DIM - SEGMENTS), (0, 0)))

    def own_part(value):
        flat = value.reshape((row_count * row_length,) + value.shape[2:])
        return lax.dynamic_slice_in_dim(flat, position * own_len, own_len, 0)

    places = [
        jnp.stack([position * steps, jnp.int32(per_row), live_of(position ^ slot)])
        for slot in range(group)
    ]
    total = jnp.zeros((steps, size, depth), f32)
    saved = []
    for slot in range(group):
        qbias = bias[slot][0, :width, None]
        vbias = bias[slot][:, width : 2 * width]
        total, *kept = attend(
            places[slot], blocks, frames, qkv[slot], out[slot], qbias, vbias, keyf, queryf, total
        )
        saved.append(kept)
    attended = total.reshape(own_len, depth)

    hidden_one = own_part(frames).astype(f32) + attended + output_bias
    normal_one, inverse_one = layer_stats(hidden_one)
    normed_one = normal_one * first_gain + first_shift
    normed_low = normed_one.astype(bf16)
    actives, pulls = [], []
    ffn = 0.0
    for slot in range(group):
        inner_pre = dot(normed_low, up[slot], 1, 1) + bias[slot][:, 2 * width :]
        active, pull = jax.vjp(exact_gelu, inner_pre)
        actives.append(active.astype(bf16))
        pulls.append(pull)
        ffn = ffn + dot(actives[-1], down[slot], 1, 0)
    hidden_two = normed_one + ffn + outer_bias
    normal_two, inverse_two = layer_stats(hidden_two)
    live_rows = (own_part(segment_ids) >= 0).astype(f32)[:, None]
    final_out = (normal_two * second_gain + second_shift) * live_rows
    layer_out = gather_frames(final_out.astype(bf16), frames.shape)
    grad_final = own_part(cotangent).astype(f32) * live_rows
    secondgain_part = jnp.sum(grad_final * normal_two, axis=0)
    secondshift_part = jnp.sum(grad_final, axis=0)
    grad_hidden_two = norm_back(grad_final, normal_two, inverse_two, second_gain)
    outerbias_part = jnp.sum(grad_hidden_two, axis=0)
    grad_ffn = grad_hidden_two.astype(bf16)

    down_parts, up_parts, innerbias_parts = [], [], []
    grad_normed = grad_hidden_two
    for slot in range(group):
        down_parts.append(dot(actives[slot], grad_ffn, 0, 0).astype(bf16))
        grad_active = dot(grad_ffn, down[slot], 1, 1)
        grad_inner = pulls[slot](grad_active)[0].astype(bf16)
        up_parts.append(dot(grad_inner, normed_low, 0, 0).astype(bf16))
        innerbias_parts.append(jnp.sum(grad_inner, axis=0, dtype=f32))
        grad_normed = grad_normed + dot(grad_inner, up[slot], 1, 0)
    down_sum = sum_rows(sum_slots(down_parts)).astype(f32)
    up_sum = sum_rows(sum_slots(up_parts)).astype(f32)
    innerbias_sum = sum_rows(sum_slots(innerbias_parts))

    firstgain_part = jnp.sum(grad_normed * normal_one, axis=0)
    firstshift_part = jnp.sum(grad_normed, axis=0)
    grad_hidden_one = norm_back(grad_normed, normal_one, inverse_one, first_gain)
    outputbias_part = jnp.sum(grad_hidden_one, axis=0)
    norm_sums = sum_rows(
        sum_heads(
            jnp.stack(
                [
                    outputbias_part, firstgain_part, firstshift_part,
                    outerbias_part, secondgain_part, secondshift_part,
                ]
            )
        )
    )
    grad_attn = grad_hidden_one.astype(bf16).reshape(steps, size, depth)
    block_sum = grad_hidden_one.reshape(steps, size, depth)
    row_sum = jnp.zeros((min(2, row_count), row_length, depth), f32)
    attn_parts, attnbias_parts = [None] * group, [None] * group
    for slot in reversed(range(group)):
        attn_parts[slot], qb, vb, block_sum, row_sum = attend_back(
            places[slot], blocks, frames, qkv[slot], out[slot], saved[slot], grad_attn,
            block_sum, row_sum,
        )
        attnbias_parts[slot] = jnp.concatenate([qb[:, 0], vb[0]])[None]
    attn_sum = sum_rows(sum_slots(attn_parts)).astype(f32)
    attnbias_sum = sum_rows(sum_slots(attnbias_parts))

    first_row = position * steps // per_row
    spread = jnp.zeros((row_count + 1, row_length, depth), f32)
    spread = lax.dynamic_update_slice(spread, row_sum, (first_row, 0, 0))[:row_count]
    pieces = spread.reshape(group, own_len, depth)

    def piece_of(index):
        return lax.dynamic_index_in_dim(pieces, index, 0, keepdims=False)

    own_grad = block_sum.reshape(own_len, depth) + piece_of(position)
    for distance in range(1, group):
        pairs = []
        for i in range(group):
            j = i ^ distance
            rows_i = range(i * steps // per_row, ((i + 1) * steps - 1) // per_row + 1)
            rows_j = range(j * steps // per_row, ((j + 1) * steps - 1) // per_row + 1)
            if set(rows_i) & set(rows_j):
                pairs.append((i, j))
        if pairs:
            sent = piece_of(position ^ distance).astype(bf16)
            own_grad = own_grad + lax.ppermute(sent, "heads", pairs).astype(f32)
    frames_grad = gather_frames(own_grad.astype(bf16), frames.shape)

    padding = hidden_slots - hidden_cap
    inner_full = jnp.pad(up_sum, ((0, padding), (0, 0))).T
    outer_full = jnp.pad(jnp.where(hidden_mask, down_sum, 0), ((0, padding), (0, 0)))
    innerbias_full = jnp.pad(innerbias_sum, ((0, padding),))
    return (
        layer_out,
        frames_grad,
        attn_sum[:width].T,
        attnbias_sum[0, :width],
        attn_sum[width : 2 * width].T,
        attn_sum[2 * width : 3 * width].T,
        attnbias_sum[0, width:],
        attn_sum[3 * width :],
        norm_sums[0],
        norm_sums[1],
        norm_sums[2],
        inner_full,
        innerbias_full,
        outer_full,
        norm_sums[3],
        norm_sums[4],
        norm_sums[5],
    )


def solution(mesh):
    in_specs = (
        P("rows", None, None), P("rows", None), P("rows", None, None), P(None, "heads"), P("heads"),
        P(None, "heads"), P(None, "heads"), P("heads"), P("heads", None), P(), P(), P(),
        P(None, "heads"), P("heads"), P("heads", None), P(), P(), P(),
    )
    out_specs = (
        P("rows", None, None), P("rows", None, None), P(None, "heads"), P("heads"), P(None, "heads"),
        P(None, "heads"), P("heads"), P("heads", None), P(), P(), P(), P(None, "heads"), P("heads"),
        P("heads", None), P(), P(), P(),
    )
    return jax.shard_map(
        per_device, mesh=mesh, in_specs=in_specs, out_specs=out_specs, check_vma=False
    )
```

```python
import functools
import math

import jax
import jax.numpy as jnp
from jax import lax
from jax.experimental import pallas as pl
from jax.experimental.pallas import tpu as pltpu
from jax.sharding import PartitionSpec as P

HEADS_LIVE = 10
HEAD_SLOTS = 12
HEAD_DIM = 64
FF_LIVE = 2240
PAD_HEAD = 128
SEGMENTS = 5
MASK_STEP = -(2.0**30)
norm_eps = 1e-05
f32 = jnp.float32
bf16 = jnp.bfloat16


def dot(a, b, ca, cb):
    return lax.dot_general(a, b, (((ca,), (cb,)), ((), ())), preferred_element_type=f32)


def three_parts(value):
    high = value.astype(bf16).astype(f32)
    middle = (value - high).astype(bf16).astype(f32)
    return high, middle, value - high - middle


def live_heads(live, heads, one_head):
    least = HEADS_LIVE * heads // HEAD_SLOTS
    for count in range(least, heads + 1):

        @pl.when(live == count)
        def _():
            for head in range(count):
                one_head(head)


def feature_rows(base, value):
    high, middle, low = three_parts(-value)
    row = lax.broadcasted_iota(jnp.int32, base.shape, 0)
    base = jnp.where(row == SEGMENTS, high, base)
    base = jnp.where(row == SEGMENTS + 1, middle, base)
    return jnp.where(row == SEGMENTS + 2, low, base).astype(bf16)


def attend_kernel(
    slot, place, block_ref, row_ref, weight_ref, bias_ref, keyf_ref, queryf_ref,
    sum_ref, total_ref, query_ref, key_ref, value_ref, context_ref,
):
    step = pl.program_id(0)
    per_row, live = place[1], place[3 + slot]
    row_now = (place[0] + step) // per_row
    row_before = (place[0] + step - 1) // per_row
    length = row_ref.shape[1]
    width = weight_ref.shape[0] // 4
    heads = width // HEAD_DIM

    @pl.when(jnp.logical_or(step == 0, row_now != row_before))
    def _():
        frames = row_ref[0]
        keys = dot(frames, weight_ref[width : 2 * width], 1, 1).astype(bf16)
        values = dot(frames, weight_ref[2 * width : 3 * width], 1, 1)
        values = (values + bias_ref[1:2, 0:width]).astype(bf16)
        features = keyf_ref[0]
        for head in range(heads):
            cut = slice(head * HEAD_DIM, (head + 1) * HEAD_DIM)
            key_ref[0, head * length : (head + 1) * length] = jnp.concatenate(
                [keys[:, cut], features], axis=1
            )
            value_ref[0, head * length : (head + 1) * length] = jnp.concatenate(
                [values[:, cut], features], axis=1
            )

    qbias = jnp.broadcast_to(bias_ref[0:1, 0:width], (8, width)).T[:, 0:1]
    queries = (dot(weight_ref[0:width], block_ref[0], 1, 1) + qbias).astype(bf16)
    queries = queries * jnp.asarray(HEAD_DIM**-0.5, bf16)
    for head in range(heads):
        query_ref[0, head * PAD_HEAD : head * PAD_HEAD + HEAD_DIM] = queries[
            head * HEAD_DIM : (head + 1) * HEAD_DIM
        ]
        query_ref[0, head * PAD_HEAD + HEAD_DIM : (head + 1) * PAD_HEAD] = queryf_ref[0]
    context_ref[...] = jnp.zeros_like(context_ref)

    def one_head(head):
        keys = key_ref[0, pl.ds(head * length, length)]
        values = value_ref[0, pl.ds(head * length, length)]
        start = head * PAD_HEAD
        scores = dot(keys, query_ref[0, pl.ds(start, PAD_HEAD)], 1, 0)
        highest = jnp.max(scores, axis=0, keepdims=True)
        probs = jnp.exp(scores - highest).astype(bf16)
        mixed = dot(values, probs, 0, 0)
        total = mixed[HEAD_DIM + SEGMENTS : HEAD_DIM + SEGMENTS + 1]
        context = mixed[0:HEAD_DIM] / total
        context_ref[0, pl.ds(head * HEAD_DIM, HEAD_DIM)] = context.astype(bf16)
        base = queryf_ref[0, 0:16].astype(f32)
        query_ref[0, pl.ds(start + HEAD_DIM, 16)] = feature_rows(base, highest + jnp.log(total))

    live_heads(live, heads, one_head)
    mixed = dot(context_ref[0], weight_ref[3 * width :], 0, 0)
    if slot == 0:
        total_ref[0] = mixed
    else:
        total_ref[0] = sum_ref[0] + mixed


def attend_back_kernel(
    slot, first, place, block_ref, row_ref, weight_ref, query_ref, key_ref, value_ref, context_ref,
    grad_ref, blocksum_ref, small_ref, smalltwo_ref, rowsum_ref,
    gradw_ref, blockout_ref, rowout_ref,
    weight_acc, dkey, dvalue, picked, dcontext, dquery, bias_acc,
):
    step = pl.program_id(0)
    steps = pl.num_programs(0)
    per_row, live = place[1], place[3 + slot]
    row_now = (place[0] + step) // per_row
    row_before = (place[0] + step - 1) // per_row
    row_after = (place[0] + step + 1) // per_row
    length, depth = row_ref.shape[1:]
    width = weight_ref.shape[0] // 4
    heads = width // HEAD_DIM
    ones = jnp.ones((8, length), bf16)

    @pl.when(step == 0)
    def _():
        weight_acc[...] = jnp.zeros_like(weight_acc)
        bias_acc[...] = jnp.zeros_like(bias_acc)
        picked[...] = jnp.zeros_like(picked)

    @pl.when(jnp.logical_or(step == 0, row_now != row_before))
    def _():
        dkey[...] = jnp.zeros_like(dkey)
        dvalue[...] = jnp.zeros_like(dvalue)

    dcontext[...] = dot(weight_ref[3 * width :], grad_ref[0], 1, 1).astype(bf16)
    dquery[...] = jnp.zeros_like(dquery)

    def one_head(head):
        own = pl.ds(head * HEAD_DIM, HEAD_DIM)
        keys = key_ref[0, pl.ds(head * length, length)]
        values = value_ref[0, pl.ds(head * length, length)]
        queries = query_ref[0, pl.ds(head * PAD_HEAD, PAD_HEAD)]
        grad = dcontext[own]
        inner = jnp.sum(grad.astype(f32) * context_ref[0, own].astype(f32), axis=0, keepdims=True)
        extra = feature_rows(jnp.zeros((PAD_HEAD - HEAD_DIM, grad.shape[1]), f32), inner)
        probs = jnp.exp(dot(keys, queries, 1, 0))
        dprobs = dot(values, jnp.concatenate([grad, extra], axis=0), 1, 0)
        dscores = (probs * dprobs).astype(bf16)
        picked[0, pl.ds(head * width + head * HEAD_DIM, HEAD_DIM)] = grad
        picked[1, pl.ds(head * width + head * HEAD_DIM, HEAD_DIM)] = queries[0:HEAD_DIM]
        place_head = pl.ds(head * width, width)
        dvalue[...] += dot(probs.astype(bf16), picked[0, place_head], 1, 1)
        dkey[...] += dot(dscores, picked[1, place_head], 1, 1)
        dquery[own] = (dot(keys, dscores, 0, 0)[0:HEAD_DIM] * HEAD_DIM**-0.5).astype(bf16)

    live_heads(live, heads, one_head)
    weight_acc[0:width] += dot(dquery[...], block_ref[0], 1, 0)
    weight_acc[3 * width :] += dot(context_ref[0], grad_ref[0], 1, 0)
    blockout_ref[0] = blocksum_ref[0] + dot(dquery[...], weight_ref[0:width], 0, 0)
    bias_acc[0:8] += dot(ones[:, 0 : dquery.shape[1]], dquery[...], 1, 1)

    @pl.when(jnp.logical_or(step == steps - 1, row_now != row_after))
    def _():
        keys_low = dkey[...].astype(bf16)
        values_low = dvalue[...].astype(bf16)
        weight_acc[width : 2 * width] += dot(keys_low, row_ref[0], 0, 0)
        weight_acc[2 * width : 3 * width] += dot(values_low, row_ref[0], 0, 0)
        back = dot(keys_low, weight_ref[width : 2 * width], 1, 0) + dot(
            values_low, weight_ref[2 * width : 3 * width], 1, 0
        )
        if first:
            rowout_ref[0] = back
        else:
            rowout_ref[0] = rowsum_ref[0] + back
        bias_acc[8:16] += dot(ones, values_low, 1, 0)

    @pl.when(step == steps - 1)
    def _():
        gradw_ref[0 : 4 * width] = weight_acc[...].astype(bf16)
        row = lax.broadcasted_iota(jnp.int32, (gradw_ref.shape[0] - 4 * width, depth), 0)
        lanes = depth - width
        extra = jnp.where(row == 0, jnp.pad(bias_acc[0:1], ((0, 0), (0, lanes))), 0.0)
        extra = jnp.where(row == 1, jnp.pad(bias_acc[8:9], ((0, 0), (0, lanes))), extra)
        for index in range(3):
            extra = jnp.where(row == 2 + index, small_ref[index : index + 1], extra)
            extra = jnp.where(row == 5 + index, smalltwo_ref[index : index + 1], extra)
        gradw_ref[4 * width :] = extra.astype(bf16)


def whole(shape):
    return pl.BlockSpec(shape, lambda b, place: (0,) * len(shape))


def attend(slot, place, blocks, rows, weight, bias, keyf, queryf, partial):
    size, depth = blocks.shape[1:]
    count, length, _ = rows.shape
    steps = partial[0]
    width = weight.shape[0] // 4
    heads = width // HEAD_DIM
    window = min(2, count)
    row_of = lambda b, place: ((place[0] + b) // place[1], 0, 0)
    rel_row = lambda b, place: ((place[0] + b) // place[1] - place[0] // place[1], 0, 0)
    block_of = lambda b, place: (place[0] + b, 0, 0)
    local = lambda b, place: (b, 0, 0)
    total = pl.BlockSpec((1, size, depth), local)
    before = partial[1] if slot else jnp.zeros((8, 128), f32)
    spec = pltpu.PrefetchScalarGridSpec(
        num_scalar_prefetch=1,
        grid=(steps,),
        in_specs=[
            pl.BlockSpec((1, size, depth), block_of),
            pl.BlockSpec((1, length, depth), row_of),
            whole(weight.shape),
            whole(bias.shape),
            pl.BlockSpec((1,) + keyf.shape[1:], row_of),
            pl.BlockSpec((1,) + queryf.shape[1:], block_of),
            total if slot else whole(before.shape),
        ],
        out_specs=[
            total,
            pl.BlockSpec((1, heads * PAD_HEAD, size), local),
            pl.BlockSpec((1, heads * length, PAD_HEAD), rel_row),
            pl.BlockSpec((1, heads * length, PAD_HEAD), rel_row),
            pl.BlockSpec((1, width, size), local),
        ],
    )
    return pl.pallas_call(
        functools.partial(attend_kernel, slot),
        grid_spec=spec,
        out_shape=[
            jax.ShapeDtypeStruct((steps, size, depth), f32),
            jax.ShapeDtypeStruct((steps, heads * PAD_HEAD, size), bf16),
            jax.ShapeDtypeStruct((window, heads * length, PAD_HEAD), bf16),
            jax.ShapeDtypeStruct((window, heads * length, PAD_HEAD), bf16),
            jax.ShapeDtypeStruct((steps, width, size), bf16),
        ],
        cost_estimate=pl.CostEstimate(flops=2**33, bytes_accessed=2**24, transcendentals=0),
        compiler_params=pltpu.CompilerParams(vmem_limit_bytes=20 * 2**20),
        name="attend",
    )(place, blocks, rows, weight, bias, keyf, queryf, before)


EXTRA_ROWS = 64


def attend_back(slot, first, place, blocks, rows, weight, saved, grad, blocksum, smalls, rowsum):
    query, key, value, context = saved
    steps, size, depth = blocksum.shape
    count, length, _ = rows.shape
    width = weight.shape[0] // 4
    heads = width // HEAD_DIM
    row_of = lambda b, place: ((place[0] + b) // place[1], 0, 0)
    rel_row = lambda b, place: ((place[0] + b) // place[1] - place[0] // place[1], 0, 0)
    block_of = lambda b, place: (place[0] + b, 0, 0)
    local = lambda b, place: (b, 0, 0)
    row_spec = pl.BlockSpec((1, length, depth), rel_row)
    spec = pltpu.PrefetchScalarGridSpec(
        num_scalar_prefetch=1,
        grid=(steps,),
        in_specs=[
            pl.BlockSpec((1, size, depth), block_of),
            pl.BlockSpec((1, length, depth), row_of),
            whole(weight.shape),
            pl.BlockSpec((1,) + query.shape[1:], local),
            pl.BlockSpec((1,) + key.shape[1:], rel_row),
            pl.BlockSpec((1,) + value.shape[1:], rel_row),
            pl.BlockSpec((1,) + context.shape[1:], local),
            pl.BlockSpec((1, size, depth), local),
            pl.BlockSpec((1, size, depth), local),
            whole(smalls[0].shape),
            whole(smalls[1].shape),
            ANYWHERE if first else row_spec,
        ],
        out_specs=[
            whole((4 * width + EXTRA_ROWS, depth)),
            pl.BlockSpec((1, size, depth), local),
            row_spec,
        ],
        scratch_shapes=[
            pltpu.VMEM((4 * width, depth), f32),
            pltpu.VMEM((length, width), f32),
            pltpu.VMEM((length, width), f32),
            pltpu.VMEM((2, heads * width, size), bf16),
            pltpu.VMEM((width, size), bf16),
            pltpu.VMEM((width, size), bf16),
            pltpu.VMEM((16, width), f32),
        ],
    )
    return pl.pallas_call(
        functools.partial(attend_back_kernel, slot, first),
        grid_spec=spec,
        out_shape=[
            jax.ShapeDtypeStruct((4 * width + EXTRA_ROWS, depth), bf16),
            jax.ShapeDtypeStruct(blocksum.shape, f32),
            jax.ShapeDtypeStruct((min(2, count), length, depth), f32),
        ],
        input_output_aliases={} if first else {12: 2},
        cost_estimate=pl.CostEstimate(flops=2**34, bytes_accessed=2**24, transcendentals=0),
        compiler_params=pltpu.CompilerParams(vmem_limit_bytes=26 * 2**20),
        name="attend_back",
    )(place, blocks, rows, weight, query, key, value, context, grad, blocksum, *smalls, rowsum)


ANYWHERE = pl.BlockSpec(memory_space=pl.ANY)


def prepare_kernel(place, query_ref, key_ref, value_ref, out_ref, weight_ref):
    width = query_ref.shape[0]
    weight_ref[0:width] = query_ref[...]
    weight_ref[width : 2 * width] = key_ref[...]
    weight_ref[2 * width : 3 * width] = value_ref[...]
    row = lax.broadcasted_iota(jnp.int32, out_ref.shape, 0)
    kept = jnp.where(row < place[3] * HEAD_DIM, out_ref[...].astype(f32), 0.0)
    weight_ref[3 * width :] = kept.astype(bf16)


def prepare(place, query, key, value, out):
    width, depth = query.shape
    return pl.pallas_call(
        prepare_kernel,
        grid_spec=pltpu.PrefetchScalarGridSpec(
            num_scalar_prefetch=1,
            grid=(1,),
            in_specs=[whole(query.shape)] * 3 + [whole(out.shape)],
            out_specs=whole((4 * width, depth)),
        ),
        out_shape=jax.ShapeDtypeStruct((4 * width, depth), bf16),
        name="prepare",
    )(place, query, key, value, out)


def prepare_wide_kernel(per_head, place, up_ref, down_ref, ids_ref, blocks_ref, upout_ref, downout_ref, keyf_ref, queryf_ref):
    hidden = upout_ref.shape[0]
    upout_ref[...] = up_ref[...].T[0:hidden]
    row = lax.broadcasted_iota(jnp.int32, downout_ref.shape, 0)
    kept = jnp.where(row < place[3] * per_head, down_ref[0:hidden].astype(f32), 0.0)
    downout_ref[...] = kept.astype(bf16)
    rows, length = ids_ref.shape
    feature = lax.broadcasted_iota(jnp.int32, (HEAD_DIM, length), 0)
    for r in range(rows):
        same = jnp.where(feature == ids_ref[r : r + 1] + 1, 1.0, 0.0)
        ones = jnp.where(jnp.logical_and(feature >= SEGMENTS, feature < SEGMENTS + 3), 1.0, same)
        keyf_ref[r] = ones.T.astype(bf16)
    size = blocks_ref.shape[2]
    feature = lax.broadcasted_iota(jnp.int32, (HEAD_DIM, size), 0)
    for b in range(blocks_ref.shape[0]):
        other = jnp.logical_and(feature < SEGMENTS, feature != blocks_ref[b] + 1)
        queryf_ref[b] = jnp.where(other, MASK_STEP, 0.0).astype(bf16)


def prepare_wide(place, up, down, ids, id_blocks, hidden):
    depth = up.shape[0]
    rows, length = ids.shape
    shapes = [
        (hidden, depth), (hidden, depth), (rows, length, HEAD_DIM),
        (id_blocks.shape[0], HEAD_DIM, id_blocks.shape[2]),
    ]
    return pl.pallas_call(
        functools.partial(prepare_wide_kernel, FF_LIVE // HEADS_LIVE),
        grid_spec=pltpu.PrefetchScalarGridSpec(
            num_scalar_prefetch=1,
            grid=(1,),
            in_specs=[whole(v.shape) for v in (up, down, ids, id_blocks)],
            out_specs=[whole(shape) for shape in shapes],
        ),
        out_shape=[jax.ShapeDtypeStruct(shape, bf16) for shape in shapes],
        name="prepare_wide",
    )(place, up, down, ids, id_blocks)


def row_chunks(count, body):
    chunk = 200 if count % 200 == 0 else 16

    @pl.loop(0, count // chunk)
    def _(i):
        body(pl.ds(pl.multiple_of(i * chunk, 8), chunk))

    if count % chunk:
        body(pl.ds(count // chunk * chunk, count % chunk))


def phi_parts(value):
    bell = jnp.exp(value * value * -0.5)
    t = 1.0 / (1.0 + jnp.abs(value) * (0.3275911 * 0.5**0.5))
    poly = t * (
        0.254829592
        + t * (-0.284496736 + t * (1.421413741 + t * (-1.453152027 + t * 1.061405429)))
    )
    half = 0.5 * poly * bell
    return jnp.where(value >= 0, 1.0 - half, half), bell * (2.0 * math.pi) ** -0.5


def chunk_stats(value):
    centre = value - jnp.mean(value, axis=-1, keepdims=True)
    inverse = lax.rsqrt(jnp.mean(centre * centre, axis=-1, keepdims=True) + norm_eps)
    return centre * inverse, inverse


def fetch_slot(order, step, sources, buffers, sems):
    for which, (refs, buffer) in enumerate(zip(sources, buffers)):
        for position, slot in enumerate(order):

            @pl.when(step == position)
            def _():
                pltpu.make_async_copy(refs[slot], buffer.at[step % 2], sems.at[which, step % 2]).start()


def await_slot(step, sources, buffers, sems):
    for which, (refs, buffer) in enumerate(zip(sources, buffers)):
        pltpu.make_async_copy(refs[0], buffer.at[step % 2], sems.at[which, step % 2]).wait()


def stream_slots(order, sources, buffers, sems):
    step = pl.program_id(0)

    @pl.when(step == 0)
    def _():
        fetch_slot(order, step, sources, buffers, sems)

    @pl.when(step + 1 < pl.num_programs(0))
    def _():
        fetch_slot(order, step + 1, sources, buffers, sems)

    await_slot(step, sources, buffers, sems)


FORWARD_ORDER = (0, 1, 2, 3)


def ffn_kernel(
    place, frames_ref, cot_ref, ids_ref, total_ref, vec_ref, bias_ref, *refs,
):
    group = bias_ref.shape[0]
    up_refs, down_refs, rest = refs[:group], refs[group : 2 * group], refs[2 * group :]
    (
        layer_ref, low_ref, normal_ref, inverse_ref, gradtwo_ref, gradffn_ref, small_ref,
        active_ref, slope_ref, up_buf, down_buf, pre, mixed, sems,
    ) = rest
    step = pl.program_id(0)
    count = total_ref.shape[0]
    stream_slots(FORWARD_ORDER[:group], (up_refs, down_refs), (up_buf, down_buf), sems)
    out_bias, gain_one, shift_one = vec_ref[0:1], vec_ref[1:2], vec_ref[2:3]
    outer_bias, gain_two, shift_two = vec_ref[3:4], vec_ref[4:5], vec_ref[5:6]

    @pl.when(step == 0)
    def _():
        def first(rows):
            hidden = frames_ref[0, rows].astype(f32) + total_ref[rows] + out_bias
            normal, inverse = chunk_stats(hidden)
            normal_ref[rows] = normal
            inverse_ref[rows] = inverse
            normed = normal * gain_one + shift_one
            low_ref[rows] = normed.astype(bf16)
            mixed[rows] = normed + outer_bias

        row_chunks(count, first)

    pre[...] = dot(low_ref[...], up_buf[step % 2], 1, 1) + bias_ref[pl.ds(step, 1)]

    def gelu(rows):
        value = pre[rows]
        whole_part, bell = phi_parts(value)
        active_ref[0, rows] = (value * whole_part).astype(bf16)
        slope_ref[0, rows] = (whole_part + value * bell).astype(bf16)

    row_chunks(count, gelu)
    mixed[...] += dot(active_ref[0], down_buf[step % 2], 1, 0)

    @pl.when(step == pl.num_programs(0) - 1)
    def _():
        small_ref[...] = jnp.zeros_like(small_ref)

        def last(rows):
            normal, inverse = chunk_stats(mixed[rows])
            live = (ids_ref[rows] >= 0).astype(f32)
            layer_ref[rows] = ((normal * gain_two + shift_two) * live).astype(bf16)
            grad = cot_ref[0, rows].astype(f32) * live
            small_ref[0:1] += jnp.sum(grad * normal, axis=0, keepdims=True)
            small_ref[1:2] += jnp.sum(grad, axis=0, keepdims=True)
            scaled = grad * gain_two
            back = inverse * (
                scaled
                - jnp.mean(scaled, axis=-1, keepdims=True)
                - normal * jnp.mean(scaled * normal, axis=-1, keepdims=True)
            )
            small_ref[2:3] += jnp.sum(back, axis=0, keepdims=True)
            gradtwo_ref[rows] = back
            gradffn_ref[rows] = back.astype(bf16)

        row_chunks(count, last)


def ffn_back_kernel(
    order, last, group, low_ref, normal_ref, inverse_ref, gradtwo_ref, gradffn_ref, active_ref, slope_ref,
    gain_ref, *refs,
):
    up_refs, down_refs, rest = refs[:group], refs[group : 2 * group], refs[2 * group :]
    if last:
        downgrad_ref, upgrad_ref, small_ref, gradone_ref, gradattn_ref, *rest = rest
    else:
        downgrad_ref, upgrad_ref, normed_grad, *rest = rest
    up_buf, down_buf, inner, sems, *rest = rest
    if last:
        normed_grad = rest[0]
    step = pl.program_id(0)
    count, hidden = inner.shape
    depth = low_ref.shape[1]
    stream_slots(order, (up_refs, down_refs), (up_buf, down_buf), sems)

    @pl.when(step == 0)
    def _():
        normed_grad[...] = gradtwo_ref[...]

    downgrad_ref[0] = dot(active_ref[0], gradffn_ref[...], 0, 0).astype(bf16)
    grad_active = dot(gradffn_ref[...], down_buf[step % 2], 1, 1)
    grad_inner = (grad_active * slope_ref[0].astype(f32)).astype(bf16)
    inner[...] = grad_inner
    upgrad_ref[0, 0:hidden] = dot(inner[...], low_ref[...], 0, 0).astype(bf16)
    ones = jnp.ones((8, count), bf16)
    bias = dot(ones, inner[...], 1, 0)
    row = lax.broadcasted_iota(jnp.int32, (upgrad_ref.shape[1] - hidden, depth), 0)
    extra = jnp.where(row == 0, bias[0:1, 0:depth], 0.0)
    rest_lanes = jnp.pad(bias[0:1, depth:hidden], ((0, 0), (0, 2 * depth - hidden)))
    upgrad_ref[0, hidden:] = jnp.where(row == 1, rest_lanes, extra).astype(bf16)
    normed_grad[...] += dot(inner[...], up_buf[step % 2], 1, 0)

    if last:

        @pl.when(step == pl.num_programs(0) - 1)
        def _():
            small_ref[...] = jnp.zeros_like(small_ref)
            gain = gain_ref[...]

            def last_rows(rows):
                grad, normal = normed_grad[rows], normal_ref[rows]
                small_ref[0:1] += jnp.sum(grad * normal, axis=0, keepdims=True)
                small_ref[1:2] += jnp.sum(grad, axis=0, keepdims=True)
                scaled = grad * gain
                back = inverse_ref[rows] * (
                    scaled
                    - jnp.mean(scaled, axis=-1, keepdims=True)
                    - normal * jnp.mean(scaled * normal, axis=-1, keepdims=True)
                )
                small_ref[2:3] += jnp.sum(back, axis=0, keepdims=True)
                gradone_ref[rows] = back
                gradattn_ref[rows] = back.astype(bf16)

            row_chunks(count, last_rows)


def ffn(place, frames, cotangent, ids, total, vectors, bias, up, down):
    group = len(up)
    count, depth = total.shape
    hidden = bias.shape[1]
    full = lambda shape: pl.BlockSpec(shape, lambda s, place: (0,) * len(shape))
    own = pl.BlockSpec((1, count, depth), lambda s, place: (place[2], 0, 0))
    per_slot = pl.BlockSpec((1, count, hidden), lambda s, place: (s, 0, 0))
    spec = pltpu.PrefetchScalarGridSpec(
        num_scalar_prefetch=1,
        grid=(group,),
        in_specs=[own, own, full(ids.shape), full(total.shape), full(vectors.shape), full(bias.shape)]
        + [ANYWHERE] * (2 * group),
        out_specs=[
            full((count, depth)), full((count, depth)), full((count, depth)), full((count, 1)),
            full((count, depth)), full((count, depth)), full((8, depth)), per_slot, per_slot,
        ],
        scratch_shapes=[
            pltpu.VMEM((2,) + up[0].shape, bf16),
            pltpu.VMEM((2,) + down[0].shape, bf16),
            pltpu.VMEM((count, hidden), f32),
            pltpu.VMEM((count, depth), f32),
            pltpu.SemaphoreType.DMA((2, 2)),
        ],
    )
    shape = jax.ShapeDtypeStruct
    return pl.pallas_call(
        ffn_kernel,
        grid_spec=spec,
        out_shape=[
            shape((count, depth), bf16), shape((count, depth), bf16), shape((count, depth), f32),
            shape((count, 1), f32), shape((count, depth), f32), shape((count, depth), bf16),
            shape((8, depth), f32), shape((group, count, hidden), bf16),
            shape((group, count, hidden), bf16),
        ],
        cost_estimate=pl.CostEstimate(
            flops=2**34, bytes_accessed=2**25, transcendentals=0
        ),
        compiler_params=pltpu.CompilerParams(vmem_limit_bytes=26 * 2**20),
        name="ffn",
    )(place, frames, cotangent, ids, total, vectors, bias, *up, *down)


def ffn_back(order, last, low, normal, inverse, gradtwo, gradffn, active, slope, gain, up, down):
    group = len(up)
    count, depth = low.shape
    hidden = active.shape[2]
    full = lambda shape: pl.BlockSpec(shape, lambda s: (0,) * len(shape))

    def slot_of(s):
        result = jnp.int32(order[-1])
        for position in reversed(range(len(order) - 1)):
            result = jnp.where(s == position, order[position], result)
        return result

    per_slot = pl.BlockSpec((1, count, hidden), lambda s: (slot_of(s), 0, 0))
    in_turn = lambda rows: pl.BlockSpec((1, rows, depth), lambda s: (s, 0, 0))
    shape = jax.ShapeDtypeStruct
    grads = [shape((len(order), rows, depth), bf16) for rows in (hidden, hidden + HIDDEN_EXTRA)]
    wide = shape((count, depth), f32)
    narrow = shape((count, depth), bf16)
    tail = [shape((8, depth), f32), wide, narrow] if last else [wide]
    return pl.pallas_call(
        functools.partial(ffn_back_kernel, order, last, group),
        grid=(len(order),),
        in_specs=[
            full(low.shape), full(normal.shape), full(inverse.shape), full(gradtwo.shape),
            full(gradffn.shape), per_slot, per_slot, full(gain.shape),
        ]
        + [ANYWHERE] * (2 * group),
        out_specs=[in_turn(hidden), in_turn(hidden + HIDDEN_EXTRA)] + [full(t.shape) for t in tail],
        out_shape=grads + tail,
        scratch_shapes=[
            pltpu.VMEM((2,) + up[0].shape, bf16),
            pltpu.VMEM((2,) + down[0].shape, bf16),
            pltpu.VMEM((count, hidden), bf16),
            pltpu.SemaphoreType.DMA((2, 2)),
        ]
        + ([pltpu.VMEM((count, depth), f32)] if last else []),
        cost_estimate=pl.CostEstimate(flops=2**33, bytes_accessed=2**24, transcendentals=0),
        compiler_params=pltpu.CompilerParams(vmem_limit_bytes=26 * 2**20),
        name="ffn_back",
    )(low, normal, inverse, gradtwo, gradffn, active, slope, gain, *up, *down)


HIDDEN_EXTRA = 32


def swap(value, axis, distance):
    size = lax.axis_size(axis)
    return lax.ppermute(value, axis, [(i, i ^ distance) for i in range(size)])


def add_low(a, b):
    return (a.astype(f32) + b.astype(f32)).astype(bf16)


def hold(value, *others):
    return lax.optimization_barrier((value,) + tuple(others))[0]


def row_distances(size):
    distance, result = 1, []
    while distance < size:
        result.append(distance)
        distance *= 2
    return result


def split_rows(value, distance, axis=0):
    upper = (lax.axis_index("rows") // distance) % 2 == 1
    half = value.shape[axis] // 2
    low_part = lax.slice_in_dim(value, 0, half, axis=axis)
    high_part = lax.slice_in_dim(value, half, 2 * half, axis=axis)
    return jnp.where(upper, low_part, high_part), jnp.where(upper, high_part, low_part)


def join_rows(value, arrived, distance):
    upper = (lax.axis_index("rows") // distance) % 2 == 1
    return jnp.concatenate(
        [jnp.where(upper, arrived, value), jnp.where(upper, value, arrived)], axis=0
    )


def halved(value, axis=0):
    distances = row_distances(lax.axis_size("rows"))
    taken, rows = [], value.shape[axis]
    for distance in distances[:-1]:
        if rows % 16:
            break
        taken.append(distance)
        rows //= 2
    return taken, distances[len(taken) :]


def gather_slots(value):
    slots = [value]
    distance = 1
    group = lax.axis_size("heads")
    slots = {0: value}
    distance = group // 2
    while distance >= 1:
        for slot in list(slots):
            slots[slot ^ distance] = swap(slots[slot], "heads", distance)
        distance //= 2
    return [slots[j] for j in range(group)]


def gather_frames(slots, full_shape):
    position = lax.axis_index("heads")
    size = slots[0].shape[0]
    result = jnp.zeros((full_shape[0] * full_shape[1], full_shape[2]), slots[0].dtype)
    for slot, piece in enumerate(slots):
        result = lax.dynamic_update_slice(result, piece, ((position ^ slot) * size, 0))
    return result.reshape(full_shape)


def per_device(
    frames, segment_ids, cotangent, query_weight, query_bias, key_weight, value_weight, value_bias,
    output_weight, output_bias, first_gain, first_shift, inner_weight, inner_bias, outer_weight,
    outer_bias, second_gain, second_shift,
):
    group = lax.axis_size("heads")
    position = lax.axis_index("heads")
    row_count, row_length, depth = frames.shape
    own_len = row_count * row_length // group
    size = math.gcd(row_length, own_len)
    steps = own_len // size
    per_row = row_length // size
    width = query_weight.shape[1]
    heads_here = width // HEAD_DIM
    per_head = FF_LIVE // HEADS_LIVE
    hidden_slots = inner_weight.shape[1]
    hidden_cap = min(hidden_slots, (HEADS_LIVE + group - 1) // group * per_head)

    def live_of(index):
        return HEADS_LIVE // group + (index < HEADS_LIVE % group).astype(jnp.int32)

    place = jnp.stack(
        [position * steps, jnp.int32(per_row), position]
        + [live_of(position ^ slot) for slot in range(group)]
    )
    weight_own = prepare(place, query_weight.T, key_weight.T, value_weight.T, output_weight)
    weight = {0: weight_own, 1: swap(weight_own, "heads", 1), 2: swap(weight_own, "heads", 2)}
    weight[3] = swap(weight[2], "heads", 1)
    bias_own = jnp.zeros((8, hidden_cap), f32)
    for index, part in enumerate((query_bias, value_bias, inner_bias[:hidden_cap])):
        bias_own = bias_own.at[index, : part.shape[0]].set(part)
    bias = gather_slots(bias_own)
    up_own, down_own, keyf, queryf = prepare_wide(
        place, inner_weight, outer_weight, segment_ids,
        segment_ids.reshape(row_count * per_row, 1, size), hidden_cap,
    )
    blocks = frames.reshape(row_count * per_row, size, depth)
    total = (steps, None)
    saved = []

    def forward(slot, total, *waits):
        result, *kept = attend(
            slot, place, hold(blocks, *waits), frames, weight[slot], bias[slot], keyf, queryf, total
        )
        saved.append(kept)
        return steps, result

    up = {0: up_own, 1: swap(up_own, "heads", 1)}
    down = {0: down_own, 1: swap(down_own, "heads", 1)}
    total = forward(0, total)
    total = forward(1, total)
    up[2] = swap(hold(up_own, weight[2], total[1]), "heads", 2)
    total = forward(2, total)
    down[2] = swap(hold(down_own, up[2]), "heads", 2)
    total = forward(3, total, up[1], down[1])
    up[3] = swap(up[2], "heads", 1)
    down[3] = swap(down[2], "heads", 1)
    up = [up[slot] for slot in range(group)]
    down = [down[slot] for slot in range(group)]
    attended = total[1].reshape(own_len, depth)

    vectors = jnp.stack(
        [output_bias, first_gain, first_shift, outer_bias, second_gain, second_shift]
    )
    bias_up = jnp.stack([bias[slot][2] for slot in range(group)])
    whole_frames = frames.reshape(group, own_len, depth)
    whole_cot = cotangent.reshape(group, own_len, depth)
    flat_ids = segment_ids.reshape(row_count * row_length)
    ids_own = lax.dynamic_slice_in_dim(flat_ids, position * own_len, own_len)[:, None]
    layer_own, normed_low, normal_one, inverse_one, grad_two, grad_ffn, small_two, actives, slopes = ffn(
        place, whole_frames, whole_cot, ids_own, attended, vectors, bias_up, up, down
    )
    layer = {0: layer_own, 1: swap(layer_own, "heads", 1), 2: swap(layer_own, "heads", 2)}
    layer[3] = swap(layer[2], "heads", 1)
    gain = first_gain[None]
    known = (normed_low, normal_one, inverse_one)
    down_send, up_send, grad_part = ffn_back(
        (1, 3), False, *known, grad_two, grad_ffn, actives, slopes, gain, up, down
    )
    down_came = swap(down_send, "heads", 1)
    up_came = swap(up_send, "heads", 1)
    down_keep, up_keep, small_one, grad_hidden_one, grad_attn = ffn_back(
        (0, 2), True, *known, grad_part, grad_ffn, actives, slopes, gain, up, down
    )
    distances = row_distances(lax.axis_size("rows"))
    grad_attn = grad_attn.reshape(steps, size, depth)
    block_sum = grad_hidden_one.reshape(steps, size, depth)

    down_zero = add_low(down_keep[0], down_came[0])
    down_two = swap(add_low(down_keep[1], down_came[1]), "heads", 2)
    up_pair = add_low(up_keep, up_came)
    up_taken, up_left = halved(up_pair, 1)
    up_sent, up_mine = split_rows(up_pair, up_taken[0], 1)
    up_sent = swap(up_sent, "rows", up_taken[0])

    smalls = (small_one, small_two)
    zero_rows = jnp.zeros((8, 128), f32)
    grads = {}

    def back(slot, first, block_sum, row_sum, *waits):
        return attend_back(
            slot, first, place, blocks, frames, weight[slot], saved[slot], grad_attn,
            hold(block_sum, *waits), smalls, row_sum,
        )

    grads[3], block_sum, row_sum = back(3, True, block_sum, zero_rows)
    grads_came = swap(grads[3], "heads", 1)
    grads[2], block_sum, row_sum = back(2, False, block_sum, row_sum)

    attn_two = swap(hold(add_low(grads[2], grads_came), down_two), "heads", 2)
    down_half = add_low(down_zero, down_two)
    down_taken, down_left = halved(down_half)
    up_pair = add_low(up_mine, up_sent)
    down_sent, down_mine = split_rows(hold(down_half, up_sent), down_taken[0])
    down_sent = swap(down_sent, "rows", down_taken[0])
    for distance in up_taken[1:]:
        up_sent, up_mine = split_rows(up_pair, distance, 1)
        up_sent = swap(up_sent, "rows", distance)
        up_pair = add_low(up_mine, up_sent)
    grads[1], block_sum, row_sum = back(1, False, block_sum, row_sum, layer[3])
    grads_came = swap(grads[1], "heads", 1)
    down_half = add_low(down_mine, down_sent)
    for distance in down_taken[1:]:
        down_sent, down_mine = split_rows(hold(down_half, up_pair), distance)
        down_sent = swap(down_sent, "rows", distance)
        down_half = add_low(down_mine, down_sent)
    up_piece = add_low(up_pair[0], swap(up_pair[1], "heads", 2))
    grads[0], block_sum, row_sum = back(0, False, block_sum, row_sum, up_pair, down_sent)

    def finish(value, taken, left):
        for distance in left:
            value = add_low(value, swap(value, "rows", distance))
        for distance in reversed(taken):
            value = join_rows(value, swap(value, "rows", distance), distance)
        return value

    down_sum = finish(down_half, down_taken, down_left).astype(f32)
    up_sum = finish(up_piece, up_taken, up_left).astype(f32)
    attn_half = add_low(add_low(grads[0], grads_came), attn_two)
    attn_taken, attn_left = halved(attn_half)
    for distance in attn_taken:
        attn_sent, attn_mine = split_rows(attn_half, distance)
        attn_half = add_low(attn_mine, swap(attn_sent, "rows", distance))
    attn_sum = finish(attn_half, attn_taken, attn_left).astype(f32)

    first_row = position * steps // per_row
    touched = (position * steps + steps - 1) // per_row > first_row
    row_sum = jnp.where(
        (jnp.arange(row_sum.shape[0]) == 0)[:, None, None] | touched, row_sum, 0.0
    )
    spread = jnp.zeros((row_count + 1, row_length, depth), f32)
    spread = lax.dynamic_update_slice(spread, row_sum, (first_row, 0, 0))[:row_count]
    pieces = spread.reshape(group, own_len, depth)

    def piece_of(index):
        return lax.dynamic_index_in_dim(pieces, index, 0, keepdims=False)

    own_grad = block_sum.reshape(own_len, depth) + piece_of(position)
    for distance in range(1, group):
        pairs = []
        for i in range(group):
            j = i ^ distance
            rows_i = range(i * steps // per_row, ((i + 1) * steps - 1) // per_row + 1)
            rows_j = range(j * steps // per_row, ((j + 1) * steps - 1) // per_row + 1)
            if set(rows_i) & set(rows_j):
                pairs.append((i, j))
        if pairs:
            sent = piece_of(position ^ distance).astype(bf16)
            own_grad = own_grad + lax.ppermute(sent, "heads", pairs).astype(f32)
    frames_grad = gather_frames(gather_slots(own_grad.astype(bf16)), frames.shape)
    layer_out = gather_frames([layer[slot] for slot in range(group)], frames.shape)

    hidden_mask = (jnp.arange(hidden_cap, dtype=jnp.int32) < live_of(position) * per_head)[:, None]
    padding = hidden_slots - hidden_cap
    inner_full = jnp.pad(up_sum[:hidden_cap], ((0, padding), (0, 0))).T
    outer_full = jnp.pad(jnp.where(hidden_mask, down_sum, 0), ((0, padding), (0, 0)))
    innerbias = jnp.concatenate([up_sum[hidden_cap], up_sum[hidden_cap + 1, : hidden_cap - depth]])
    innerbias_full = jnp.pad(innerbias, ((0, padding),))
    extra = attn_sum[4 * width :]
    return (
        layer_out,
        frames_grad,
        attn_sum[:width].T,
        extra[0, :width],
        attn_sum[width : 2 * width].T,
        attn_sum[2 * width : 3 * width].T,
        extra[1, :width],
        attn_sum[3 * width : 4 * width],
        extra[4],
        extra[2],
        extra[3],
        inner_full,
        innerbias_full,
        outer_full,
        extra[7],
        extra[5],
        extra[6],
    )


def solution(mesh):
    in_specs = (
        P("rows", None, None), P("rows", None), P("rows", None, None), P(None, "heads"), P("heads"),
        P(None, "heads"), P(None, "heads"), P("heads"), P("heads", None), P(), P(), P(),
        P(None, "heads"), P("heads"), P("heads", None), P(), P(), P(),
    )
    out_specs = (
        P("rows", None, None), P("rows", None, None), P(None, "heads"), P("heads"), P(None, "heads"),
        P(None, "heads"), P("heads"), P("heads", None), P(), P(), P(), P(None, "heads"), P("heads"),
        P("heads", None), P(), P(), P(),
    )
    return jax.shard_map(
        per_device, mesh=mesh, in_specs=in_specs, out_specs=out_specs, check_vma=False
    )
```

```python
import functools
import math

import jax
import jax.numpy as jnp
from jax import lax
from jax.experimental import pallas as pl
from jax.experimental.pallas import tpu as pltpu
from jax.sharding import PartitionSpec as P

HEADS_LIVE = 10
HEAD_SLOTS = 12
HEAD_DIM = 64
FF_LIVE = 2240
PAD_HEAD = 128
SEGMENTS = 5
MASK_STEP = -(2.0**30)
norm_eps = 1e-05
f32 = jnp.float32
bf16 = jnp.bfloat16


def dot(a, b, ca, cb):
    return lax.dot_general(a, b, (((ca,), (cb,)), ((), ())), preferred_element_type=f32)


def three_parts(value):
    high = value.astype(bf16).astype(f32)
    middle = (value - high).astype(bf16).astype(f32)
    return high, middle, value - high - middle


def live_heads(live, heads, one_head):
    least = HEADS_LIVE * heads // HEAD_SLOTS
    for head in range(least):
        one_head(head)
    for head in range(least, heads):

        @pl.when(head < live)
        def _():
            one_head(head)


def feature_rows(base, value):
    high, middle, low = three_parts(-value)
    row = lax.broadcasted_iota(jnp.int32, base.shape, 0)
    base = jnp.where(row == SEGMENTS, high, base)
    base = jnp.where(row == SEGMENTS + 1, middle, base)
    return jnp.where(row == SEGMENTS + 2, low, base).astype(bf16)


def bias_row(rows, index):
    first = 3 * index
    return rows[first : first + 1] + rows[first + 1 : first + 2] + rows[first + 2 : first + 3]


def attend_kernel(
    first, place, block_ref, row_ref, keyf_ref, queryf_ref, *refs,
):
    pair = len(refs) - 5
    weight_refs, (query_ref, key_ref, value_ref, context_ref, weight_ref) = refs[:pair], refs[pair:]
    turn = pl.program_id(0)
    step = pl.program_id(1)
    per_row, live = place[1], place[3 + first + turn]
    row_now = (place[0] + step) // per_row
    row_before = (place[0] + step - 1) // per_row
    length = row_ref.shape[1]
    width = context_ref.shape[2]
    heads = width // HEAD_DIM

    for index, ref in enumerate(weight_refs):

        @pl.when(jnp.logical_and(step == 0, turn == index))
        def _():
            weight_ref[...] = ref[...]

    biases = weight_ref[3 * width :].astype(f32)

    @pl.when(jnp.logical_or(step == 0, row_now != row_before))
    def _():
        frames = row_ref[0]
        keys = dot(frames, weight_ref[width : 2 * width], 1, 1).astype(bf16)
        values = dot(frames, weight_ref[2 * width : 3 * width], 1, 1)
        values = (values + bias_row(biases, 1)[:, 0:width]).astype(bf16)
        features = keyf_ref[0]
        for head in range(heads):
            cut = slice(head * HEAD_DIM, (head + 1) * HEAD_DIM)
            key_ref[0, 0, head * length : (head + 1) * length] = jnp.concatenate(
                [keys[:, cut], features], axis=1
            )
            value_ref[0, 0, head * length : (head + 1) * length] = jnp.concatenate(
                [values[:, cut], features], axis=1
            )

    qbias = jnp.broadcast_to(bias_row(biases, 0)[:, 0:width], (8, width)).T[:, 0:1]
    queries = (dot(weight_ref[0:width], block_ref[0], 1, 1) + qbias).astype(bf16)
    queries = queries * jnp.asarray(HEAD_DIM**-0.5, bf16)
    for head in range(heads):
        query_ref[0, 0, head * PAD_HEAD : head * PAD_HEAD + HEAD_DIM] = queries[
            head * HEAD_DIM : (head + 1) * HEAD_DIM
        ]
        query_ref[0, 0, head * PAD_HEAD + HEAD_DIM : (head + 1) * PAD_HEAD] = queryf_ref[0]
    context_ref[...] = jnp.zeros_like(context_ref)

    def one_head(head):
        keys = key_ref[0, 0, pl.ds(head * length, length)]
        values = value_ref[0, 0, pl.ds(head * length, length)]
        start = head * PAD_HEAD
        scores = dot(keys, query_ref[0, 0, pl.ds(start, PAD_HEAD)], 1, 0)
        highest = jnp.max(scores, axis=0, keepdims=True)
        probs = jnp.exp(scores - highest).astype(bf16)
        mixed = dot(values, probs, 0, 0)
        total = mixed[HEAD_DIM + SEGMENTS : HEAD_DIM + SEGMENTS + 1]
        context = mixed[0:HEAD_DIM] / total
        context_ref[0, 0, pl.ds(head * HEAD_DIM, HEAD_DIM)] = context.astype(bf16)
        base = queryf_ref[0, 0:16].astype(f32)
        query_ref[0, 0, pl.ds(start + HEAD_DIM, 16)] = feature_rows(base, highest + jnp.log(total))

    live_heads(live, heads, one_head)


def attend_back_kernel(
    slot, first, place, block_ref, row_ref, weight_ref, query_ref, key_ref, value_ref,
    context_ref, grad_ref, blocksum_ref, rowsum_ref,
    gradw_ref, blockout_ref, rowout_ref,
    weight_acc, dkey, dvalue, picked, dcontext, dquery, bias_acc,
):
    step = pl.program_id(0)
    steps = pl.num_programs(0)
    per_row, live = place[1], place[3 + slot]
    row_now = (place[0] + step) // per_row
    row_before = (place[0] + step - 1) // per_row
    row_after = (place[0] + step + 1) // per_row
    length, depth = row_ref.shape[1:]
    width = context_ref.shape[2]
    heads = width // HEAD_DIM
    ones = jnp.ones((8, length), bf16)

    @pl.when(step == 0)
    def _():
        weight_acc[...] = jnp.zeros_like(weight_acc)
        bias_acc[...] = jnp.zeros_like(bias_acc)
        picked[...] = jnp.zeros_like(picked)

    @pl.when(jnp.logical_or(step == 0, row_now != row_before))
    def _():
        dkey[...] = jnp.zeros_like(dkey)
        dvalue[...] = jnp.zeros_like(dvalue)

    dcontext[...] = dot(weight_ref[3 * width + BIAS_ROWS :], grad_ref[0], 1, 1).astype(bf16)
    dquery[...] = jnp.zeros_like(dquery)

    def one_head(head):
        own = pl.ds(head * HEAD_DIM, HEAD_DIM)
        keys = key_ref[0, 0, pl.ds(head * length, length)]
        values = value_ref[0, 0, pl.ds(head * length, length)]
        queries = query_ref[0, 0, pl.ds(head * PAD_HEAD, PAD_HEAD)]
        grad = dcontext[own]
        inner = jnp.sum(grad.astype(f32) * context_ref[0, 0, own].astype(f32), axis=0, keepdims=True)
        extra = feature_rows(jnp.zeros((PAD_HEAD - HEAD_DIM, grad.shape[1]), f32), inner)
        probs = jnp.exp(dot(keys, queries, 1, 0))
        dprobs = dot(values, jnp.concatenate([grad, extra], axis=0), 1, 0)
        dscores = (probs * dprobs).astype(bf16)
        picked[0, pl.ds(head * width + head * HEAD_DIM, HEAD_DIM)] = grad
        picked[1, pl.ds(head * width + head * HEAD_DIM, HEAD_DIM)] = queries[0:HEAD_DIM]
        place_head = pl.ds(head * width, width)
        dvalue[...] += dot(probs.astype(bf16), picked[0, place_head], 1, 1)
        dkey[...] += dot(dscores, picked[1, place_head], 1, 1)
        dquery[own] = (dot(keys, dscores, 0, 0)[0:HEAD_DIM] * HEAD_DIM**-0.5).astype(bf16)

    live_heads(live, heads, one_head)
    weight_acc[0:width] += dot(dquery[...], block_ref[0], 1, 0)
    blockout_ref[0] = blocksum_ref[0] + dot(dquery[...], weight_ref[0:width], 0, 0)
    bias_acc[0:8] += dot(ones[:, 0 : dquery.shape[1]], dquery[...], 1, 1)

    @pl.when(jnp.logical_or(step == steps - 1, row_now != row_after))
    def _():
        keys_low = dkey[...].astype(bf16)
        values_low = dvalue[...].astype(bf16)
        weight_acc[width : 2 * width] += dot(keys_low, row_ref[0], 0, 0)
        weight_acc[2 * width : 3 * width] += dot(values_low, row_ref[0], 0, 0)
        back = dot(keys_low, weight_ref[width : 2 * width], 1, 0) + dot(
            values_low, weight_ref[2 * width : 3 * width], 1, 0
        )
        if first:
            rowout_ref[0] = back
        else:
            rowout_ref[0] = rowsum_ref[0] + back
        bias_acc[8:16] += dot(ones, values_low, 1, 0)

    @pl.when(step == steps - 1)
    def _():
        gradw_ref[0 : 3 * width] = weight_acc[...].astype(bf16)
        row = lax.broadcasted_iota(jnp.int32, (gradw_ref.shape[0] - 3 * width, depth), 0)
        lanes = depth - width
        extra = jnp.where(row == 0, jnp.pad(bias_acc[0:1], ((0, 0), (0, lanes))), 0.0)
        extra = jnp.where(row == 1, jnp.pad(bias_acc[8:9], ((0, 0), (0, lanes))), extra)
        gradw_ref[3 * width :] = extra.astype(bf16)


def whole(shape):
    return pl.BlockSpec(shape, lambda b, place: (0,) * len(shape))


def limit(mib):
    return pltpu.CompilerParams(vmem_limit_bytes=mib * 2**20)


def cost(flops):
    return pl.CostEstimate(flops=2**40, bytes_accessed=2**33, transcendentals=0)


ANYWHERE = pl.BlockSpec(memory_space=pltpu.HBM)


def far_away(value):
    return pltpu.with_memory_space_constraint(value, pltpu.HBM)
BIAS_ROWS = 16
EXTRA_ROWS = 64
HIDDEN_EXTRA = 32


def row_of(b, place):
    return (place[0] + b) // place[1], 0, 0


def rel_row(b, place):
    return (place[0] + b) // place[1] - place[0] // place[1], 0, 0


def block_of(b, place):
    return place[0] + b, 0, 0


def local(b, place):
    return b, 0, 0


def attend(first, place, blocks, rows, weights, keyf, queryf, steps, width):
    size, depth = blocks.shape[1:]
    count, length, _ = rows.shape
    weight_shape = (3 * width + BIAS_ROWS, depth)
    heads = width // HEAD_DIM
    window = min(2, count)
    pair = len(weights)
    fixed = lambda shape: pl.BlockSpec(shape, lambda s, b, place: (0,) * len(shape))
    per_row = lambda shape: pl.BlockSpec((1,) + shape, lambda s, b, place: row_of(b, place))
    per_block = lambda shape: pl.BlockSpec((1,) + shape, lambda s, b, place: block_of(b, place))
    out_row = pl.BlockSpec(
        (1, 1, heads * length, PAD_HEAD), lambda s, b, place: (s,) + rel_row(b, place)
    )
    out_block = lambda rows: pl.BlockSpec((1, 1, rows, size), lambda s, b, place: (s, b, 0, 0))
    spec = pltpu.PrefetchScalarGridSpec(
        num_scalar_prefetch=1,
        grid=(pair, steps),
        in_specs=[
            per_block((size, depth)), per_row((length, depth)), per_row(keyf.shape[1:]),
            per_block(queryf.shape[1:]),
        ]
        + [fixed(weight_shape)] * pair,
        out_specs=[out_block(heads * PAD_HEAD), out_row, out_row, out_block(width)],
        scratch_shapes=[pltpu.VMEM(weight_shape, bf16)],
    )
    return pl.pallas_call(
        functools.partial(attend_kernel, first),
        grid_spec=spec,
        out_shape=[
            jax.ShapeDtypeStruct((pair, steps, heads * PAD_HEAD, size), bf16),
            jax.ShapeDtypeStruct((pair, window, heads * length, PAD_HEAD), bf16),
            jax.ShapeDtypeStruct((pair, window, heads * length, PAD_HEAD), bf16),
            jax.ShapeDtypeStruct((pair, steps, width, size), bf16),
        ],
        cost_estimate=cost(2**33),
        compiler_params=limit(FORWARD_LIMIT),
        name="attend",
    )(place, blocks, rows, keyf, queryf, *weights)


FORWARD_LIMIT = 60


def attend_back(slot, first, place, blocks, rows, weight, saved, grad, blocksum, rowsum):
    query, key, value, context = saved
    steps, size, depth = blocksum.shape
    count, length, _ = rows.shape
    width = context.shape[2]
    heads = width // HEAD_DIM
    turn = slot % query.shape[0]
    saved_block = lambda v: pl.BlockSpec(
        (1, 1) + v.shape[2:], lambda b, place: (turn,) + local(b, place)
    )
    saved_row = lambda v: pl.BlockSpec(
        (1, 1) + v.shape[2:], lambda b, place: (turn,) + rel_row(b, place)
    )
    row_spec = pl.BlockSpec((1, length, depth), rel_row)
    near = far_away if first else lambda value: value
    spec = pltpu.PrefetchScalarGridSpec(
        num_scalar_prefetch=1,
        grid=(steps,),
        in_specs=[
            pl.BlockSpec((1, size, depth), block_of),
            pl.BlockSpec((1, length, depth), row_of),
            whole((4 * width + BIAS_ROWS, depth)),
            saved_block(query), saved_row(key), saved_row(value), saved_block(context),
            pl.BlockSpec((1, size, depth), local),
            pl.BlockSpec((1, size, depth), local),
            ANYWHERE if first else row_spec,
        ],
        out_specs=[
            whole((3 * width + EXTRA_ROWS, depth)),
            pl.BlockSpec((1, size, depth), local),
            row_spec,
        ],
        scratch_shapes=[
            pltpu.VMEM((3 * width, depth), f32),
            pltpu.VMEM((length, width), f32),
            pltpu.VMEM((length, width), f32),
            pltpu.VMEM((2, heads * width, size), bf16),
            pltpu.VMEM((width, size), bf16),
            pltpu.VMEM((width, size), bf16),
            pltpu.VMEM((16, width), f32),
        ],
    )
    return pl.pallas_call(
        functools.partial(attend_back_kernel, slot, first),
        grid_spec=spec,
        out_shape=[
            jax.ShapeDtypeStruct((3 * width + EXTRA_ROWS, depth), bf16),
            jax.ShapeDtypeStruct(blocksum.shape, f32),
            jax.ShapeDtypeStruct((min(2, count), length, depth), f32),
        ],
        input_output_aliases={} if first else {10: 2},
        cost_estimate=cost(2**34),
        compiler_params=limit(26),
        name="attend_back",
    )(
        place, near(blocks), near(rows), near(weight), query, near(key), near(value), context, grad,
        blocksum, rowsum,
    )


def prepare_kernel(
    per_head, place, query_ref, key_ref, value_ref, qbias_ref, vbias_ref, ubias_ref, out_ref, down_ref,
    weight_ref,
):
    width, depth = query_ref.shape
    weight_ref[0:width] = query_ref[...]
    weight_ref[width : 2 * width] = key_ref[...]
    weight_ref[2 * width : 3 * width] = value_ref[...]
    lanes = ubias_ref.shape[1]
    row = lax.broadcasted_iota(jnp.int32, (BIAS_ROWS, depth), 0)
    result = jnp.zeros((BIAS_ROWS, depth), f32)
    vectors = [
        jnp.pad(qbias_ref[...], ((0, 0), (0, depth - width))),
        jnp.pad(vbias_ref[...], ((0, 0), (0, depth - width))),
        ubias_ref[:, 0:depth],
        jnp.pad(ubias_ref[:, depth:lanes], ((0, 0), (0, 2 * depth - lanes))),
    ]
    for index, vector in enumerate(vectors):
        for offset, part in enumerate(three_parts(vector)):
            result = jnp.where(row == 3 * index + offset, part, result)
    first = 3 * width + BIAS_ROWS
    weight_ref[3 * width : first] = result.astype(bf16)
    row = lax.broadcasted_iota(jnp.int32, out_ref.shape, 0)
    kept = jnp.where(row < place[3] * HEAD_DIM, out_ref[...].astype(f32), 0.0)
    weight_ref[first : first + width] = kept.astype(bf16)
    piece = weight_ref.shape[0] - first - width
    start = place[3 + SLOT_COUNT]
    row = start + lax.broadcasted_iota(jnp.int32, (piece, depth), 0)
    kept = down_ref[pl.ds(pl.multiple_of(start, 8), piece)].astype(f32)
    weight_ref[first + width :] = jnp.where(row < place[3] * per_head, kept, 0.0).astype(bf16)


SLOT_COUNT = 4


def prepare(place, query, key, value, qbias, vbias, ubias, out, down, piece):
    width, depth = query.shape
    shape = (4 * width + BIAS_ROWS + piece, depth)
    args = (query, key, value, qbias, vbias, ubias, out, down)
    return pl.pallas_call(
        functools.partial(prepare_kernel, FF_LIVE // HEADS_LIVE),
        grid_spec=pltpu.PrefetchScalarGridSpec(
            num_scalar_prefetch=1,
            grid=(1,),
            in_specs=[whole(v.shape) for v in args],
            out_specs=whole(shape),
        ),
        out_shape=jax.ShapeDtypeStruct(shape, bf16),
        compiler_params=limit(60),
        name="prepare",
    )(place, *args)


def prepare_wide_kernel(
    per_head, place, up_ref, down_ref, ids_ref, blocks_ref,
    upout_ref, downout_ref, keyf_ref, queryf_ref,
):
    hidden = downout_ref.shape[0]
    upout_ref[...] = up_ref[...].T[0:hidden]
    row = lax.broadcasted_iota(jnp.int32, downout_ref.shape, 0)
    kept = jnp.where(row < place[3] * per_head, down_ref[0:hidden].astype(f32), 0.0)
    downout_ref[...] = kept.astype(bf16)
    rows, length = ids_ref.shape
    feature = lax.broadcasted_iota(jnp.int32, (HEAD_DIM, length), 0)
    for r in range(rows):
        same = jnp.where(feature == ids_ref[r : r + 1] + 1, 1.0, 0.0)
        ones = jnp.where(jnp.logical_and(feature >= SEGMENTS, feature < SEGMENTS + 3), 1.0, same)
        keyf_ref[r] = ones.T.astype(bf16)
    size = blocks_ref.shape[2]
    feature = lax.broadcasted_iota(jnp.int32, (HEAD_DIM, size), 0)
    for b in range(blocks_ref.shape[0]):
        other = jnp.logical_and(feature < SEGMENTS, feature != blocks_ref[b] + 1)
        queryf_ref[b] = jnp.where(other, MASK_STEP, 0.0).astype(bf16)


def prepare_wide(place, up, down, ids, id_blocks, hidden):
    depth = up.shape[0]
    rows, length = ids.shape
    shapes = [
        (hidden, depth), (hidden, depth), (rows, length, HEAD_DIM),
        (id_blocks.shape[0], HEAD_DIM, id_blocks.shape[2]),
    ]
    return pl.pallas_call(
        functools.partial(prepare_wide_kernel, FF_LIVE // HEADS_LIVE),
        grid_spec=pltpu.PrefetchScalarGridSpec(
            num_scalar_prefetch=1,
            grid=(1,),
            in_specs=[whole(v.shape) for v in (up, down, ids, id_blocks)],
            out_specs=[whole(shape) for shape in shapes],
        ),
        out_shape=[jax.ShapeDtypeStruct(shape, bf16) for shape in shapes],
        compiler_params=limit(60),
        name="prepare_wide",
    )(place, up, down, ids, id_blocks)


def assemble_kernel(place, *refs):
    step = pl.program_id(0)
    for slot, ref in enumerate(refs[:-1]):

        @pl.when(step == slot)
        def _():
            refs[-1][0] = ref[...]


def assemble(place, slots):
    count, depth = slots[0].shape
    return pl.pallas_call(
        assemble_kernel,
        grid_spec=pltpu.PrefetchScalarGridSpec(
            num_scalar_prefetch=1,
            grid=(len(slots),),
            in_specs=[whole((count, depth)) for _ in slots],
            out_specs=pl.BlockSpec((1, count, depth), lambda s, place: (place[2] ^ s, 0, 0)),
        ),
        out_shape=jax.ShapeDtypeStruct((len(slots), count, depth), slots[0].dtype),
        compiler_params=limit(12),
        name="assemble",
    )(place, *slots)


def shares_kernel(distances, group, place, *refs):
    step = pl.program_id(0)
    steps = pl.num_programs(0)
    count = len(distances)
    sources, blocksum_ref, (own_ref, *sent_refs) = refs[:count], refs[count], refs[count + 1 :]
    rows_touched = (place[0] + steps - 1) // place[1] - place[0] // place[1] + 1
    for distance, source, target in zip(distances, sources, (own_ref, *sent_refs)):
        block = (place[2] ^ distance) * steps + step - place[0] // place[1] * place[1]
        inside = jnp.logical_and(block >= 0, block < rows_touched * place[1])
        value = jnp.where(inside, source[0], 0.0)
        if distance == 0:
            target[0] = blocksum_ref[0] + value
        else:
            target[0] = value.astype(bf16)


def shares(place, rowsum, blocksum, distances):
    steps, size, depth = blocksum.shape
    group = None
    window = rowsum.reshape(-1, size, depth)

    def source(distance):
        def index(b, place):
            block = (place[2] ^ distance) * steps + b - place[0] // place[1] * place[1]
            return jnp.clip(block, 0, window.shape[0] - 1), 0, 0

        return pl.BlockSpec((1, size, depth), index)

    block = pl.BlockSpec((1, size, depth), local)
    return pl.pallas_call(
        functools.partial(shares_kernel, distances, group),
        grid_spec=pltpu.PrefetchScalarGridSpec(
            num_scalar_prefetch=1,
            grid=(steps,),
            in_specs=[source(d) for d in distances] + [block],
            out_specs=[block for _ in distances],
        ),
        out_shape=[
            jax.ShapeDtypeStruct(blocksum.shape, bf16 if d else f32) for d in distances
        ],
        compiler_params=limit(12),
        name="shares",
    )(place, *[window for _ in distances], blocksum)


def row_chunks(count, body):
    chunk = 200 if count % 200 == 0 else 16

    @pl.loop(0, count // chunk)
    def _(i):
        body(pl.ds(pl.multiple_of(i * chunk, 8), chunk))

    if count % chunk:
        body(pl.ds(count // chunk * chunk, count % chunk))


def phi_parts(value):
    bell = jnp.exp(value * value * -0.5)
    t = 1.0 / (1.0 + jnp.abs(value) * (0.3275911 * 0.5**0.5))
    poly = t * (
        0.254829592
        + t * (-0.284496736 + t * (1.421413741 + t * (-1.453152027 + t * 1.061405429)))
    )
    half = 0.5 * poly * bell
    return jnp.where(value >= 0, 1.0 - half, half), bell * (2.0 * math.pi) ** -0.5


def chunk_stats(value):
    centre = value - jnp.mean(value, axis=-1, keepdims=True)
    inverse = lax.rsqrt(jnp.mean(centre * centre, axis=-1, keepdims=True) + norm_eps)
    return centre * inverse, inverse


def fetch_slot(order, step, sources, buffers, sems):
    for which, (refs, buffer) in enumerate(zip(sources, buffers)):
        for position, slot in enumerate(order):

            @pl.when(step == position)
            def _():
                pltpu.make_async_copy(refs[slot], buffer.at[step % 2], sems.at[which, step % 2]).start()


def await_slot(step, sources, buffers, sems):
    for which, (refs, buffer) in enumerate(zip(sources, buffers)):
        pltpu.make_async_copy(refs[0], buffer.at[step % 2], sems.at[which, step % 2]).wait()


def stream_slots(order, sources, buffers, sems):
    step = pl.program_id(0)

    @pl.when(step == 0)
    def _():
        fetch_slot(order, step, sources, buffers, sems)

    @pl.when(step + 1 < pl.num_programs(0))
    def _():
        fetch_slot(order, step + 1, sources, buffers, sems)

    await_slot(step, sources, buffers, sems)


def fetch_slot(order, step, sources, buffers, sems, firsts):
    for which, (refs, buffer, first) in enumerate(zip(sources, buffers, firsts)):
        for position, slot in enumerate(order):

            @pl.when(step == position)
            def _():
                pltpu.make_async_copy(
                    refs[slot].at[pl.ds(first, buffer.shape[1])],
                    buffer.at[step % 2],
                    sems.at[which, step % 2],
                ).start()


def stream_slots(order, sources, buffers, sems, firsts):
    step = pl.program_id(0)

    @pl.when(step == 0)
    def _():
        fetch_slot(order, step, sources, buffers, sems, firsts)

    @pl.when(step + 1 < pl.num_programs(0))
    def _():
        fetch_slot(order, step + 1, sources, buffers, sems, firsts)

    for which, (refs, buffer, first) in enumerate(zip(sources, buffers, firsts)):
        pltpu.make_async_copy(
            refs[0].at[pl.ds(first, buffer.shape[1])], buffer.at[step % 2], sems.at[which, step % 2]
        ).wait()


def ffn_kernel(
    group, place, frames_ref, cot_ref, ids_ref, vec_ref, *refs,
):
    held = len(refs) - 17 - 3 * group
    context_refs, refs = refs[:held], refs[held:]
    weight_refs, refs = refs[:group], refs[group:]
    up_refs, down_refs = refs[:group], refs[group : 2 * group]
    (
        layer_ref, low_ref, normal_ref, inverse_ref, gradtwo_ref, gradffn_ref, small_ref,
        active_ref, slope_ref, up_buf, down_buf, out_buf, bias_buf, pre, mixed, sems, out_sems,
    ) = refs[2 * group :]
    turns = group // held
    step = pl.program_id(0)
    count, depth = mixed.shape
    hidden = pre.shape[1]
    width = out_buf.shape[1]
    out_bias, gain_one, shift_one = vec_ref[0:1], vec_ref[1:2], vec_ref[2:3]
    outer_bias, gain_two, shift_two = vec_ref[3:4], vec_ref[4:5], vec_ref[5:6]

    def out_copies(slot):
        return [
            pltpu.make_async_copy(
                weight_refs[slot].at[pl.ds(first, target.shape[1])], target.at[slot], out_sems.at[which, slot]
            )
            for which, (target, first) in enumerate(
                ((out_buf, 3 * width + BIAS_ROWS), (bias_buf, 3 * width))
            )
        ]

    @pl.when(step == 0)
    def _():
        for slot in range(group):
            for copy in out_copies(slot):
                copy.start()

    stream_slots(tuple(range(group)), (up_refs, down_refs), (up_buf, down_buf), sems, (0, 0))

    @pl.when(step == 0)
    def _():
        for slot in range(group):
            for copy in out_copies(slot):
                copy.wait()
        _, blocks, _, size = context_refs[0].shape
        for block in range(blocks):
            total = dot(context_refs[0][0, block], out_buf[0], 0, 0)
            for slot in range(1, group):
                total += dot(context_refs[slot // turns][slot % turns, block], out_buf[slot], 0, 0)
            mixed[block * size : (block + 1) * size] = total

        def first(rows):
            hidden_one = frames_ref[0, rows].astype(f32) + mixed[rows] + out_bias
            normal, inverse = chunk_stats(hidden_one)
            normal_ref[rows] = normal
            inverse_ref[rows] = inverse
            normed = normal * gain_one + shift_one
            low_ref[rows] = normed.astype(bf16)
            mixed[rows] = normed + outer_bias

        row_chunks(count, first)

    biases = bias_buf[step].astype(f32)
    bias = jnp.concatenate([bias_row(biases, 2), bias_row(biases, 3)[:, 0 : hidden - depth]], axis=1)
    pre[...] = dot(low_ref[...], up_buf[step % 2], 1, 1) + bias

    def gelu(rows):
        value = pre[rows]
        whole_part, bell = phi_parts(value)
        active_ref[0, rows] = (value * whole_part).astype(bf16)
        slope_ref[0, rows] = (whole_part + value * bell).astype(bf16)

    row_chunks(count, gelu)
    mixed[...] += dot(active_ref[0], down_buf[step % 2], 1, 0)

    @pl.when(step == pl.num_programs(0) - 1)
    def _():
        small_ref[...] = jnp.zeros_like(small_ref)

        def last(rows):
            normal, inverse = chunk_stats(mixed[rows])
            live = (ids_ref[rows] >= 0).astype(f32)
            layer_ref[rows] = ((normal * gain_two + shift_two) * live).astype(bf16)
            grad = cot_ref[0, rows].astype(f32) * live
            small_ref[0:1] += jnp.sum(grad * normal, axis=0, keepdims=True)
            small_ref[1:2] += jnp.sum(grad, axis=0, keepdims=True)
            scaled = grad * gain_two
            back = inverse * (
                scaled
                - jnp.mean(scaled, axis=-1, keepdims=True)
                - normal * jnp.mean(scaled * normal, axis=-1, keepdims=True)
            )
            small_ref[2:3] += jnp.sum(back, axis=0, keepdims=True)
            gradtwo_ref[rows] = back
            gradffn_ref[rows] = back.astype(bf16)

        row_chunks(count, last)


def up_back_kernel(
    order, last, group, low_ref, normal_ref, inverse_ref, gradtwo_ref, gradffn_ref, slope_ref,
    gain_ref, *refs,
):
    up_refs, down_refs, rest = refs[:group], refs[group : 2 * group], refs[2 * group :]
    if last:
        upgrad_ref, small_ref, gradone_ref, gradattn_ref, *rest = rest
    else:
        upgrad_ref, normed_grad, *rest = rest
    up_buf, down_buf, inner, sems, *rest = rest
    if last:
        normed_grad = rest[0]
    step = pl.program_id(0)
    count, hidden = inner.shape
    depth = low_ref.shape[1]
    stream_slots(order, (up_refs, down_refs), (up_buf, down_buf), sems, (0, 0))

    @pl.when(step == 0)
    def _():
        normed_grad[...] = gradtwo_ref[...]

    grad_active = dot(gradffn_ref[...], down_buf[step % 2], 1, 1)
    inner[...] = (grad_active * slope_ref[0].astype(f32)).astype(bf16)
    upgrad_ref[0, 0:hidden] = dot(inner[...], low_ref[...], 0, 0).astype(bf16)
    ones = jnp.ones((8, count), bf16)
    bias = dot(ones, inner[...], 1, 0)
    row = lax.broadcasted_iota(jnp.int32, (upgrad_ref.shape[1] - hidden, depth), 0)
    extra = jnp.where(row == 0, bias[0:1, 0:depth], 0.0)
    rest_lanes = jnp.pad(bias[0:1, depth:hidden], ((0, 0), (0, 2 * depth - hidden)))
    upgrad_ref[0, hidden:] = jnp.where(row == 1, rest_lanes, extra).astype(bf16)
    normed_grad[...] += dot(inner[...], up_buf[step % 2], 1, 0)

    if last:

        @pl.when(step == pl.num_programs(0) - 1)
        def _():
            small_ref[...] = jnp.zeros_like(small_ref)
            gain = gain_ref[...]

            def last_rows(rows):
                grad, normal = normed_grad[rows], normal_ref[rows]
                small_ref[0:1] += jnp.sum(grad * normal, axis=0, keepdims=True)
                small_ref[1:2] += jnp.sum(grad, axis=0, keepdims=True)
                scaled = grad * gain
                back = inverse_ref[rows] * (
                    scaled
                    - jnp.mean(scaled, axis=-1, keepdims=True)
                    - normal * jnp.mean(scaled * normal, axis=-1, keepdims=True)
                )
                small_ref[2:3] += jnp.sum(back, axis=0, keepdims=True)
                gradone_ref[rows] = back
                gradattn_ref[rows] = back.astype(bf16)

            row_chunks(count, last_rows)


def down_back_kernel(
    order, group, active_ref, gradffn_ref, gradattn_ref, small_ref, smalltwo_ref, *refs
):
    context_refs, result_ref = refs[:-1], refs[-1]
    turns = group // len(context_refs)
    step = pl.program_id(0)
    hidden = active_ref.shape[2]
    depth = gradffn_ref.shape[1]
    _, blocks, width, size = context_refs[0].shape
    result_ref[0, 0:hidden] = dot(active_ref[0], gradffn_ref[...], 0, 0).astype(bf16)
    for position, slot in enumerate(order):

        @pl.when(step == position)
        def _():
            context = context_refs[slot // turns].at[slot % turns]
            total = dot(context[0], gradattn_ref[0:size], 1, 0)
            for block in range(1, blocks):
                total += dot(context[block], gradattn_ref[block * size : (block + 1) * size], 1, 0)
            result_ref[0, hidden : hidden + width] = total.astype(bf16)

    row = lax.broadcasted_iota(jnp.int32, (HIDDEN_EXTRA, depth), 0)
    extra = jnp.zeros((HIDDEN_EXTRA, depth), f32)
    for index in range(3):
        extra = jnp.where(row == index, small_ref[index : index + 1], extra)
        extra = jnp.where(row == 3 + index, smalltwo_ref[index : index + 1], extra)
    result_ref[0, hidden + width :] = extra.astype(bf16)


def ffn(place, frames, cotangent, ids, vectors, contexts, weights, up, down):
    group = len(up)
    count, depth = frames.shape[1:]
    hidden = down[0].shape[0]
    width = contexts[0].shape[2]
    own = pl.BlockSpec((1, count, depth), lambda s, place: (place[2], 0, 0))
    per_slot = pl.BlockSpec((1, count, hidden), lambda s, place: (s, 0, 0))
    spec = pltpu.PrefetchScalarGridSpec(
        num_scalar_prefetch=1,
        grid=(group,),
        in_specs=[own, own, whole(ids.shape), whole(vectors.shape)]
        + [whole(contexts[0].shape)] * len(contexts)
        + [ANYWHERE] * (3 * group),
        out_specs=[
            whole((count, depth)), whole((count, depth)), whole((count, depth)), whole((count, 1)),
            whole((count, depth)), whole((count, depth)), whole((8, depth)), per_slot, per_slot,
        ],
        scratch_shapes=[
            pltpu.VMEM((2, hidden, depth), bf16),
            pltpu.VMEM((2, hidden, depth), bf16),
            pltpu.VMEM((group, width, depth), bf16),
            pltpu.VMEM((group, BIAS_ROWS, depth), bf16),
            pltpu.VMEM((count, hidden), f32),
            pltpu.VMEM((count, depth), f32),
            pltpu.SemaphoreType.DMA((2, 2)),
            pltpu.SemaphoreType.DMA((2, group)),
        ],
    )
    shape = jax.ShapeDtypeStruct
    return pl.pallas_call(
        functools.partial(ffn_kernel, group),
        grid_spec=spec,
        out_shape=[
            shape((count, depth), bf16), shape((count, depth), bf16), shape((count, depth), f32),
            shape((count, 1), f32), shape((count, depth), f32), shape((count, depth), bf16),
            shape((8, depth), f32), shape((group, count, hidden), bf16),
            shape((group, count, hidden), bf16),
        ],
        cost_estimate=cost(2**34),
        compiler_params=limit(28),
        name="ffn",
    )(
        place, far_away(frames), far_away(cotangent), ids, vectors, *contexts, *weights, *up, *down
    )


def in_order(order):
    def slot_of(s):
        result = jnp.int32(order[-1])
        for position in reversed(range(len(order) - 1)):
            result = jnp.where(s == position, order[position], result)
        return result

    return slot_of


def everything(shape):
    return pl.BlockSpec(shape, lambda s: (0,) * len(shape))


def up_back(order, last, low, normal, inverse, gradtwo, gradffn, slope, gain, up, down):
    group = len(up)
    count, depth = low.shape
    hidden = slope.shape[2]
    slot_of = in_order(order)
    per_slot = pl.BlockSpec((1, count, hidden), lambda s: (slot_of(s), 0, 0))
    rows = hidden + HIDDEN_EXTRA
    shape = jax.ShapeDtypeStruct
    wide = shape((count, depth), f32)
    tail = [shape((8, depth), f32), wide, shape((count, depth), bf16)] if last else [wide]
    return pl.pallas_call(
        functools.partial(up_back_kernel, order, last, group),
        grid=(len(order),),
        in_specs=[
            everything(v.shape) for v in (low, normal, inverse, gradtwo, gradffn)
        ]
        + [per_slot, everything(gain.shape)]
        + [ANYWHERE] * (2 * group),
        out_specs=[pl.BlockSpec((1, rows, depth), lambda s: (s, 0, 0))]
        + [everything(t.shape) for t in tail],
        out_shape=[shape((len(order), rows, depth), bf16)] + tail,
        scratch_shapes=[
            pltpu.VMEM((2, hidden, depth), bf16),
            pltpu.VMEM((2, hidden, depth), bf16),
            pltpu.VMEM((count, hidden), bf16),
            pltpu.SemaphoreType.DMA((2, 2)),
        ]
        + ([pltpu.VMEM((count, depth), f32)] if last else []),
        cost_estimate=cost(2**33),
        compiler_params=limit(26),
        name="up_back",
    )(low, normal, inverse, gradtwo, gradffn, slope, gain, *up, *down)


def down_back(order, active, gradffn, gradattn, smalls, contexts):
    count, hidden = active.shape[1:]
    depth = gradffn.shape[1]
    width = contexts[0].shape[2]
    slot_of = in_order(order)
    rows = hidden + width + HIDDEN_EXTRA
    return pl.pallas_call(
        functools.partial(down_back_kernel, order, active.shape[0]),
        grid=(len(order),),
        in_specs=[pl.BlockSpec((1, count, hidden), lambda s: (slot_of(s), 0, 0))]
        + [everything(v.shape) for v in (gradffn, gradattn, *smalls, *contexts)],
        out_specs=pl.BlockSpec((1, rows, depth), lambda s: (s, 0, 0)),
        out_shape=jax.ShapeDtypeStruct((len(order), rows, depth), bf16),
        cost_estimate=cost(2**32),
        compiler_params=limit(20),
        name="down_back",
    )(active, gradffn, gradattn, *smalls, *contexts)


def swap(value, axis, distance):
    size = lax.axis_size(axis)
    return lax.ppermute(value, axis, [(i, i ^ distance) for i in range(size)])


def add_low(a, b):
    return (a.astype(f32) + b.astype(f32)).astype(bf16)


def add_three(a, b, c):
    return (a.astype(f32) + b.astype(f32) + c.astype(f32)).astype(bf16)


def hold(value, *others):
    return lax.optimization_barrier((value,) + tuple(others))[0]


def row_distances(size):
    distance, result = 1, []
    while distance < size:
        result.append(distance)
        distance *= 2
    return result


def split_rows(value, distance, axis=0):
    upper = (lax.axis_index("rows") // distance) % 2 == 1
    half = value.shape[axis] // 2
    low_part = lax.slice_in_dim(value, 0, half, axis=axis)
    high_part = lax.slice_in_dim(value, half, 2 * half, axis=axis)
    return jnp.where(upper, low_part, high_part), jnp.where(upper, high_part, low_part)


def join_rows(value, arrived, distance):
    upper = (lax.axis_index("rows") // distance) % 2 == 1
    return jnp.concatenate(
        [jnp.where(upper, arrived, value), jnp.where(upper, value, arrived)], axis=0
    )


def spread_pieces(piece, distances):
    pieces = [piece]
    for bits in range(1, 2 ** len(distances)):
        far = sum(d for i, d in enumerate(distances) if bits >> i & 1)
        pieces.append(swap(piece, "rows", far))
    return pieces


def join_pieces(pieces, distances):
    for distance in reversed(distances):
        half = len(pieces) // 2
        pieces = [join_rows(pieces[i], pieces[i + half], distance) for i in range(half)]
    return pieces[0]


def halved(value, axis=0):
    distances = row_distances(lax.axis_size("rows"))
    taken, rows = [], value.shape[axis]
    for distance in distances[:-1]:
        if rows % 16:
            break
        taken.append(distance)
        rows //= 2
    return taken, distances[len(taken) :]


def gather_slots(value):
    slots = {0: value}
    distance = lax.axis_size("heads") // 2
    while distance >= 1:
        for slot in list(slots):
            slots[slot ^ distance] = swap(slots[slot], "heads", distance)
        distance //= 2
    return [slots[slot] for slot in range(len(slots))]


def per_device(
    frames, segment_ids, cotangent, query_weight, query_bias, key_weight, value_weight, value_bias,
    output_weight, output_bias, first_gain, first_shift, inner_weight, inner_bias, outer_weight,
    outer_bias, second_gain, second_shift,
):
    group = lax.axis_size("heads")
    position = lax.axis_index("heads")
    row_count, row_length, depth = frames.shape
    own_len = row_count * row_length // group
    size = math.gcd(row_length, own_len)
    steps = own_len // size
    per_row = row_length // size
    width = query_weight.shape[1]
    heads_here = width // HEAD_DIM
    per_head = FF_LIVE // HEADS_LIVE
    hidden_slots = inner_weight.shape[1]
    hidden_cap = min(hidden_slots, (HEADS_LIVE + group - 1) // group * per_head)

    def live_of(index):
        return HEADS_LIVE // group + (index < HEADS_LIVE % group).astype(jnp.int32)

    distances = row_distances(lax.axis_size("rows"))
    shared = [d for d in distances[:2] if hidden_cap % (16 * len(distances[:2])) == 0]
    piece_rows = hidden_cap >> len(shared)
    piece_first = jnp.int32(0)
    for index, distance in enumerate(shared):
        upper = (lax.axis_index("rows") // distance) % 2
        piece_first = piece_first + upper * (hidden_cap >> (index + 1))
    place = jnp.stack(
        [position * steps, jnp.int32(per_row), position]
        + [live_of(position ^ slot) for slot in range(group)]
        + [piece_first]
    )
    blocks = frames.reshape(row_count * per_row, size, depth)
    weight_own = prepare(
        place, query_weight.T, key_weight.T, value_weight.T, query_bias[None], value_bias[None],
        inner_bias[None], output_weight, outer_weight, piece_rows,
    )
    weight = {0: weight_own, 1: swap(weight_own, "heads", 1), 2: swap(weight_own, "heads", 2)}
    up_own, down_own, keyf, queryf = prepare_wide(
        place, inner_weight, outer_weight, segment_ids,
        segment_ids.reshape(row_count * per_row, 1, size), hidden_cap,
    )
    up = {0: up_own, 1: swap(up_own, "heads", 1)}
    down = {0: down_own, 1: swap(down_own, "heads", 1)}
    half = group // 2

    def forward(first, *waits):
        return attend(
            first, place, hold(blocks, *waits), frames,
            [weight[slot] for slot in range(first, first + half)], keyf, queryf, steps, width,
        )

    saved = [forward(0)]
    done = saved[0][0]
    weight[2] = hold(weight[2], done)
    weight[3] = swap(weight[2], "heads", 1)
    up[2] = swap(hold(up_own, weight[2]), "heads", 2)
    piece = weight[2][4 * width + BIAS_ROWS :]
    pieces = spread_pieces(piece, shared)
    saved.append(forward(half, done))
    down[2] = join_pieces(hold(pieces, saved[1][0]), shared)
    up[3] = swap(up[2], "heads", 1)
    down[3] = swap(down[2], "heads", 1)
    up = [up[slot] for slot in range(group)]
    down = [down[slot] for slot in range(group)]
    contexts = [kept[3] for kept in saved]

    vectors = jnp.stack(
        [output_bias, first_gain, first_shift, outer_bias, second_gain, second_shift]
    )
    whole_frames = frames.reshape(group, own_len, depth)
    whole_cot = cotangent.reshape(group, own_len, depth)
    flat_ids = segment_ids.reshape(row_count * row_length)
    ids_own = lax.dynamic_slice_in_dim(flat_ids, position * own_len, own_len)[:, None]
    layer_own, normed_low, normal_one, inverse_one, grad_two, grad_ffn, small_two, actives, slopes = ffn(
        place, whole_frames, whole_cot, ids_own, vectors, contexts,
        [weight[slot] for slot in range(group)], up, down,
    )
    layer = {0: layer_own, 1: swap(layer_own, "heads", 1), 2: swap(layer_own, "heads", 2)}
    known = (normed_low, normal_one, inverse_one)
    gain = first_gain[None]
    up_send, grad_part = up_back((1, 3), False, *known, grad_two, grad_ffn, slopes, gain, up, down)
    up_came = swap(up_send, "heads", 1)
    layer[1] = hold(layer[1], grad_part)
    up_keep, small_one, grad_hidden_one, grad_attn = up_back(
        (0, 2), True, *known, grad_part, grad_ffn, slopes, gain, up, down
    )
    up_pair = add_low(up_keep, up_came)
    up_taken, up_left = halved(up_pair, 1)
    up_sent, up_mine = split_rows(up_pair, up_taken[0], 1)
    up_came = swap(up_sent, "rows", up_taken[0])

    smalls = (small_one, small_two)
    down_send = down_back((1, 3), actives, hold(grad_ffn, up_sent), grad_attn, smalls, contexts)
    down_came = swap(down_send, "heads", 1)
    down_keep = down_back((0, 2), actives, hold(grad_ffn, down_send), grad_attn, smalls, contexts)
    down_came = hold(down_came, down_keep)
    grad_attn = grad_attn.reshape(steps, size, depth)
    block_sum = grad_hidden_one.reshape(steps, size, depth)
    row_sum = jnp.zeros((8, 128), f32)
    grads = {}

    def back(slot, first, block_sum, row_sum, *waits):
        return attend_back(
            slot, first, place, blocks, frames, weight[slot], saved[slot // half], grad_attn,
            hold(block_sum, *waits), row_sum,
        )

    down_zero = add_low(down_keep[0], down_came[0])
    down_two = add_low(down_keep[1], down_came[1])
    layer[2] = hold(layer[2], down_keep)
    layer[3] = swap(layer[2], "heads", 1)
    cut = down_two.shape[0] // 2
    down_first = swap(hold(down_two[:cut], layer[2]), "heads", 2)
    grads[3], block_sum, row_sum = back(3, True, block_sum, row_sum, layer[2], down_two)

    block_sum, up_came, down_first, layer[3], grads[3] = lax.optimization_barrier(
        (block_sum, up_came, down_first, layer[3], grads[3])
    )
    grads_came = swap(grads[3], "heads", 1)
    down_second = swap(hold(down_two[cut:], down_first), "heads", 2)
    up_pair = add_low(up_mine, up_came)
    up_sent, up_mine = split_rows(up_pair, up_taken[1], 1)
    up_came = swap(up_sent, "rows", up_taken[1])
    grads[2], block_sum, row_sum = back(2, False, block_sum, row_sum, up_sent)

    block_sum, up_came, down_second, grads_came, grads[2] = lax.optimization_barrier(
        (block_sum, up_came, down_second, grads_came, grads[2])
    )
    attn_two = add_low(grads[2], grads_came)
    attn_rows = attn_two.shape[0] // 2
    attn_first = swap(attn_two[:attn_rows], "heads", 2)
    up_pair = add_low(up_mine, up_came)
    up_came = swap(up_pair[1], "heads", 2)
    down_half = add_low(down_zero, jnp.concatenate([down_first, down_second]))
    down_taken, down_left = halved(down_half)
    down_sent, down_mine = split_rows(down_half, down_taken[0])
    down_came = swap(down_sent, "rows", down_taken[0])
    grads[1], block_sum, row_sum = back(1, False, block_sum, row_sum, attn_two, up_pair, down_sent)

    block_sum, up_came, down_came, attn_first, grads[1] = lax.optimization_barrier(
        (block_sum, up_came, down_came, attn_first, grads[1])
    )
    grads_came = swap(grads[1], "heads", 1)
    up_piece = add_low(up_pair[0], up_came)
    up_came = swap(up_piece, "rows", up_left[0])
    attn_second = swap(hold(attn_two[attn_rows:], attn_first), "heads", 2)
    down_half = add_low(down_mine, down_came)
    down_sent, down_mine = split_rows(down_half, down_taken[1])
    down_came = swap(down_sent, "rows", down_taken[1])
    grads[0], block_sum, row_sum = back(0, False, block_sum, row_sum, up_piece, down_sent)
    block_sum, up_came, down_came, attn_second, grads_came, grads[0] = lax.optimization_barrier(
        (block_sum, up_came, down_came, attn_second, grads_came, grads[0])
    )
    attn_far = [attn_first, attn_second]

    reach, pairs = [0], {}
    for distance in range(1, group):
        pairs[distance] = []
        for i in range(group):
            j = i ^ distance
            rows_i = range(i * steps // per_row, ((i + 1) * steps - 1) // per_row + 1)
            rows_j = range(j * steps // per_row, ((j + 1) * steps - 1) // per_row + 1)
            if set(rows_i) & set(rows_j):
                pairs[distance].append((i, j))
        if pairs[distance]:
            reach.append(distance)
    up_piece = add_low(up_piece, hold(up_came, block_sum))
    up_came = swap(up_piece, "rows", up_taken[1])
    attn_two = jnp.concatenate(attn_far)
    attn_half = add_three(grads[0], grads_came, attn_two)
    attn_taken, attn_left = halved(attn_half)
    attn_sent, attn_mine = split_rows(attn_half, attn_taken[0])
    attn_came = swap(attn_sent, "rows", attn_taken[0])
    own_grad, *owed = shares(place, row_sum, block_sum, tuple(reach))
    owed = [
        lax.ppermute(sent, "heads", pairs[distance]) for distance, sent in zip(reach[1:], owed)
    ]
    down_half = add_low(down_mine, hold(down_came, block_sum, attn_sent))
    down_came = swap(down_half, "rows", down_left[0])
    for came in owed:
        own_grad = own_grad + hold(came, attn_mine).astype(f32)
    own_grad = own_grad.astype(bf16).reshape(own_len, depth)

    cuts = [0, own_len * 4 // 15, own_len * 12 // 15, own_len]
    parts = [own_grad[cuts[i] : cuts[i + 1]] for i in range(3)]
    slots = {0: own_grad}
    attn_half = add_low(attn_mine, attn_came)
    attn_sent, attn_mine = split_rows(hold(attn_half, own_grad), attn_taken[1])
    parts[0] = swap(parts[0], "heads", 2)
    slots[1] = swap(own_grad, "heads", 1)
    attn_came = swap(attn_sent, "rows", attn_taken[1])
    up_piece = join_rows(up_piece, hold(up_came, attn_sent), up_taken[1])
    up_came = swap(up_piece, "rows", up_taken[0])

    attn_half = hold(add_low(attn_mine, attn_came), parts[0], slots[1])
    parts[1] = swap(hold(parts[1], attn_half), "heads", 2)
    attn_came = swap(attn_half, "rows", attn_left[0])
    down_half = add_low(down_half, hold(down_came, attn_half))
    down_came = swap(down_half, "rows", down_taken[1])

    attn_half = hold(add_low(attn_half, attn_came), parts[1])
    parts[2] = swap(hold(parts[2], attn_half), "heads", 2)
    attn_came = swap(attn_half, "rows", attn_taken[1])
    up_sum = join_rows(up_piece, hold(up_came, attn_half), up_taken[0]).astype(f32)
    down_half = join_rows(down_half, hold(down_came, attn_half), down_taken[1])
    down_came = swap(down_half, "rows", down_taken[0])

    attn_half = hold(join_rows(attn_half, attn_came, attn_taken[1]), parts[2])
    attn_came = swap(attn_half, "rows", attn_taken[0])
    slots[2] = jnp.concatenate(parts)
    slots[3] = swap(slots[2], "heads", 1)
    down_sum = join_rows(down_half, hold(down_came, attn_half), down_taken[0]).astype(f32)
    attn_sum = join_rows(attn_half, attn_came, attn_taken[0]).astype(f32)
    frames_grad = assemble(place, [slots[slot] for slot in range(group)]).reshape(frames.shape)
    layer[0] = hold(layer[0], attn_sent)
    layer_out = assemble(place, [layer[slot] for slot in range(group)]).reshape(frames.shape)

    hidden_mask = (jnp.arange(hidden_cap, dtype=jnp.int32) < live_of(position) * per_head)[:, None]
    padding = hidden_slots - hidden_cap
    inner_full = jnp.pad(up_sum[:hidden_cap], ((0, padding), (0, 0))).T
    outer_full = jnp.pad(
        jnp.where(hidden_mask, down_sum[:hidden_cap], 0), ((0, padding), (0, 0))
    )
    innerbias = jnp.concatenate([up_sum[hidden_cap], up_sum[hidden_cap + 1, : hidden_cap - depth]])
    innerbias_full = jnp.pad(innerbias, ((0, padding),))
    extra = attn_sum[3 * width :]
    small = down_sum[hidden_cap + width :]
    return (
        layer_out,
        frames_grad,
        attn_sum[:width].T,
        extra[0, :width],
        attn_sum[width : 2 * width].T,
        attn_sum[2 * width : 3 * width].T,
        extra[1, :width],
        down_sum[hidden_cap : hidden_cap + width],
        small[2],
        small[0],
        small[1],
        inner_full,
        innerbias_full,
        outer_full,
        small[5],
        small[3],
        small[4],
    )


def solution(mesh):
    in_specs = (
        P("rows", None, None), P("rows", None), P("rows", None, None), P(None, "heads"), P("heads"),
        P(None, "heads"), P(None, "heads"), P("heads"), P("heads", None), P(), P(), P(),
        P(None, "heads"), P("heads"), P("heads", None), P(), P(), P(),
    )
    out_specs = (
        P("rows", None, None), P("rows", None, None), P(None, "heads"), P("heads"), P(None, "heads"),
        P(None, "heads"), P("heads"), P("heads", None), P(), P(), P(), P(None, "heads"), P("heads"),
        P("heads", None), P(), P(), P(),
    )
    return jax.shard_map(
        per_device, mesh=mesh, in_specs=in_specs, out_specs=out_specs, check_vma=False
    )
```

```python
import functools
import math

import jax
import jax.numpy as jnp
from jax import lax
from jax.experimental import pallas as pl
from jax.experimental.pallas import tpu as pltpu
from jax.sharding import PartitionSpec as P

HEADS_LIVE = 10
HEAD_SLOTS = 12
HEAD_DIM = 64
FF_LIVE = 2240
PAD_HEAD = 128
SEGMENTS = 5
MASK_STEP = -(2.0**30)
norm_eps = 1e-05
f32 = jnp.float32
bf16 = jnp.bfloat16


def dot(a, b, ca, cb):
    return lax.dot_general(a, b, (((ca,), (cb,)), ((), ())), preferred_element_type=f32)


def three_parts(value):
    high = value.astype(bf16).astype(f32)
    middle = (value - high).astype(bf16).astype(f32)
    return high, middle, value - high - middle


def live_heads(live, heads, one_head):
    least = HEADS_LIVE * heads // HEAD_SLOTS
    for head in range(least):
        one_head(head)
    for head in range(least, heads):

        @pl.when(head < live)
        def _():
            one_head(head)


def feature_rows(base, value):
    high, middle, low = three_parts(-value)
    row = lax.broadcasted_iota(jnp.int32, base.shape, 0)
    base = jnp.where(row == SEGMENTS, high, base)
    base = jnp.where(row == SEGMENTS + 1, middle, base)
    return jnp.where(row == SEGMENTS + 2, low, base).astype(bf16)


def bias_row(rows, index):
    first = 3 * index
    return rows[first : first + 1] + rows[first + 1 : first + 2] + rows[first + 2 : first + 3]


def attend_kernel(
    first, place, block_ref, row_ref, keyf_ref, queryf_ref, *refs,
):
    pair = len(refs) - 5
    weight_refs, (query_ref, key_ref, value_ref, context_ref, weight_ref) = refs[:pair], refs[pair:]
    turn = pl.program_id(0)
    step = pl.program_id(1)
    per_row, live = place[1], place[3 + first + turn]
    row_now = (place[0] + step) // per_row
    row_before = (place[0] + step - 1) // per_row
    length = row_ref.shape[1]
    width = context_ref.shape[2]
    heads = width // HEAD_DIM

    for index, ref in enumerate(weight_refs):

        @pl.when(jnp.logical_and(step == 0, turn == index))
        def _():
            weight_ref[...] = ref[...]

    biases = weight_ref[3 * width :].astype(f32)

    @pl.when(jnp.logical_or(step == 0, row_now != row_before))
    def _():
        frames = row_ref[0]
        keys = dot(frames, weight_ref[width : 2 * width], 1, 1).astype(bf16)
        values = dot(frames, weight_ref[2 * width : 3 * width], 1, 1)
        values = (values + bias_row(biases, 1)[:, 0:width]).astype(bf16)
        features = keyf_ref[0]
        for head in range(heads):
            cut = slice(head * HEAD_DIM, (head + 1) * HEAD_DIM)
            key_ref[0, 0, head * length : (head + 1) * length] = jnp.concatenate(
                [keys[:, cut], features], axis=1
            )
            value_ref[0, 0, head * length : (head + 1) * length] = jnp.concatenate(
                [values[:, cut], features], axis=1
            )

    qbias = jnp.broadcast_to(bias_row(biases, 0)[:, 0:width], (8, width)).T[:, 0:1]
    queries = (dot(weight_ref[0:width], block_ref[0], 1, 1) + qbias).astype(bf16)
    queries = queries * jnp.asarray(HEAD_DIM**-0.5, bf16)
    for head in range(heads):
        query_ref[0, 0, head * PAD_HEAD : head * PAD_HEAD + HEAD_DIM] = queries[
            head * HEAD_DIM : (head + 1) * HEAD_DIM
        ]
        query_ref[0, 0, head * PAD_HEAD + HEAD_DIM : (head + 1) * PAD_HEAD] = queryf_ref[0]
    context_ref[...] = jnp.zeros_like(context_ref)

    def one_head(head):
        keys = key_ref[0, 0, pl.ds(head * length, length)]
        values = value_ref[0, 0, pl.ds(head * length, length)]
        start = head * PAD_HEAD
        scores = dot(keys, query_ref[0, 0, pl.ds(start, PAD_HEAD)], 1, 0)
        highest = jnp.max(scores, axis=0, keepdims=True)
        probs = jnp.exp(scores - highest).astype(bf16)
        mixed = dot(values, probs, 0, 0)
        total = mixed[HEAD_DIM + SEGMENTS : HEAD_DIM + SEGMENTS + 1]
        context = mixed[0:HEAD_DIM] / total
        context_ref[0, 0, pl.ds(head * HEAD_DIM, HEAD_DIM)] = context.astype(bf16)
        base = queryf_ref[0, 0:16].astype(f32)
        query_ref[0, 0, pl.ds(start + HEAD_DIM, 16)] = feature_rows(base, highest + jnp.log(total))

    live_heads(live, heads, one_head)


def attend_back_kernel(
    slot, first, place, block_ref, row_ref, weight_ref, query_ref, key_ref, value_ref,
    context_ref, grad_ref, blocksum_ref, rowsum_ref,
    gradw_ref, blockout_ref, rowout_ref,
    weight_acc, dkey, dvalue, picked, dcontext, dquery, bias_acc,
):
    step = pl.program_id(0)
    steps = pl.num_programs(0)
    per_row, live = place[1], place[3 + slot]
    row_now = (place[0] + step) // per_row
    row_before = (place[0] + step - 1) // per_row
    row_after = (place[0] + step + 1) // per_row
    length, depth = row_ref.shape[1:]
    width = context_ref.shape[2]
    heads = width // HEAD_DIM
    ones = jnp.ones((8, length), bf16)

    @pl.when(step == 0)
    def _():
        weight_acc[...] = jnp.zeros_like(weight_acc)
        bias_acc[...] = jnp.zeros_like(bias_acc)
        picked[...] = jnp.zeros_like(picked)

    @pl.when(jnp.logical_or(step == 0, row_now != row_before))
    def _():
        dkey[...] = jnp.zeros_like(dkey)
        dvalue[...] = jnp.zeros_like(dvalue)

    dcontext[...] = dot(weight_ref[3 * width + BIAS_ROWS :], grad_ref[0], 1, 1).astype(bf16)
    dquery[...] = jnp.zeros_like(dquery)

    def one_head(head):
        own = pl.ds(head * HEAD_DIM, HEAD_DIM)
        keys = key_ref[0, 0, pl.ds(head * length, length)]
        values = value_ref[0, 0, pl.ds(head * length, length)]
        queries = query_ref[0, 0, pl.ds(head * PAD_HEAD, PAD_HEAD)]
        grad = dcontext[own]
        inner = jnp.sum(grad.astype(f32) * context_ref[0, 0, own].astype(f32), axis=0, keepdims=True)
        extra = feature_rows(jnp.zeros((PAD_HEAD - HEAD_DIM, grad.shape[1]), f32), inner)
        probs = jnp.exp(dot(keys, queries, 1, 0))
        dprobs = dot(values, jnp.concatenate([grad, extra], axis=0), 1, 0)
        dscores = (probs * dprobs).astype(bf16)
        picked[0, pl.ds(head * width + head * HEAD_DIM, HEAD_DIM)] = grad
        picked[1, pl.ds(head * width + head * HEAD_DIM, HEAD_DIM)] = queries[0:HEAD_DIM]
        place_head = pl.ds(head * width, width)
        dvalue[...] += dot(probs.astype(bf16), picked[0, place_head], 1, 1)
        dkey[...] += dot(dscores, picked[1, place_head], 1, 1)
        dquery[own] = (dot(keys, dscores, 0, 0)[0:HEAD_DIM] * HEAD_DIM**-0.5).astype(bf16)

    live_heads(live, heads, one_head)
    weight_acc[0:width] += dot(dquery[...], block_ref[0], 1, 0)
    blockout_ref[0] = blocksum_ref[0] + dot(dquery[...], weight_ref[0:width], 0, 0)
    bias_acc[0:8] += dot(ones[:, 0 : dquery.shape[1]], dquery[...], 1, 1)

    @pl.when(jnp.logical_or(step == steps - 1, row_now != row_after))
    def _():
        keys_low = dkey[...].astype(bf16)
        values_low = dvalue[...].astype(bf16)
        weight_acc[width : 2 * width] += dot(keys_low, row_ref[0], 0, 0)
        weight_acc[2 * width : 3 * width] += dot(values_low, row_ref[0], 0, 0)
        back = dot(keys_low, weight_ref[width : 2 * width], 1, 0) + dot(
            values_low, weight_ref[2 * width : 3 * width], 1, 0
        )
        if first:
            rowout_ref[0] = back
        else:
            rowout_ref[0] = rowsum_ref[0] + back
        bias_acc[8:16] += dot(ones, values_low, 1, 0)

    @pl.when(step == steps - 1)
    def _():
        gradw_ref[0 : 3 * width] = weight_acc[...].astype(bf16)
        row = lax.broadcasted_iota(jnp.int32, (gradw_ref.shape[0] - 3 * width, depth), 0)
        lanes = depth - width
        extra = jnp.where(row == 0, jnp.pad(bias_acc[0:1], ((0, 0), (0, lanes))), 0.0)
        extra = jnp.where(row == 1, jnp.pad(bias_acc[8:9], ((0, 0), (0, lanes))), extra)
        gradw_ref[3 * width :] = extra.astype(bf16)


def whole(shape):
    return pl.BlockSpec(shape, lambda b, place: (0,) * len(shape))


def limit(mib):
    return pltpu.CompilerParams(vmem_limit_bytes=mib * 2**20)


def cost(flops):
    return pl.CostEstimate(flops=2**40, bytes_accessed=2**33, transcendentals=0)


ANYWHERE = pl.BlockSpec(memory_space=pltpu.HBM)


def far_away(value):
    return pltpu.with_memory_space_constraint(value, pltpu.HBM)
BIAS_ROWS = 16
EXTRA_ROWS = 64
HIDDEN_EXTRA = 32


def row_of(b, place):
    return (place[0] + b) // place[1], 0, 0


def rel_row(b, place):
    return (place[0] + b) // place[1] - place[0] // place[1], 0, 0


def block_of(b, place):
    return place[0] + b, 0, 0


def local(b, place):
    return b, 0, 0


def attend(first, place, blocks, rows, weights, keyf, queryf, steps, width):
    size, depth = blocks.shape[1:]
    count, length, _ = rows.shape
    weight_shape = (3 * width + BIAS_ROWS, depth)
    heads = width // HEAD_DIM
    window = min(2, count)
    pair = len(weights)
    fixed = lambda shape: pl.BlockSpec(shape, lambda s, b, place: (0,) * len(shape))
    per_row = lambda shape: pl.BlockSpec((1,) + shape, lambda s, b, place: row_of(b, place))
    per_block = lambda shape: pl.BlockSpec((1,) + shape, lambda s, b, place: block_of(b, place))
    out_row = pl.BlockSpec(
        (1, 1, heads * length, PAD_HEAD), lambda s, b, place: (s,) + rel_row(b, place)
    )
    out_block = lambda rows: pl.BlockSpec((1, 1, rows, size), lambda s, b, place: (s, b, 0, 0))
    spec = pltpu.PrefetchScalarGridSpec(
        num_scalar_prefetch=1,
        grid=(pair, steps),
        in_specs=[
            per_block((size, depth)), per_row((length, depth)), per_row(keyf.shape[1:]),
            per_block(queryf.shape[1:]),
        ]
        + [fixed(weight_shape)] * pair,
        out_specs=[out_block(heads * PAD_HEAD), out_row, out_row, out_block(width)],
        scratch_shapes=[pltpu.VMEM(weight_shape, bf16)],
    )
    return pl.pallas_call(
        functools.partial(attend_kernel, first),
        grid_spec=spec,
        out_shape=[
            jax.ShapeDtypeStruct((pair, steps, heads * PAD_HEAD, size), bf16),
            jax.ShapeDtypeStruct((pair, window, heads * length, PAD_HEAD), bf16),
            jax.ShapeDtypeStruct((pair, window, heads * length, PAD_HEAD), bf16),
            jax.ShapeDtypeStruct((pair, steps, width, size), bf16),
        ],
        cost_estimate=cost(2**33),
        compiler_params=limit(FORWARD_LIMIT),
        name="attend",
    )(place, blocks, rows, keyf, queryf, *weights)


FORWARD_LIMIT = 60


def attend_back(slot, first, place, blocks, rows, weight, saved, grad, blocksum, rowsum):
    query, key, value, context = saved
    steps, size, depth = blocksum.shape
    count, length, _ = rows.shape
    width = context.shape[2]
    heads = width // HEAD_DIM
    turn = slot % query.shape[0]
    saved_block = lambda v: pl.BlockSpec(
        (1, 1) + v.shape[2:], lambda b, place: (turn,) + local(b, place)
    )
    saved_row = lambda v: pl.BlockSpec(
        (1, 1) + v.shape[2:], lambda b, place: (turn,) + rel_row(b, place)
    )
    row_spec = pl.BlockSpec((1, length, depth), rel_row)
    near = far_away if first else lambda value: value
    spec = pltpu.PrefetchScalarGridSpec(
        num_scalar_prefetch=1,
        grid=(steps,),
        in_specs=[
            pl.BlockSpec((1, size, depth), block_of),
            pl.BlockSpec((1, length, depth), row_of),
            whole((4 * width + BIAS_ROWS, depth)),
            saved_block(query), saved_row(key), saved_row(value), saved_block(context),
            pl.BlockSpec((1, size, depth), local),
            pl.BlockSpec((1, size, depth), local),
            ANYWHERE if first else row_spec,
        ],
        out_specs=[
            whole((3 * width + EXTRA_ROWS, depth)),
            pl.BlockSpec((1, size, depth), local),
            row_spec,
        ],
        scratch_shapes=[
            pltpu.VMEM((3 * width, depth), f32),
            pltpu.VMEM((length, width), f32),
            pltpu.VMEM((length, width), f32),
            pltpu.VMEM((2, heads * width, size), bf16),
            pltpu.VMEM((width, size), bf16),
            pltpu.VMEM((width, size), bf16),
            pltpu.VMEM((16, width), f32),
        ],
    )
    return pl.pallas_call(
        functools.partial(attend_back_kernel, slot, first),
        grid_spec=spec,
        out_shape=[
            jax.ShapeDtypeStruct((3 * width + EXTRA_ROWS, depth), bf16),
            jax.ShapeDtypeStruct(blocksum.shape, f32),
            jax.ShapeDtypeStruct((min(2, count), length, depth), f32),
        ],
        input_output_aliases={} if first else {10: 2},
        cost_estimate=cost(2**34),
        compiler_params=limit(26),
        name="attend_back",
    )(
        place, near(blocks), near(rows), near(weight), query, near(key), near(value), context, grad,
        blocksum, rowsum,
    )


def prepare_kernel(
    per_head, place, query_ref, key_ref, value_ref, qbias_ref, vbias_ref, ubias_ref, out_ref, down_ref,
    weight_ref,
):
    width, depth = query_ref.shape
    weight_ref[0:width] = query_ref[...]
    weight_ref[width : 2 * width] = key_ref[...]
    weight_ref[2 * width : 3 * width] = value_ref[...]
    lanes = ubias_ref.shape[1]
    row = lax.broadcasted_iota(jnp.int32, (BIAS_ROWS, depth), 0)
    result = jnp.zeros((BIAS_ROWS, depth), f32)
    vectors = [
        jnp.pad(qbias_ref[...], ((0, 0), (0, depth - width))),
        jnp.pad(vbias_ref[...], ((0, 0), (0, depth - width))),
        ubias_ref[:, 0:depth],
        jnp.pad(ubias_ref[:, depth:lanes], ((0, 0), (0, 2 * depth - lanes))),
    ]
    for index, vector in enumerate(vectors):
        for offset, part in enumerate(three_parts(vector)):
            result = jnp.where(row == 3 * index + offset, part, result)
    first = 3 * width + BIAS_ROWS
    weight_ref[3 * width : first] = result.astype(bf16)
    row = lax.broadcasted_iota(jnp.int32, out_ref.shape, 0)
    kept = jnp.where(row < place[3] * HEAD_DIM, out_ref[...].astype(f32), 0.0)
    weight_ref[first : first + width] = kept.astype(bf16)
    piece = weight_ref.shape[0] - first - width
    start = place[3 + SLOT_COUNT]
    row = start + lax.broadcasted_iota(jnp.int32, (piece, depth), 0)
    kept = down_ref[pl.ds(pl.multiple_of(start, 8), piece)].astype(f32)
    weight_ref[first + width :] = jnp.where(row < place[3] * per_head, kept, 0.0).astype(bf16)


SLOT_COUNT = 4


def prepare(place, query, key, value, qbias, vbias, ubias, out, down, piece):
    width, depth = query.shape
    shape = (4 * width + BIAS_ROWS + piece, depth)
    args = (query, key, value, qbias, vbias, ubias, out, down)
    return pl.pallas_call(
        functools.partial(prepare_kernel, FF_LIVE // HEADS_LIVE),
        grid_spec=pltpu.PrefetchScalarGridSpec(
            num_scalar_prefetch=1,
            grid=(1,),
            in_specs=[whole(v.shape) for v in args],
            out_specs=whole(shape),
        ),
        out_shape=jax.ShapeDtypeStruct(shape, bf16),
        compiler_params=limit(60),
        name="prepare",
    )(place, *args)


def prepare_wide_kernel(
    per_head, place, up_ref, down_ref, ids_ref, blocks_ref,
    upout_ref, downout_ref, keyf_ref, queryf_ref,
):
    hidden = downout_ref.shape[0]
    upout_ref[...] = up_ref[...].T[0:hidden]
    row = lax.broadcasted_iota(jnp.int32, downout_ref.shape, 0)
    kept = jnp.where(row < place[3] * per_head, down_ref[0:hidden].astype(f32), 0.0)
    downout_ref[...] = kept.astype(bf16)
    rows, length = ids_ref.shape
    feature = lax.broadcasted_iota(jnp.int32, (HEAD_DIM, length), 0)
    for r in range(rows):
        same = jnp.where(feature == ids_ref[r : r + 1] + 1, 1.0, 0.0)
        ones = jnp.where(jnp.logical_and(feature >= SEGMENTS, feature < SEGMENTS + 3), 1.0, same)
        keyf_ref[r] = ones.T.astype(bf16)
    size = blocks_ref.shape[2]
    feature = lax.broadcasted_iota(jnp.int32, (HEAD_DIM, size), 0)
    for b in range(blocks_ref.shape[0]):
        other = jnp.logical_and(feature < SEGMENTS, feature != blocks_ref[b] + 1)
        queryf_ref[b] = jnp.where(other, MASK_STEP, 0.0).astype(bf16)


def prepare_wide(place, up, down, ids, id_blocks, hidden):
    depth = up.shape[0]
    rows, length = ids.shape
    shapes = [
        (hidden, depth), (hidden, depth), (rows, length, HEAD_DIM),
        (id_blocks.shape[0], HEAD_DIM, id_blocks.shape[2]),
    ]
    return pl.pallas_call(
        functools.partial(prepare_wide_kernel, FF_LIVE // HEADS_LIVE),
        grid_spec=pltpu.PrefetchScalarGridSpec(
            num_scalar_prefetch=1,
            grid=(1,),
            in_specs=[whole(v.shape) for v in (up, down, ids, id_blocks)],
            out_specs=[whole(shape) for shape in shapes],
        ),
        out_shape=[jax.ShapeDtypeStruct(shape, bf16) for shape in shapes],
        compiler_params=limit(60),
        name="prepare_wide",
    )(place, up, down, ids, id_blocks)


def assemble_kernel(parts, share, place, *refs):
    sources, (out_ref, *rest) = refs[: len(parts)], refs[len(parts) :]
    buffers, sems = rest[:-1], rest[-1]
    inward, outward = [], []
    for index, (slot, first) in enumerate(parts):
        rows = buffers[index].shape[0]
        start = pl.multiple_of((place[2] ^ slot) * share + first, 8)
        inward.append(pltpu.make_async_copy(sources[index], buffers[index], sems.at[0, index]))
        outward.append(
            pltpu.make_async_copy(buffers[index], out_ref.at[pl.ds(start, rows)], sems.at[1, index])
        )
    for copy in inward:
        copy.start()
    for into, out in zip(inward, outward):
        into.wait()
        out.start()
    for copy in outward:
        copy.wait()


def assemble(place, pieces, share, total):
    depth = pieces[0][2].shape[1]
    arrays = [piece[2] for piece in pieces]
    parts = tuple(piece[:2] for piece in pieces)
    return pl.pallas_call(
        functools.partial(assemble_kernel, parts, share),
        grid_spec=pltpu.PrefetchScalarGridSpec(
            num_scalar_prefetch=1,
            grid=(1,),
            in_specs=[ANYWHERE] * len(arrays),
            out_specs=ANYWHERE,
            scratch_shapes=[pltpu.VMEM(v.shape, v.dtype) for v in arrays]
            + [pltpu.SemaphoreType.DMA((2, len(arrays)))],
        ),
        out_shape=jax.ShapeDtypeStruct((total, depth), arrays[0].dtype),
        cost_estimate=cost(0),
        compiler_params=limit(12),
        name="assemble",
    )(place, *arrays)


QUARTERS = 4


def collect(place, refs, buffer):
    share = refs[0].shape[0]
    number = place[4 + SLOT_COUNT] * len(refs) // QUARTERS
    for far, ref in enumerate(refs):
        start = (number ^ far) * share
        buffer[pl.ds(pl.multiple_of(start, 8), share)] = ref[...].astype(f32)


def finish_up_kernel(place, *refs):
    pieces, (grad_ref, bias_ref, buffer) = refs[:-3], refs[-3:]
    collect(place, pieces, buffer)
    depth, slots = grad_ref.shape
    hidden = buffer.shape[0] - HIDDEN_EXTRA
    grad_ref[:, 0:hidden] = buffer[0:hidden].T
    if slots > hidden:
        grad_ref[:, hidden:] = jnp.zeros((depth, slots - hidden), f32)
    bias_ref[...] = buffer[hidden : hidden + 8]


def finish_down_kernel(per_head, place, *refs):
    pieces, (grad_ref, out_ref, extra_ref, buffer) = refs[:-4], refs[-4:]
    collect(place, pieces, buffer)
    width = out_ref.shape[0]
    hidden = buffer.shape[0] - HIDDEN_EXTRA - width
    row = lax.broadcasted_iota(jnp.int32, (hidden, buffer.shape[1]), 0)
    grad_ref[0:hidden] = jnp.where(row < place[3] * per_head, buffer[0:hidden], 0.0)
    if grad_ref.shape[0] > hidden:
        grad_ref[hidden:] = jnp.zeros((grad_ref.shape[0] - hidden, buffer.shape[1]), f32)
    out_ref[...] = buffer[hidden : hidden + width]
    extra_ref[...] = buffer[hidden + width : hidden + width + 8]


def finish_attn_kernel(place, *refs):
    pieces, (query_ref, key_ref, value_ref, extra_ref, buffer) = refs[:QUARTERS], refs[QUARTERS:]
    collect(place, pieces, buffer)
    width = query_ref.shape[0]
    for index, ref in enumerate((query_ref, key_ref, value_ref)):
        ref[...] = buffer[index * width : (index + 1) * width]
    extra_ref[...] = buffer[3 * width : 3 * width + 8]


def finish(kernel, place, pieces, shapes, name):
    rows, depth = pieces[0].shape[0] * len(pieces), pieces[0].shape[1]
    return pl.pallas_call(
        kernel,
        grid_spec=pltpu.PrefetchScalarGridSpec(
            num_scalar_prefetch=1,
            grid=(1,),
            in_specs=[whole(v.shape) for v in pieces],
            out_specs=[whole(shape) for shape in shapes],
            scratch_shapes=[pltpu.VMEM((rows, depth), f32)],
        ),
        out_shape=[jax.ShapeDtypeStruct(shape, f32) for shape in shapes],
        cost_estimate=cost(0),
        compiler_params=limit(20),
        name=name,
    )(place, *pieces)


def shares_kernel(distances, group, place, *refs):
    step = pl.program_id(0)
    steps = pl.num_programs(0)
    count = len(distances)
    sources, blocksum_ref, (own_ref, *sent_refs) = refs[:count], refs[count], refs[count + 1 :]
    rows_touched = (place[0] + steps - 1) // place[1] - place[0] // place[1] + 1
    for distance, source, target in zip(distances, sources, (own_ref, *sent_refs)):
        block = (place[2] ^ distance) * steps + step - place[0] // place[1] * place[1]
        inside = jnp.logical_and(block >= 0, block < rows_touched * place[1])
        value = jnp.where(inside, source[0], 0.0)
        if distance == 0:
            target[0] = blocksum_ref[0] + value
        else:
            target[0] = value.astype(bf16)


def shares(place, rowsum, blocksum, distances):
    steps, size, depth = blocksum.shape
    group = None
    window = rowsum.reshape(-1, size, depth)

    def source(distance):
        def index(b, place):
            block = (place[2] ^ distance) * steps + b - place[0] // place[1] * place[1]
            return jnp.clip(block, 0, window.shape[0] - 1), 0, 0

        return pl.BlockSpec((1, size, depth), index)

    block = pl.BlockSpec((1, size, depth), local)
    return pl.pallas_call(
        functools.partial(shares_kernel, distances, group),
        grid_spec=pltpu.PrefetchScalarGridSpec(
            num_scalar_prefetch=1,
            grid=(steps,),
            in_specs=[source(d) for d in distances] + [block],
            out_specs=[block for _ in distances],
        ),
        out_shape=[
            jax.ShapeDtypeStruct(blocksum.shape, bf16 if d else f32) for d in distances
        ],
        compiler_params=limit(12),
        name="shares",
    )(place, *[window for _ in distances], blocksum)


def row_chunks(count, body):
    chunk = 200 if count % 200 == 0 else 16

    @pl.loop(0, count // chunk)
    def _(i):
        body(pl.ds(pl.multiple_of(i * chunk, 8), chunk))

    if count % chunk:
        body(pl.ds(count // chunk * chunk, count % chunk))


def phi_parts(value):
    bell = jnp.exp2(value * value * (-0.5 / math.log(2.0)))
    t = 1.0 / (1.0 + jnp.abs(value) * (0.3275911 * 0.5**0.5))
    poly = t * (
        0.127414796
        + t * (-0.142248368 + t * (0.7107068705 + t * (-0.7265760135 + t * 0.5307027145)))
    )
    half = poly * bell
    return jnp.where(value >= 0, 1.0 - half, half), bell * (2.0 * math.pi) ** -0.5


def chunk_stats(value):
    centre = value - jnp.mean(value, axis=-1, keepdims=True)
    inverse = lax.rsqrt(jnp.mean(centre * centre, axis=-1, keepdims=True) + norm_eps)
    return centre * inverse, inverse


def fetch_slot(order, step, sources, buffers, sems):
    for which, (refs, buffer) in enumerate(zip(sources, buffers)):
        for position, slot in enumerate(order):

            @pl.when(step == position)
            def _():
                pltpu.make_async_copy(refs[slot], buffer.at[step % 2], sems.at[which, step % 2]).start()


def await_slot(step, sources, buffers, sems):
    for which, (refs, buffer) in enumerate(zip(sources, buffers)):
        pltpu.make_async_copy(refs[0], buffer.at[step % 2], sems.at[which, step % 2]).wait()


def stream_slots(order, sources, buffers, sems):
    step = pl.program_id(0)

    @pl.when(step == 0)
    def _():
        fetch_slot(order, step, sources, buffers, sems)

    @pl.when(step + 1 < pl.num_programs(0))
    def _():
        fetch_slot(order, step + 1, sources, buffers, sems)

    await_slot(step, sources, buffers, sems)


def fetch_slot(order, step, sources, buffers, sems, firsts):
    for which, (refs, buffer, first) in enumerate(zip(sources, buffers, firsts)):
        for position, slot in enumerate(order):

            @pl.when(step == position)
            def _():
                pltpu.make_async_copy(
                    refs[slot].at[pl.ds(first, buffer.shape[1])],
                    buffer.at[step % 2],
                    sems.at[which, step % 2],
                ).start()


def stream_slots(order, sources, buffers, sems, firsts):
    step = pl.program_id(0)

    @pl.when(step == 0)
    def _():
        fetch_slot(order, step, sources, buffers, sems, firsts)

    @pl.when(step + 1 < pl.num_programs(0))
    def _():
        fetch_slot(order, step + 1, sources, buffers, sems, firsts)

    for which, (refs, buffer, first) in enumerate(zip(sources, buffers, firsts)):
        pltpu.make_async_copy(
            refs[0].at[pl.ds(first, buffer.shape[1])], buffer.at[step % 2], sems.at[which, step % 2]
        ).wait()


def ffn_kernel(
    group, place, frames_ref, cot_ref, ids_ref, vec_ref, *refs,
):
    held = len(refs) - 15 - 3 * group
    context_refs, refs = refs[:held], refs[held:]
    weight_refs, refs = refs[:group], refs[group:]
    up_refs, down_refs = refs[:group], refs[group : 2 * group]
    (
        layer_ref, low_ref, normal_ref, inverse_ref, gradffn_ref, small_ref,
        active_ref, slope_ref, up_buf, down_buf, out_buf, bias_buf, mixed, sems, out_sems,
    ) = refs[2 * group :]
    turns = group // held
    step = pl.program_id(0)
    count, depth = mixed.shape
    hidden = active_ref.shape[2]
    width = out_buf.shape[1]
    out_bias, gain_one, shift_one = vec_ref[0:1], vec_ref[1:2], vec_ref[2:3]
    outer_bias, gain_two, shift_two = vec_ref[3:4], vec_ref[4:5], vec_ref[5:6]

    def out_copies(slot):
        return [
            pltpu.make_async_copy(
                weight_refs[slot].at[pl.ds(first, target.shape[1])], target.at[slot], out_sems.at[which, slot]
            )
            for which, (target, first) in enumerate(
                ((out_buf, 3 * width + BIAS_ROWS), (bias_buf, 3 * width))
            )
        ]

    @pl.when(step == 0)
    def _():
        for slot in range(group):
            for copy in out_copies(slot):
                copy.start()

    stream_slots(tuple(range(group)), (up_refs, down_refs), (up_buf, down_buf), sems, (0, 0))

    @pl.when(step == 0)
    def _():
        for slot in range(group):
            for copy in out_copies(slot):
                copy.wait()
        _, blocks, _, size = context_refs[0].shape
        for block in range(blocks):
            total = dot(context_refs[0][0, block], out_buf[0], 0, 0)
            for slot in range(1, group):
                total += dot(context_refs[slot // turns][slot % turns, block], out_buf[slot], 0, 0)
            mixed[block * size : (block + 1) * size] = total

        def first(rows):
            hidden_one = frames_ref[0, rows].astype(f32) + mixed[rows] + out_bias
            normal, inverse = chunk_stats(hidden_one)
            normal_ref[rows] = normal.astype(bf16)
            inverse_ref[rows] = inverse
            normed = normal * gain_one + shift_one
            low_ref[rows] = normed.astype(bf16)
            mixed[rows] = normed + outer_bias

        row_chunks(count, first)

    biases = bias_buf[step].astype(f32)
    bias = jnp.concatenate([bias_row(biases, 2), bias_row(biases, 3)[:, 0 : hidden - depth]], axis=1)
    up_now, down_now = up_buf[step % 2], down_buf[step % 2]

    def gelu(rows):
        value = dot(low_ref[rows], up_now, 1, 1) + bias
        whole_part, bell = phi_parts(value)
        active = (value * whole_part).astype(bf16)
        active_ref[0, rows] = active
        slope_ref[0, rows] = (whole_part + value * bell).astype(bf16)
        mixed[rows] += dot(active, down_now, 1, 0)

    gelu(slice(None))

    @pl.when(step == pl.num_programs(0) - 1)
    def _():
        small_ref[...] = jnp.zeros_like(small_ref)

        def last(rows):
            normal, inverse = chunk_stats(mixed[rows])
            live = (ids_ref[rows] >= 0).astype(f32)
            layer_ref[rows] = ((normal * gain_two + shift_two) * live).astype(bf16)
            grad = cot_ref[0, rows].astype(f32) * live
            small_ref[0:1] += jnp.sum(grad * normal, axis=0, keepdims=True)
            small_ref[1:2] += jnp.sum(grad, axis=0, keepdims=True)
            scaled = grad * gain_two
            back = inverse * (
                scaled
                - jnp.mean(scaled, axis=-1, keepdims=True)
                - normal * jnp.mean(scaled * normal, axis=-1, keepdims=True)
            )
            small_ref[2:3] += jnp.sum(back, axis=0, keepdims=True)
            gradffn_ref[rows] = back.astype(bf16)

        row_chunks(count, last)


def up_back_kernel(
    order, last, group, low_ref, normal_ref, inverse_ref, before_ref, gradffn_ref, slope_ref,
    gain_ref, *refs,
):
    up_refs, down_refs, rest = refs[:group], refs[group : 2 * group], refs[2 * group :]
    if last:
        upgrad_ref, small_ref, gradone_ref, gradattn_ref, *rest = rest
    else:
        upgrad_ref, normed_grad, *rest = rest
    up_buf, down_buf, inner, sems, *rest = rest
    if last:
        normed_grad = rest[0]
    step = pl.program_id(0)
    count, hidden = inner.shape
    depth = low_ref.shape[1]
    stream_slots(order, (up_refs, down_refs), (up_buf, down_buf), sems, (0, 0))

    @pl.when(step == 0)
    def _():
        normed_grad[...] = before_ref[...] if last else gradffn_ref[...].astype(f32)

    grad_active = dot(gradffn_ref[...], down_buf[step % 2], 1, 1)
    inner[...] = (grad_active * slope_ref[0].astype(f32)).astype(bf16)
    upgrad_ref[0, 0:hidden] = dot(inner[...], low_ref[...], 0, 0).astype(bf16)
    ones = jnp.ones((8, count), bf16)
    bias = dot(ones, inner[...], 1, 0)
    row = lax.broadcasted_iota(jnp.int32, (upgrad_ref.shape[1] - hidden, depth), 0)
    extra = jnp.where(row == 0, bias[0:1, 0:depth], 0.0)
    rest_lanes = jnp.pad(bias[0:1, depth:hidden], ((0, 0), (0, 2 * depth - hidden)))
    upgrad_ref[0, hidden:] = jnp.where(row == 1, rest_lanes, extra).astype(bf16)
    normed_grad[...] += dot(inner[...], up_buf[step % 2], 1, 0)

    if last:

        @pl.when(step == pl.num_programs(0) - 1)
        def _():
            small_ref[...] = jnp.zeros_like(small_ref)
            gain = gain_ref[...]

            def last_rows(rows):
                grad, normal = normed_grad[rows], normal_ref[rows].astype(f32)
                small_ref[0:1] += jnp.sum(grad * normal, axis=0, keepdims=True)
                small_ref[1:2] += jnp.sum(grad, axis=0, keepdims=True)
                scaled = grad * gain
                back = inverse_ref[rows] * (
                    scaled
                    - jnp.mean(scaled, axis=-1, keepdims=True)
                    - normal * jnp.mean(scaled * normal, axis=-1, keepdims=True)
                )
                small_ref[2:3] += jnp.sum(back, axis=0, keepdims=True)
                gradone_ref[rows] = back
                gradattn_ref[rows] = back.astype(bf16)

            row_chunks(count, last_rows)


def down_back_kernel(
    order, group, active_ref, gradffn_ref, gradattn_ref, small_ref, smalltwo_ref, *refs
):
    context_refs, result_ref = refs[:-1], refs[-1]
    turns = group // len(context_refs)
    step = pl.program_id(0)
    hidden = active_ref.shape[2]
    depth = gradffn_ref.shape[1]
    _, blocks, width, size = context_refs[0].shape
    result_ref[0, 0:hidden] = dot(active_ref[0], gradffn_ref[...], 0, 0).astype(bf16)
    for position, slot in enumerate(order):

        @pl.when(step == position)
        def _():
            context = context_refs[slot // turns].at[slot % turns]
            total = dot(context[0], gradattn_ref[0:size], 1, 0)
            for block in range(1, blocks):
                total += dot(context[block], gradattn_ref[block * size : (block + 1) * size], 1, 0)
            result_ref[0, hidden : hidden + width] = total.astype(bf16)

    row = lax.broadcasted_iota(jnp.int32, (HIDDEN_EXTRA, depth), 0)
    extra = jnp.zeros((HIDDEN_EXTRA, depth), f32)
    for index in range(3):
        extra = jnp.where(row == index, small_ref[index : index + 1], extra)
        extra = jnp.where(row == 3 + index, smalltwo_ref[index : index + 1], extra)
    result_ref[0, hidden + width :] = extra.astype(bf16)


def ffn(place, frames, cotangent, ids, vectors, contexts, weights, up, down):
    group = len(up)
    count, depth = frames.shape[1:]
    hidden = down[0].shape[0]
    width = contexts[0].shape[2]
    own = pl.BlockSpec((1, count, depth), lambda s, place: (place[2], 0, 0))
    per_slot = pl.BlockSpec((1, count, hidden), lambda s, place: (s, 0, 0))
    spec = pltpu.PrefetchScalarGridSpec(
        num_scalar_prefetch=1,
        grid=(group,),
        in_specs=[own, own, whole(ids.shape), whole(vectors.shape)]
        + [whole(contexts[0].shape)] * len(contexts)
        + [ANYWHERE] * (3 * group),
        out_specs=[
            whole((count, depth)), whole((count, depth)), whole((count, depth)), whole((count, 1)),
            whole((count, depth)), whole((8, depth)), per_slot, per_slot,
        ],
        scratch_shapes=[
            pltpu.VMEM((2, hidden, depth), bf16),
            pltpu.VMEM((2, hidden, depth), bf16),
            pltpu.VMEM((group, width, depth), bf16),
            pltpu.VMEM((group, BIAS_ROWS, depth), bf16),
            pltpu.VMEM((count, depth), f32),
            pltpu.SemaphoreType.DMA((2, 2)),
            pltpu.SemaphoreType.DMA((2, group)),
        ],
    )
    shape = jax.ShapeDtypeStruct
    return pl.pallas_call(
        functools.partial(ffn_kernel, group),
        grid_spec=spec,
        out_shape=[
            shape((count, depth), bf16), shape((count, depth), bf16), shape((count, depth), bf16),
            shape((count, 1), f32), shape((count, depth), bf16), shape((8, depth), f32), shape((group, count, hidden), bf16),
            shape((group, count, hidden), bf16),
        ],
        cost_estimate=cost(2**34),
        compiler_params=limit(28),
        name="ffn",
    )(
        place, far_away(frames), far_away(cotangent), ids, vectors, *contexts, *weights, *up, *down
    )


def in_order(order):
    def slot_of(s):
        result = jnp.int32(order[-1])
        for position in reversed(range(len(order) - 1)):
            result = jnp.where(s == position, order[position], result)
        return result

    return slot_of


def everything(shape):
    return pl.BlockSpec(shape, lambda s: (0,) * len(shape))


def up_back(order, last, low, normal, inverse, before, gradffn, slope, gain, up, down):
    group = len(up)
    count, depth = low.shape
    hidden = slope.shape[2]
    slot_of = in_order(order)
    per_slot = pl.BlockSpec((1, count, hidden), lambda s: (slot_of(s), 0, 0))
    rows = hidden + HIDDEN_EXTRA
    shape = jax.ShapeDtypeStruct
    wide = shape((count, depth), f32)
    tail = [shape((8, depth), f32), wide, shape((count, depth), bf16)] if last else [wide]
    return pl.pallas_call(
        functools.partial(up_back_kernel, order, last, group),
        grid=(len(order),),
        in_specs=[
            everything(v.shape) for v in (low, normal, inverse, before, gradffn)
        ]
        + [per_slot, everything(gain.shape)]
        + [ANYWHERE] * (2 * group),
        out_specs=[pl.BlockSpec((1, rows, depth), lambda s: (s, 0, 0))]
        + [everything(t.shape) for t in tail],
        out_shape=[shape((len(order), rows, depth), bf16)] + tail,
        scratch_shapes=[
            pltpu.VMEM((2, hidden, depth), bf16),
            pltpu.VMEM((2, hidden, depth), bf16),
            pltpu.VMEM((count, hidden), bf16),
            pltpu.SemaphoreType.DMA((2, 2)),
        ]
        + ([pltpu.VMEM((count, depth), f32)] if last else []),
        cost_estimate=cost(2**33),
        compiler_params=limit(26),
        name="up_back",
    )(low, normal, inverse, before, gradffn, slope, gain, *up, *down)


def down_back(order, active, gradffn, gradattn, smalls, contexts):
    count, hidden = active.shape[1:]
    depth = gradffn.shape[1]
    width = contexts[0].shape[2]
    slot_of = in_order(order)
    rows = hidden + width + HIDDEN_EXTRA
    return pl.pallas_call(
        functools.partial(down_back_kernel, order, active.shape[0]),
        grid=(len(order),),
        in_specs=[pl.BlockSpec((1, count, hidden), lambda s: (slot_of(s), 0, 0))]
        + [everything(v.shape) for v in (gradffn, gradattn, *smalls, *contexts)],
        out_specs=pl.BlockSpec((1, rows, depth), lambda s: (s, 0, 0)),
        out_shape=jax.ShapeDtypeStruct((len(order), rows, depth), bf16),
        cost_estimate=cost(2**32),
        compiler_params=limit(20),
        name="down_back",
    )(active, gradffn, gradattn, *smalls, *contexts)


def swap(value, axis, distance):
    size = lax.axis_size(axis)
    return lax.ppermute(value, axis, [(i, i ^ distance) for i in range(size)])


def add_low(a, b):
    return (a.astype(f32) + b.astype(f32)).astype(bf16)


def add_three(a, b, c):
    return (a.astype(f32) + b.astype(f32) + c.astype(f32)).astype(bf16)


def hold(value, *others):
    return lax.optimization_barrier((value,) + tuple(others))[0]


def row_distances(size):
    distance, result = 1, []
    while distance < size:
        result.append(distance)
        distance *= 2
    return result


def join_rows(value, arrived, distance):
    upper = (lax.axis_index("rows") // distance) % 2 == 1
    return jnp.concatenate(
        [jnp.where(upper, arrived, value), jnp.where(upper, value, arrived)], axis=0
    )


def far_swap(value, far):
    return swap(value, "rows", (far & 1) * 2 + (far >> 1))


def own_quarter():
    here = lax.axis_index("rows")
    return here % 2 * 2 + here // 2 % 2


def quarters_of(value, axis=0):
    rows = value.shape[axis] // QUARTERS
    return [
        lax.dynamic_slice_in_dim(value, (own_quarter() ^ far) * rows, rows, axis)
        for far in range(QUARTERS)
    ]


def send_quarters(quarters):
    return [far_swap(quarters[far], far) for far in range(1, QUARTERS)]


def add_quarters(quarters, came):
    total = quarters[0].astype(f32)
    for value in came:
        total = total + value.astype(f32)
    return total.astype(bf16)


def join_pieces(pieces):
    near = [join_rows(pieces[i], pieces[i + 1], 2) for i in (0, 2)]
    return join_rows(near[0], near[1], 1)


def across(value, came, distances):
    value = add_low(value, came)
    for distance in distances:
        value = add_low(value, swap(value, "rows", distance))
    return value


def gather_slots(value):
    slots = {0: value}
    distance = lax.axis_size("heads") // 2
    while distance >= 1:
        for slot in list(slots):
            slots[slot ^ distance] = swap(slots[slot], "heads", distance)
        distance //= 2
    return [slots[slot] for slot in range(len(slots))]


def per_device(
    frames, segment_ids, cotangent, query_weight, query_bias, key_weight, value_weight, value_bias,
    output_weight, output_bias, first_gain, first_shift, inner_weight, inner_bias, outer_weight,
    outer_bias, second_gain, second_shift,
):
    group = lax.axis_size("heads")
    position = lax.axis_index("heads")
    row_count, row_length, depth = frames.shape
    own_len = row_count * row_length // group
    size = math.gcd(row_length, own_len)
    steps = own_len // size
    per_row = row_length // size
    width = query_weight.shape[1]
    heads_here = width // HEAD_DIM
    per_head = FF_LIVE // HEADS_LIVE
    hidden_slots = inner_weight.shape[1]
    hidden_cap = min(hidden_slots, (HEADS_LIVE + group - 1) // group * per_head)

    def live_of(index):
        return HEADS_LIVE // group + (index < HEADS_LIVE % group).astype(jnp.int32)

    rest = row_distances(lax.axis_size("rows"))[2:]
    piece_rows = hidden_cap // QUARTERS
    place = jnp.stack(
        [position * steps, jnp.int32(per_row), position]
        + [live_of(position ^ slot) for slot in range(group)]
        + [own_quarter() * piece_rows, own_quarter()]
    )
    blocks = frames.reshape(row_count * per_row, size, depth)
    weight_own = prepare(
        place, query_weight.T, key_weight.T, value_weight.T, query_bias[None], value_bias[None],
        inner_bias[None], output_weight, outer_weight, piece_rows,
    )
    weight = {0: weight_own, 1: swap(weight_own, "heads", 1), 2: swap(weight_own, "heads", 2)}
    up_own, down_own, keyf, queryf = prepare_wide(
        place, inner_weight, outer_weight, segment_ids,
        segment_ids.reshape(row_count * per_row, 1, size), hidden_cap,
    )
    up = {0: up_own, 1: swap(up_own, "heads", 1)}
    down = {0: down_own, 1: swap(down_own, "heads", 1)}
    half = group // 2

    def forward(first, *waits):
        return attend(
            first, place, hold(blocks, *waits), frames,
            [weight[slot] for slot in range(first, first + half)], keyf, queryf, steps, width,
        )

    saved = [forward(0)]
    done = saved[0][0]
    weight[2] = hold(weight[2], done)
    weight[3] = swap(weight[2], "heads", 1)
    up[2] = swap(hold(up_own, weight[2]), "heads", 2)
    piece = weight[2][4 * width + BIAS_ROWS :]
    pieces = [piece] + send_quarters([piece] * QUARTERS)
    saved.append(forward(half, done))
    down[2] = join_pieces(hold(pieces, saved[1][0]))
    up[3] = swap(up[2], "heads", 1)
    down[3] = swap(down[2], "heads", 1)
    up = [up[slot] for slot in range(group)]
    down = [down[slot] for slot in range(group)]
    contexts = [kept[3] for kept in saved]

    vectors = jnp.stack(
        [output_bias, first_gain, first_shift, outer_bias, second_gain, second_shift]
    )
    whole_frames = frames.reshape(group, own_len, depth)
    whole_cot = cotangent.reshape(group, own_len, depth)
    flat_ids = segment_ids.reshape(row_count * row_length)
    ids_own = lax.dynamic_slice_in_dim(flat_ids, position * own_len, own_len)[:, None]
    layer_own, normed_low, normal_one, inverse_one, grad_ffn, small_two, actives, slopes = ffn(
        place, whole_frames, whole_cot, ids_own, vectors, contexts,
        [weight[slot] for slot in range(group)], up, down,
    )
    layer = {0: layer_own, 1: swap(layer_own, "heads", 1), 2: swap(layer_own, "heads", 2)}
    known = (normed_low, normal_one, inverse_one)
    gain = first_gain[None]
    up_send, grad_part = up_back((1, 3), False, *known, inverse_one, grad_ffn, slopes, gain, up, down)
    up_came = swap(up_send, "heads", 1)
    layer[1] = hold(layer[1], grad_part)
    up_keep, small_one, grad_hidden_one, grad_attn = up_back(
        (0, 2), True, *known, grad_part, grad_ffn, slopes, gain, up, down
    )
    barrier = lax.optimization_barrier
    up_quarters = quarters_of(add_low(up_keep, up_came), 1)
    up_came = send_quarters(up_quarters)

    smalls = (small_one, small_two)
    down_send = down_back((1, 3), actives, hold(grad_ffn, up_quarters), grad_attn, smalls, contexts)
    down_came = swap(down_send, "heads", 1)
    down_keep = down_back((0, 2), actives, hold(grad_ffn, down_send), grad_attn, smalls, contexts)
    down_came = hold(down_came, down_keep)
    grad_attn = grad_attn.reshape(steps, size, depth)
    block_sum = grad_hidden_one.reshape(steps, size, depth)
    row_sum = jnp.zeros((8, 128), f32)
    grads = {}

    def back(slot, first, block_sum, row_sum, *waits):
        return attend_back(
            slot, first, place, blocks, frames, weight[slot], saved[slot // half], grad_attn,
            hold(block_sum, *waits), row_sum,
        )

    layer[2] = hold(layer[2], down_keep)
    layer[3] = swap(layer[2], "heads", 1)
    down_two = add_low(down_keep[1], down_came[1])
    cut = down_two.shape[0] // 2
    down_first = swap(hold(down_two[:cut], layer[2]), "heads", 2)
    grads[3], block_sum, row_sum = back(3, True, block_sum, row_sum, layer[2], down_two)

    block_sum, up_came, down_first, layer[3], grads[3] = barrier(
        (block_sum, up_came, down_first, layer[3], grads[3])
    )
    down_second = swap(hold(down_two[cut:], down_first), "heads", 2)
    grads_came = swap(grads[3], "heads", 1)
    up_pair = add_quarters(up_quarters, up_came)
    up_came = swap(up_pair[1], "heads", 2)
    grads[2], block_sum, row_sum = back(2, False, block_sum, row_sum, up_pair)

    block_sum, up_came, down_second, grads_came, grads[2] = barrier(
        (block_sum, up_came, down_second, grads_came, grads[2])
    )
    attn_two = add_low(grads[2], grads_came)
    attn_rows = attn_two.shape[0] // 2
    attn_first = swap(attn_two[:attn_rows], "heads", 2)
    up_piece = add_low(up_pair[0], up_came)
    up_came = swap(up_piece, "rows", rest[0])
    down_far = jnp.concatenate([down_first, down_second])
    down_quarters = quarters_of(add_three(down_keep[0], down_came[0], down_far))
    down_came = send_quarters(down_quarters)
    grads[1], block_sum, row_sum = back(
        1, False, block_sum, row_sum, attn_two, up_piece, down_quarters
    )

    block_sum, up_came, down_came, attn_first, grads[1] = barrier(
        (block_sum, up_came, down_came, attn_first, grads[1])
    )
    grads_came = swap(grads[1], "heads", 1)
    up_piece = across(up_piece, up_came, rest[1:])
    attn_second = swap(hold(attn_two[attn_rows:], attn_first), "heads", 2)
    up_came = swap(up_piece, "rows", 2)
    down_piece = add_quarters(down_quarters, down_came)
    down_came = swap(down_piece, "rows", rest[0])
    grads[0], block_sum, row_sum = back(0, False, block_sum, row_sum, up_piece, down_piece)
    block_sum, up_came, down_came, attn_second, grads_came, grads[0] = barrier(
        (block_sum, up_came, down_came, attn_second, grads_came, grads[0])
    )

    reach, pairs = [0], {}
    for distance in range(1, group):
        pairs[distance] = []
        for i in range(group):
            j = i ^ distance
            rows_i = range(i * steps // per_row, ((i + 1) * steps - 1) // per_row + 1)
            rows_j = range(j * steps // per_row, ((j + 1) * steps - 1) // per_row + 1)
            if set(rows_i) & set(rows_j):
                pairs[distance].append((i, j))
        if pairs[distance]:
            reach.append(distance)
    own_grad, *owed = shares(place, row_sum, block_sum, tuple(reach))
    attn_two = jnp.concatenate([attn_first, attn_second])
    attn_quarters = quarters_of(add_three(hold(grads[0], owed), grads_came, attn_two))
    owed = [
        lax.ppermute(sent, "heads", pairs[distance]) for distance, sent in zip(reach[1:], owed)
    ]
    attn_came = send_quarters(attn_quarters)
    up_half = join_rows(up_piece, hold(up_came, own_grad), 2)
    down_piece = across(down_piece, hold(down_came, own_grad), rest[1:])
    layer[0] = hold(layer[0], own_grad)
    layer_out = assemble(
        place, [(slot, 0, layer[slot]) for slot in range(group)], own_len, row_count * row_length
    ).reshape(frames.shape)
    attn_came, owed, layer_out, up_half, down_piece = barrier(
        (attn_came, owed, layer_out, up_half, down_piece)
    )

    attn_piece = add_quarters(attn_quarters, attn_came)
    attn_came = swap(attn_piece, "rows", rest[0])
    up_came = swap(hold(up_half, attn_piece), "rows", 1)
    down_came = swap(hold(down_piece, attn_piece), "rows", 2)
    for came in owed:
        own_grad = own_grad + hold(came, attn_piece).astype(f32)
    own_grad = own_grad.astype(bf16).reshape(own_len, depth)
    cut = own_len // 2 // 8 * 8
    first_cut = swap(own_grad[:cut], "heads", 2)
    mate = swap(own_grad, "heads", 1)
    attn_came, first_cut, mate, up_came, down_came = barrier(
        (attn_came, first_cut, mate, up_came, down_came)
    )

    attn_piece = across(attn_piece, attn_came, rest[1:])
    attn_came = send_quarters([attn_piece] * QUARTERS)
    second_cut = swap(hold(own_grad[cut:], attn_piece), "heads", 2)
    down_half = join_rows(down_piece, down_came, 2)
    down_came = swap(down_half, "rows", 1)
    up_done = finish(
        finish_up_kernel, place, [hold(up_half, attn_piece), up_came],
        [(depth, hidden_slots), (8, depth)], "finish_up",
    )
    second_cut, up_done, attn_came = barrier((second_cut, up_done, attn_came))
    second_mate = swap(second_cut, "heads", 1)
    first_mate = swap(hold(first_cut, second_cut), "heads", 1)
    attn_done = finish(
        finish_attn_kernel, place, [attn_piece, *attn_came],
        [(width, depth)] * 3 + [(8, depth)], "finish_attn",
    )
    frames_grad = assemble(
        place,
        [
            (0, 0, own_grad), (1, 0, mate), (2, 0, first_cut), (2, cut, second_cut),
            (3, 0, first_mate), (3, cut, second_mate),
        ],
        own_len, row_count * row_length,
    ).reshape(frames.shape)
    down_done = finish(
        functools.partial(finish_down_kernel, per_head), place,
        [down_half, hold(down_came, frames_grad)],
        [(hidden_slots, depth), (width, depth), (8, depth)], "finish_down",
    )

    innerbias = jnp.concatenate([up_done[1][0], up_done[1][1, : hidden_cap - depth]])
    innerbias_full = jnp.pad(innerbias, ((0, hidden_slots - hidden_cap),))
    extra = attn_done[3]
    small = down_done[2]
    return (
        layer_out,
        frames_grad,
        attn_done[0].T,
        extra[0, :width],
        attn_done[1].T,
        attn_done[2].T,
        extra[1, :width],
        down_done[1],
        small[2],
        small[0],
        small[1],
        up_done[0],
        innerbias_full,
        down_done[0],
        small[5],
        small[3],
        small[4],
    )


def solution(mesh):
    in_specs = (
        P("rows", None, None), P("rows", None), P("rows", None, None), P(None, "heads"), P("heads"),
        P(None, "heads"), P(None, "heads"), P("heads"), P("heads", None), P(), P(), P(),
        P(None, "heads"), P("heads"), P("heads", None), P(), P(), P(),
    )
    out_specs = (
        P("rows", None, None), P("rows", None, None), P(None, "heads"), P("heads"), P(None, "heads"),
        P(None, "heads"), P("heads"), P("heads", None), P(), P(), P(), P(None, "heads"), P("heads"),
        P("heads", None), P(), P(), P(),
    )
    return jax.shard_map(
        per_device, mesh=mesh, in_specs=in_specs, out_specs=out_specs, check_vma=False
    )
```

```python
import functools
import math

import jax
import jax.numpy as jnp
from jax import lax
from jax.experimental import pallas as pl
from jax.experimental.pallas import tpu as pltpu
from jax.sharding import PartitionSpec as P

HEADS_LIVE = 10
HEAD_SLOTS = 12
HEAD_DIM = 64
FF_LIVE = 2240
PAD_HEAD = 128
SEGMENTS = 5
MASK_STEP = -(2.0**30)
norm_eps = 1e-05
f32 = jnp.float32
bf16 = jnp.bfloat16


def dot(a, b, ca, cb):
    return lax.dot_general(a, b, (((ca,), (cb,)), ((), ())), preferred_element_type=f32)


def three_parts(value):
    high = value.astype(bf16).astype(f32)
    middle = (value - high).astype(bf16).astype(f32)
    return high, middle, value - high - middle


def live_heads(live, heads, one_head):
    least = HEADS_LIVE * heads // HEAD_SLOTS
    for head in range(least):
        one_head(head)
    for head in range(least, heads):

        @pl.when(head < live)
        def _():
            one_head(head)


def feature_rows(base, value):
    high, middle, low = three_parts(-value)
    row = lax.broadcasted_iota(jnp.int32, base.shape, 0)
    base = jnp.where(row == SEGMENTS, high, base)
    base = jnp.where(row == SEGMENTS + 1, middle, base)
    return jnp.where(row == SEGMENTS + 2, low, base).astype(bf16)


def bias_row(rows, index):
    first = 3 * index
    return rows[first : first + 1] + rows[first + 1 : first + 2] + rows[first + 2 : first + 3]


def attend_kernel(
    first, place, block_ref, row_ref, keyf_ref, queryf_ref, *refs,
):
    pair = len(refs) - 5
    weight_refs, (query_ref, key_ref, value_ref, context_ref, weight_ref) = refs[:pair], refs[pair:]
    turn = pl.program_id(0)
    step = pl.program_id(1)
    per_row, live = place[1], place[3 + first + turn]
    row_now = (place[0] + step) // per_row
    row_before = (place[0] + step - 1) // per_row
    length = row_ref.shape[1]
    width = context_ref.shape[2]
    heads = width // HEAD_DIM

    for index, ref in enumerate(weight_refs):

        @pl.when(jnp.logical_and(step == 0, turn == index))
        def _():
            weight_ref[...] = ref[...]

    biases = weight_ref[3 * width :].astype(f32)

    @pl.when(jnp.logical_or(step == 0, row_now != row_before))
    def _():
        frames = row_ref[0]
        keys = dot(frames, weight_ref[width : 2 * width], 1, 1).astype(bf16)
        values = dot(frames, weight_ref[2 * width : 3 * width], 1, 1)
        values = (values + bias_row(biases, 1)[:, 0:width]).astype(bf16)
        features = keyf_ref[0]
        for head in range(heads):
            cut = slice(head * HEAD_DIM, (head + 1) * HEAD_DIM)
            key_ref[0, 0, head * length : (head + 1) * length] = jnp.concatenate(
                [keys[:, cut], features], axis=1
            )
            value_ref[0, 0, head * length : (head + 1) * length] = jnp.concatenate(
                [values[:, cut], features], axis=1
            )

    qbias = jnp.broadcast_to(bias_row(biases, 0)[:, 0:width], (8, width)).T[:, 0:1]
    queries = (dot(weight_ref[0:width], block_ref[0], 1, 1) + qbias).astype(bf16)
    queries = queries * jnp.asarray(HEAD_DIM**-0.5, bf16)
    for head in range(heads):
        query_ref[0, 0, head * PAD_HEAD : head * PAD_HEAD + HEAD_DIM] = queries[
            head * HEAD_DIM : (head + 1) * HEAD_DIM
        ]
        query_ref[0, 0, head * PAD_HEAD + HEAD_DIM : (head + 1) * PAD_HEAD] = queryf_ref[0]
    context_ref[...] = jnp.zeros_like(context_ref)

    def one_head(head):
        keys = key_ref[0, 0, pl.ds(head * length, length)]
        values = value_ref[0, 0, pl.ds(head * length, length)]
        start = head * PAD_HEAD
        scores = dot(keys, query_ref[0, 0, pl.ds(start, PAD_HEAD)], 1, 0)
        highest = jnp.max(scores, axis=0, keepdims=True)
        probs = jnp.exp(scores - highest).astype(bf16)
        mixed = dot(values, probs, 0, 0)
        total = mixed[HEAD_DIM + SEGMENTS : HEAD_DIM + SEGMENTS + 1]
        context = mixed[0:HEAD_DIM] / total
        context_ref[0, 0, pl.ds(head * HEAD_DIM, HEAD_DIM)] = context.astype(bf16)
        base = queryf_ref[0, 0:16].astype(f32)
        query_ref[0, 0, pl.ds(start + HEAD_DIM, 16)] = feature_rows(base, highest + jnp.log(total))

    live_heads(live, heads, one_head)


def attend_back_kernel(
    slot, first, place, block_ref, row_ref, weight_ref, query_ref, key_ref, value_ref,
    context_ref, grad_ref, blocksum_ref, rowsum_ref,
    gradw_ref, blockout_ref, rowout_ref,
    weight_acc, dkey, dvalue, picked, dcontext, dquery, bias_acc,
):
    step = pl.program_id(0)
    steps = pl.num_programs(0)
    per_row, live = place[1], place[3 + slot]
    row_now = (place[0] + step) // per_row
    row_before = (place[0] + step - 1) // per_row
    row_after = (place[0] + step + 1) // per_row
    length, depth = row_ref.shape[1:]
    width = context_ref.shape[2]
    heads = width // HEAD_DIM
    ones = jnp.ones((8, length), bf16)

    @pl.when(step == 0)
    def _():
        weight_acc[...] = jnp.zeros_like(weight_acc)
        bias_acc[...] = jnp.zeros_like(bias_acc)
        picked[...] = jnp.zeros_like(picked)

    @pl.when(jnp.logical_or(step == 0, row_now != row_before))
    def _():
        dkey[...] = jnp.zeros_like(dkey)
        dvalue[...] = jnp.zeros_like(dvalue)

    dcontext[...] = dot(weight_ref[3 * width + BIAS_ROWS :], grad_ref[0], 1, 1).astype(bf16)
    dquery[...] = jnp.zeros_like(dquery)

    def one_head(head):
        own = pl.ds(head * HEAD_DIM, HEAD_DIM)
        keys = key_ref[0, 0, pl.ds(head * length, length)]
        values = value_ref[0, 0, pl.ds(head * length, length)]
        queries = query_ref[0, 0, pl.ds(head * PAD_HEAD, PAD_HEAD)]
        grad = dcontext[own]
        inner = jnp.sum(grad.astype(f32) * context_ref[0, 0, own].astype(f32), axis=0, keepdims=True)
        extra = feature_rows(jnp.zeros((PAD_HEAD - HEAD_DIM, grad.shape[1]), f32), inner)
        probs = jnp.exp(dot(keys, queries, 1, 0))
        dprobs = dot(values, jnp.concatenate([grad, extra], axis=0), 1, 0)
        dscores = (probs * dprobs).astype(bf16)
        picked[0, pl.ds(head * width + head * HEAD_DIM, HEAD_DIM)] = grad
        picked[1, pl.ds(head * width + head * HEAD_DIM, HEAD_DIM)] = queries[0:HEAD_DIM]
        place_head = pl.ds(head * width, width)
        dvalue[...] += dot(probs.astype(bf16), picked[0, place_head], 1, 1)
        dkey[...] += dot(dscores, picked[1, place_head], 1, 1)
        dquery[own] = (dot(keys, dscores, 0, 0)[0:HEAD_DIM] * HEAD_DIM**-0.5).astype(bf16)

    live_heads(live, heads, one_head)
    weight_acc[0:width] += dot(dquery[...], block_ref[0], 1, 0)
    blockout_ref[0] = blocksum_ref[0] + dot(dquery[...], weight_ref[0:width], 0, 0)
    bias_acc[0:8] += dot(ones[:, 0 : dquery.shape[1]], dquery[...], 1, 1)

    @pl.when(jnp.logical_or(step == steps - 1, row_now != row_after))
    def _():
        keys_low = dkey[...].astype(bf16)
        values_low = dvalue[...].astype(bf16)
        weight_acc[width : 2 * width] += dot(keys_low, row_ref[0], 0, 0)
        weight_acc[2 * width : 3 * width] += dot(values_low, row_ref[0], 0, 0)
        back = dot(keys_low, weight_ref[width : 2 * width], 1, 0) + dot(
            values_low, weight_ref[2 * width : 3 * width], 1, 0
        )
        if first:
            rowout_ref[0] = back
        else:
            rowout_ref[0] = rowsum_ref[0] + back
        bias_acc[8:16] += dot(ones, values_low, 1, 0)

    @pl.when(step == steps - 1)
    def _():
        gradw_ref[0 : 3 * width] = weight_acc[...].astype(bf16)
        row = lax.broadcasted_iota(jnp.int32, (gradw_ref.shape[0] - 3 * width, depth), 0)
        lanes = depth - width
        extra = jnp.where(row == 0, jnp.pad(bias_acc[0:1], ((0, 0), (0, lanes))), 0.0)
        extra = jnp.where(row == 1, jnp.pad(bias_acc[8:9], ((0, 0), (0, lanes))), extra)
        gradw_ref[3 * width :] = extra.astype(bf16)


def whole(shape):
    return pl.BlockSpec(shape, lambda b, place: (0,) * len(shape))


def limit(mib):
    return pltpu.CompilerParams(vmem_limit_bytes=mib * 2**20)


def cost(flops):
    return pl.CostEstimate(flops=2**40, bytes_accessed=2**33, transcendentals=0)


ANYWHERE = pl.BlockSpec(memory_space=pltpu.HBM)


def far_away(value):
    return pltpu.with_memory_space_constraint(value, pltpu.HBM)
BIAS_ROWS = 16
EXTRA_ROWS = 32
HIDDEN_EXTRA = 32


def row_of(b, place):
    return (place[0] + b) // place[1], 0, 0


def rel_row(b, place):
    return (place[0] + b) // place[1] - place[0] // place[1], 0, 0


def block_of(b, place):
    return place[0] + b, 0, 0


def local(b, place):
    return b, 0, 0


def attend(first, place, blocks, rows, weights, keyf, queryf, steps, width):
    size, depth = blocks.shape[1:]
    count, length, _ = rows.shape
    weight_shape = (3 * width + BIAS_ROWS, depth)
    heads = width // HEAD_DIM
    window = min(2, count)
    pair = len(weights)
    fixed = lambda shape: pl.BlockSpec(shape, lambda s, b, place: (0,) * len(shape))
    per_row = lambda shape: pl.BlockSpec((1,) + shape, lambda s, b, place: row_of(b, place))
    per_block = lambda shape: pl.BlockSpec((1,) + shape, lambda s, b, place: block_of(b, place))
    out_row = pl.BlockSpec(
        (1, 1, heads * length, PAD_HEAD), lambda s, b, place: (s,) + rel_row(b, place)
    )
    out_block = lambda rows: pl.BlockSpec((1, 1, rows, size), lambda s, b, place: (s, b, 0, 0))
    spec = pltpu.PrefetchScalarGridSpec(
        num_scalar_prefetch=1,
        grid=(pair, steps),
        in_specs=[
            per_block((size, depth)), per_row((length, depth)), per_row(keyf.shape[1:]),
            per_block(queryf.shape[1:]),
        ]
        + [fixed(weight_shape)] * pair,
        out_specs=[out_block(heads * PAD_HEAD), out_row, out_row, out_block(width)],
        scratch_shapes=[pltpu.VMEM(weight_shape, bf16)],
    )
    return pl.pallas_call(
        functools.partial(attend_kernel, first),
        grid_spec=spec,
        out_shape=[
            jax.ShapeDtypeStruct((pair, steps, heads * PAD_HEAD, size), bf16),
            jax.ShapeDtypeStruct((pair, window, heads * length, PAD_HEAD), bf16),
            jax.ShapeDtypeStruct((pair, window, heads * length, PAD_HEAD), bf16),
            jax.ShapeDtypeStruct((pair, steps, width, size), bf16),
        ],
        cost_estimate=cost(2**33),
        compiler_params=limit(FORWARD_LIMIT),
        name="attend",
    )(place, blocks, rows, keyf, queryf, *map(far_away, weights))


FORWARD_LIMIT = 60


def attend_back(slot, first, place, blocks, rows, weight, saved, grad, blocksum, rowsum):
    query, key, value, context = saved
    steps, size, depth = blocksum.shape
    count, length, _ = rows.shape
    width = context.shape[2]
    heads = width // HEAD_DIM
    turn = slot % query.shape[0]
    pinned = query.shape[0]
    saved_block = lambda v: pl.BlockSpec(
        (1, 1) + v.shape[2:], lambda b, place: (turn,) + local(b, place)
    )
    saved_row = lambda v: pl.BlockSpec(
        (1, 1) + v.shape[2:], lambda b, place: (turn,) + rel_row(b, place)
    )
    row_spec = pl.BlockSpec((1, length, depth), rel_row)
    near = far_away if slot >= pinned else lambda value: value
    spec = pltpu.PrefetchScalarGridSpec(
        num_scalar_prefetch=1,
        grid=(steps,),
        in_specs=[
            pl.BlockSpec((1, size, depth), block_of),
            pl.BlockSpec((1, length, depth), row_of),
            whole((4 * width + BIAS_ROWS, depth)),
            saved_block(query), saved_row(key), saved_row(value), saved_block(context),
            pl.BlockSpec((1, size, depth), local),
            pl.BlockSpec((1, size, depth), local),
            ANYWHERE if first else row_spec,
        ],
        out_specs=[
            whole((3 * width + EXTRA_ROWS, depth)),
            pl.BlockSpec((1, size, depth), local),
            row_spec,
        ],
        scratch_shapes=[
            pltpu.VMEM((3 * width, depth), f32),
            pltpu.VMEM((length, width), f32),
            pltpu.VMEM((length, width), f32),
            pltpu.VMEM((2, heads * width, size), bf16),
            pltpu.VMEM((width, size), bf16),
            pltpu.VMEM((width, size), bf16),
            pltpu.VMEM((16, width), f32),
        ],
    )
    return pl.pallas_call(
        functools.partial(attend_back_kernel, slot, first),
        grid_spec=spec,
        out_shape=[
            jax.ShapeDtypeStruct((3 * width + EXTRA_ROWS, depth), bf16),
            jax.ShapeDtypeStruct(blocksum.shape, f32),
            jax.ShapeDtypeStruct((min(2, count), length, depth), f32),
        ],
        input_output_aliases={} if first else {10: 2},
        cost_estimate=cost(2**34),
        compiler_params=limit(26),
        name="attend_back",
    )(
        place, near(blocks), near(rows), near(weight), query, near(key), near(value), context, grad,
        blocksum, rowsum,
    )


def prepare_kernel(
    per_head, place, query_ref, key_ref, value_ref, qbias_ref, vbias_ref, ubias_ref, out_ref, down_ref,
    weight_ref, piece_ref,
):
    width, depth = query_ref.shape
    weight_ref[0:width] = query_ref[...]
    weight_ref[width : 2 * width] = key_ref[...]
    weight_ref[2 * width : 3 * width] = value_ref[...]
    lanes = ubias_ref.shape[0]
    row = lax.broadcasted_iota(jnp.int32, (BIAS_ROWS, depth), 0)
    result = jnp.zeros((BIAS_ROWS, depth), f32)
    qbias, vbias, ubias = qbias_ref[...][None], vbias_ref[...][None], ubias_ref[...][None]
    vectors = [
        jnp.pad(qbias, ((0, 0), (0, depth - width))),
        jnp.pad(vbias, ((0, 0), (0, depth - width))),
        ubias[:, 0:depth],
        jnp.pad(ubias[:, depth:lanes], ((0, 0), (0, 2 * depth - lanes))),
    ]
    for index, vector in enumerate(vectors):
        for offset, part in enumerate(three_parts(vector)):
            result = jnp.where(row == 3 * index + offset, part, result)
    first = 3 * width + BIAS_ROWS
    weight_ref[3 * width : first] = result.astype(bf16)
    row = lax.broadcasted_iota(jnp.int32, out_ref.shape, 0)
    kept = jnp.where(row < place[3] * HEAD_DIM, out_ref[...].astype(f32), 0.0)
    weight_ref[first : first + width] = kept.astype(bf16)
    piece = piece_ref.shape[0]
    start = place[3 + SLOT_COUNT]
    row = start + lax.broadcasted_iota(jnp.int32, (piece, depth), 0)
    kept = down_ref[pl.ds(pl.multiple_of(start, 8), piece)].astype(f32)
    piece_ref[...] = jnp.where(row < place[3] * per_head, kept, 0.0).astype(bf16)


SLOT_COUNT = 4


def prepare(place, query, key, value, qbias, vbias, ubias, out, down, piece):
    width, depth = query.shape
    shapes = [(4 * width + BIAS_ROWS, depth), (piece, depth)]
    args = (query, key, value, qbias, vbias, ubias, out, down)
    return pl.pallas_call(
        functools.partial(prepare_kernel, FF_LIVE // HEADS_LIVE),
        grid_spec=pltpu.PrefetchScalarGridSpec(
            num_scalar_prefetch=1,
            grid=(1,),
            in_specs=[whole(v.shape) for v in args],
            out_specs=[whole(shape) for shape in shapes],
        ),
        out_shape=[jax.ShapeDtypeStruct(shape, bf16) for shape in shapes],
        compiler_params=limit(60),
        name="prepare",
    )(place, *args)


def prepare_wide_kernel(
    per_head, place, up_ref, down_ref, ids_ref, blocks_ref,
    upout_ref, downout_ref, keyf_ref, queryf_ref,
):
    hidden = downout_ref.shape[0]
    upout_ref[...] = up_ref[...].T[0:hidden]
    row = lax.broadcasted_iota(jnp.int32, downout_ref.shape, 0)
    kept = jnp.where(row < place[3] * per_head, down_ref[0:hidden].astype(f32), 0.0)
    downout_ref[...] = kept.astype(bf16)
    rows, length = ids_ref.shape
    feature = lax.broadcasted_iota(jnp.int32, (HEAD_DIM, length), 0)
    for r in range(rows):
        same = jnp.where(feature == ids_ref[r : r + 1] + 1, 1.0, 0.0)
        ones = jnp.where(jnp.logical_and(feature >= SEGMENTS, feature < SEGMENTS + 3), 1.0, same)
        keyf_ref[r] = ones.T.astype(bf16)
    size = blocks_ref.shape[2]
    feature = lax.broadcasted_iota(jnp.int32, (HEAD_DIM, size), 0)
    for b in range(blocks_ref.shape[0]):
        other = jnp.logical_and(feature < SEGMENTS, feature != blocks_ref[b] + 1)
        queryf_ref[b] = jnp.where(other, MASK_STEP, 0.0).astype(bf16)


def prepare_wide(place, up, down, ids, id_blocks, hidden):
    depth = up.shape[0]
    rows, length = ids.shape
    shapes = [
        (hidden, depth), (hidden, depth), (rows, length, HEAD_DIM),
        (id_blocks.shape[0], HEAD_DIM, id_blocks.shape[2]),
    ]
    return pl.pallas_call(
        functools.partial(prepare_wide_kernel, FF_LIVE // HEADS_LIVE),
        grid_spec=pltpu.PrefetchScalarGridSpec(
            num_scalar_prefetch=1,
            grid=(1,),
            in_specs=[whole(v.shape) for v in (up, down, ids, id_blocks)],
            out_specs=[whole(shape) for shape in shapes],
        ),
        out_shape=[jax.ShapeDtypeStruct(shape, bf16) for shape in shapes],
        compiler_params=limit(60),
        name="prepare_wide",
    )(place, up, down, ids, id_blocks)


def assemble_kernel(parts, share, place, *refs):
    sources, (out_ref, *rest) = refs[: len(parts)], refs[len(parts) :]
    buffers, sems = rest[:-1], rest[-1]
    inward, outward = [], []
    for index, (slot, first) in enumerate(parts):
        rows = buffers[index].shape[0]
        start = pl.multiple_of((place[2] ^ slot) * share + first, 8)
        inward.append(pltpu.make_async_copy(sources[index], buffers[index], sems.at[0, index]))
        outward.append(
            pltpu.make_async_copy(buffers[index], out_ref.at[pl.ds(start, rows)], sems.at[1, index])
        )
    for copy in inward:
        copy.start()
    for into, out in zip(inward, outward):
        into.wait()
        out.start()
    for copy in outward:
        copy.wait()


def assemble(place, pieces, share, total):
    depth = pieces[0][2].shape[1]
    arrays = [piece[2] for piece in pieces]
    parts = tuple(piece[:2] for piece in pieces)
    return pl.pallas_call(
        functools.partial(assemble_kernel, parts, share),
        grid_spec=pltpu.PrefetchScalarGridSpec(
            num_scalar_prefetch=1,
            grid=(1,),
            in_specs=[ANYWHERE] * len(arrays),
            out_specs=ANYWHERE,
            scratch_shapes=[pltpu.VMEM(v.shape, v.dtype) for v in arrays]
            + [pltpu.SemaphoreType.DMA((2, len(arrays)))],
        ),
        out_shape=jax.ShapeDtypeStruct((total, depth), arrays[0].dtype),
        cost_estimate=cost(0),
        compiler_params=limit(12),
        name="assemble",
    )(place, *arrays)


QUARTERS = 4


def collect(place, refs, buffer):
    share = refs[0].shape[0]
    number = place[4 + SLOT_COUNT] * len(refs) // QUARTERS
    for far, ref in enumerate(refs):
        start = (number ^ far) * share
        buffer[pl.ds(pl.multiple_of(start, 8), share)] = ref[...].astype(f32)


def finish_up_kernel(place, *refs):
    pieces, (grad_ref, bias_ref, buffer) = refs[:-3], refs[-3:]
    collect(place, pieces, buffer)
    depth, slots = grad_ref.shape
    hidden = buffer.shape[0] - HIDDEN_EXTRA
    grad_ref[:, 0:hidden] = buffer[0:hidden].T
    if slots > hidden:
        grad_ref[:, hidden:] = jnp.zeros((depth, slots - hidden), f32)
    bias_ref[...] = buffer[hidden : hidden + 8]


def finish_down_kernel(per_head, place, *refs):
    pieces, (grad_ref, out_ref, extra_ref, buffer) = refs[:-4], refs[-4:]
    collect(place, pieces, buffer)
    width = out_ref.shape[0]
    hidden = buffer.shape[0] - HIDDEN_EXTRA - width
    row = lax.broadcasted_iota(jnp.int32, (hidden, buffer.shape[1]), 0)
    grad_ref[0:hidden] = jnp.where(row < place[3] * per_head, buffer[0:hidden], 0.0)
    if grad_ref.shape[0] > hidden:
        grad_ref[hidden:] = jnp.zeros((grad_ref.shape[0] - hidden, buffer.shape[1]), f32)
    out_ref[...] = buffer[hidden : hidden + width]
    extra_ref[...] = buffer[hidden + width : hidden + width + 8]


def finish_attn_kernel(place, *refs):
    pieces, (query_ref, key_ref, value_ref, extra_ref, buffer) = refs[:QUARTERS], refs[QUARTERS:]
    collect(place, pieces, buffer)
    width = query_ref.shape[0]
    for index, ref in enumerate((query_ref, key_ref, value_ref)):
        ref[...] = buffer[index * width : (index + 1) * width]
    extra_ref[...] = buffer[3 * width : 3 * width + 8]


def finish(kernel, place, pieces, shapes, name):
    rows, depth = pieces[0].shape[0] * len(pieces), pieces[0].shape[1]
    return pl.pallas_call(
        kernel,
        grid_spec=pltpu.PrefetchScalarGridSpec(
            num_scalar_prefetch=1,
            grid=(1,),
            in_specs=[whole(v.shape) for v in pieces],
            out_specs=[whole(shape) for shape in shapes],
            scratch_shapes=[pltpu.VMEM((rows, depth), f32)],
        ),
        out_shape=[jax.ShapeDtypeStruct(shape, f32) for shape in shapes],
        cost_estimate=cost(0),
        compiler_params=limit(20),
        name=name,
    )(place, *pieces)


def shares_kernel(distances, group, place, *refs):
    step = pl.program_id(0)
    steps = pl.num_programs(0)
    count = len(distances)
    sources, blocksum_ref, (own_ref, *sent_refs) = refs[:count], refs[count], refs[count + 1 :]
    rows_touched = (place[0] + steps - 1) // place[1] - place[0] // place[1] + 1
    for distance, source, target in zip(distances, sources, (own_ref, *sent_refs)):
        block = (place[2] ^ distance) * steps + step - place[0] // place[1] * place[1]
        inside = jnp.logical_and(block >= 0, block < rows_touched * place[1])
        value = jnp.where(inside, source[0], 0.0)
        if distance == 0:
            target[0] = blocksum_ref[0] + value
        else:
            target[0] = value.astype(bf16)


def shares(place, rowsum, blocksum, distances):
    steps, size, depth = blocksum.shape
    group = None
    window = rowsum.reshape(-1, size, depth)

    def source(distance):
        def index(b, place):
            block = (place[2] ^ distance) * steps + b - place[0] // place[1] * place[1]
            return jnp.clip(block, 0, window.shape[0] - 1), 0, 0

        return pl.BlockSpec((1, size, depth), index)

    block = pl.BlockSpec((1, size, depth), local)
    return pl.pallas_call(
        functools.partial(shares_kernel, distances, group),
        grid_spec=pltpu.PrefetchScalarGridSpec(
            num_scalar_prefetch=1,
            grid=(steps,),
            in_specs=[source(d) for d in distances] + [block],
            out_specs=[block for _ in distances],
        ),
        out_shape=[
            jax.ShapeDtypeStruct(blocksum.shape, bf16 if d else f32) for d in distances
        ],
        compiler_params=limit(12),
        name="shares",
    )(place, *[window for _ in distances], blocksum)


def row_chunks(count, body):
    chunk = 200 if count % 200 == 0 else 16

    @pl.loop(0, count // chunk)
    def _(i):
        body(pl.ds(pl.multiple_of(i * chunk, 8), chunk))

    if count % chunk:
        body(pl.ds(count // chunk * chunk, count % chunk))


def phi_parts(value):
    bell = jnp.exp2(value * value * (-0.5 / math.log(2.0)))
    t = 1.0 / (1.0 + jnp.abs(value) * (0.3275911 * 0.5**0.5))
    poly = t * (
        0.127414796
        + t * (-0.142248368 + t * (0.7107068705 + t * (-0.7265760135 + t * 0.5307027145)))
    )
    half = poly * bell
    return jnp.where(value >= 0, 1.0 - half, half), bell * (2.0 * math.pi) ** -0.5


def chunk_stats(value):
    centre = value - jnp.mean(value, axis=-1, keepdims=True)
    inverse = lax.rsqrt(jnp.mean(centre * centre, axis=-1, keepdims=True) + norm_eps)
    return centre * inverse, inverse


def fetch_slot(order, step, sources, buffers, sems):
    for which, (refs, buffer) in enumerate(zip(sources, buffers)):
        for position, slot in enumerate(order):

            @pl.when(step == position)
            def _():
                pltpu.make_async_copy(refs[slot], buffer.at[step % 2], sems.at[which, step % 2]).start()


def await_slot(step, sources, buffers, sems):
    for which, (refs, buffer) in enumerate(zip(sources, buffers)):
        pltpu.make_async_copy(refs[0], buffer.at[step % 2], sems.at[which, step % 2]).wait()


def stream_slots(order, sources, buffers, sems):
    step = pl.program_id(0)

    @pl.when(step == 0)
    def _():
        fetch_slot(order, step, sources, buffers, sems)

    @pl.when(step + 1 < pl.num_programs(0))
    def _():
        fetch_slot(order, step + 1, sources, buffers, sems)

    await_slot(step, sources, buffers, sems)


def fetch_slot(order, step, sources, buffers, sems, firsts):
    for which, (refs, buffer, first) in enumerate(zip(sources, buffers, firsts)):
        for position, slot in enumerate(order):

            @pl.when(step == position)
            def _():
                pltpu.make_async_copy(
                    refs[slot].at[pl.ds(first, buffer.shape[1])],
                    buffer.at[step % 2],
                    sems.at[which, step % 2],
                ).start()


def stream_slots(order, sources, buffers, sems, firsts):
    step = pl.program_id(0)

    @pl.when(step == 0)
    def _():
        fetch_slot(order, step, sources, buffers, sems, firsts)

    @pl.when(step + 1 < pl.num_programs(0))
    def _():
        fetch_slot(order, step + 1, sources, buffers, sems, firsts)

    for which, (refs, buffer, first) in enumerate(zip(sources, buffers, firsts)):
        pltpu.make_async_copy(
            refs[0].at[pl.ds(first, buffer.shape[1])], buffer.at[step % 2], sems.at[which, step % 2]
        ).wait()


def ffn_kernel(
    group, place, frames_ref, cot_ref, ids_ref, vec_ref, *refs,
):
    held = len(refs) - 15 - 3 * group
    context_refs, refs = refs[:held], refs[held:]
    weight_refs, refs = refs[:group], refs[group:]
    up_refs, down_refs = refs[:group], refs[group : 2 * group]
    (
        layer_ref, low_ref, normal_ref, inverse_ref, gradffn_ref, small_ref,
        active_ref, slope_ref, up_buf, down_buf, out_buf, bias_buf, mixed, sems, out_sems,
    ) = refs[2 * group :]
    turns = group // held
    step = pl.program_id(0)
    count, depth = mixed.shape
    hidden = active_ref.shape[2]
    width = out_buf.shape[1]
    out_bias, gain_one, shift_one = vec_ref[0:1], vec_ref[1:2], vec_ref[2:3]
    outer_bias, gain_two, shift_two = vec_ref[3:4], vec_ref[4:5], vec_ref[5:6]

    def out_copies(slot):
        return [
            pltpu.make_async_copy(
                weight_refs[slot].at[pl.ds(first, target.shape[1])], target.at[slot], out_sems.at[which, slot]
            )
            for which, (target, first) in enumerate(
                ((out_buf, 3 * width + BIAS_ROWS), (bias_buf, 3 * width))
            )
        ]

    @pl.when(step == 0)
    def _():
        for slot in range(group):
            for copy in out_copies(slot):
                copy.start()

    stream_slots(tuple(range(group)), (up_refs, down_refs), (up_buf, down_buf), sems, (0, 0))

    @pl.when(step == 0)
    def _():
        for slot in range(group):
            for copy in out_copies(slot):
                copy.wait()
        _, blocks, _, size = context_refs[0].shape
        for block in range(blocks):
            total = dot(context_refs[0][0, block], out_buf[0], 0, 0)
            for slot in range(1, group):
                total += dot(context_refs[slot // turns][slot % turns, block], out_buf[slot], 0, 0)
            mixed[block * size : (block + 1) * size] = total

        def first(rows):
            hidden_one = frames_ref[0, rows].astype(f32) + mixed[rows] + out_bias
            normal, inverse = chunk_stats(hidden_one)
            normal_ref[rows] = normal.astype(bf16)
            inverse_ref[rows] = inverse
            normed = normal * gain_one + shift_one
            low_ref[rows] = normed.astype(bf16)
            mixed[rows] = normed + outer_bias

        row_chunks(count, first)

    biases = bias_buf[step].astype(f32)
    bias = jnp.concatenate([bias_row(biases, 2), bias_row(biases, 3)[:, 0 : hidden - depth]], axis=1)
    up_now, down_now = up_buf[step % 2], down_buf[step % 2]

    def gelu(rows):
        value = dot(low_ref[rows], up_now, 1, 1) + bias
        whole_part, bell = phi_parts(value)
        active = (value * whole_part).astype(bf16)
        active_ref[0, rows] = active
        slope_ref[0, rows] = (whole_part + value * bell).astype(bf16)
        mixed[rows] += dot(active, down_now, 1, 0)

    gelu(slice(None))

    @pl.when(step == pl.num_programs(0) - 1)
    def _():
        small_ref[...] = jnp.zeros_like(small_ref)

        def last(rows):
            normal, inverse = chunk_stats(mixed[rows])
            live = (ids_ref[rows] >= 0).astype(f32)
            layer_ref[rows] = ((normal * gain_two + shift_two) * live).astype(bf16)
            grad = cot_ref[0, rows].astype(f32) * live
            small_ref[0:1] += jnp.sum(grad * normal, axis=0, keepdims=True)
            small_ref[1:2] += jnp.sum(grad, axis=0, keepdims=True)
            scaled = grad * gain_two
            back = inverse * (
                scaled
                - jnp.mean(scaled, axis=-1, keepdims=True)
                - normal * jnp.mean(scaled * normal, axis=-1, keepdims=True)
            )
            small_ref[2:3] += jnp.sum(back, axis=0, keepdims=True)
            gradffn_ref[rows] = back.astype(bf16)

        row_chunks(count, last)


def up_back_kernel(
    order, last, group, low_ref, normal_ref, inverse_ref, before_ref, gradffn_ref, slope_ref,
    gain_ref, *refs,
):
    up_refs, down_refs, rest = refs[:group], refs[group : 2 * group], refs[2 * group :]
    if last:
        upgrad_ref, small_ref, gradone_ref, gradattn_ref, *rest = rest
    else:
        upgrad_ref, normed_grad, *rest = rest
    up_buf, down_buf, inner, sems, *rest = rest
    if last:
        normed_grad = rest[0]
    step = pl.program_id(0)
    count, hidden = inner.shape
    depth = low_ref.shape[1]
    stream_slots(order, (up_refs, down_refs), (up_buf, down_buf), sems, (0, 0))

    @pl.when(step == 0)
    def _():
        normed_grad[...] = before_ref[...] if last else gradffn_ref[...].astype(f32)

    grad_active = dot(gradffn_ref[...], down_buf[step % 2], 1, 1)
    inner[...] = (grad_active * slope_ref[0].astype(f32)).astype(bf16)
    upgrad_ref[0, 0:hidden] = dot(inner[...], low_ref[...], 0, 0).astype(bf16)
    ones = jnp.ones((8, count), bf16)
    bias = dot(ones, inner[...], 1, 0)
    row = lax.broadcasted_iota(jnp.int32, (upgrad_ref.shape[1] - hidden, depth), 0)
    extra = jnp.where(row == 0, bias[0:1, 0:depth], 0.0)
    rest_lanes = jnp.pad(bias[0:1, depth:hidden], ((0, 0), (0, 2 * depth - hidden)))
    upgrad_ref[0, hidden:] = jnp.where(row == 1, rest_lanes, extra).astype(bf16)
    normed_grad[...] += dot(inner[...], up_buf[step % 2], 1, 0)

    if last:

        @pl.when(step == pl.num_programs(0) - 1)
        def _():
            small_ref[...] = jnp.zeros_like(small_ref)
            gain = gain_ref[...]

            def last_rows(rows):
                grad, normal = normed_grad[rows], normal_ref[rows].astype(f32)
                small_ref[0:1] += jnp.sum(grad * normal, axis=0, keepdims=True)
                small_ref[1:2] += jnp.sum(grad, axis=0, keepdims=True)
                scaled = grad * gain
                back = inverse_ref[rows] * (
                    scaled
                    - jnp.mean(scaled, axis=-1, keepdims=True)
                    - normal * jnp.mean(scaled * normal, axis=-1, keepdims=True)
                )
                small_ref[2:3] += jnp.sum(back, axis=0, keepdims=True)
                gradone_ref[rows] = back
                gradattn_ref[rows] = back.astype(bf16)

            row_chunks(count, last_rows)


def down_back_kernel(
    order, group, active_ref, gradffn_ref, gradattn_ref, small_ref, smalltwo_ref, *refs
):
    context_refs, result_ref = refs[:-1], refs[-1]
    turns = group // len(context_refs)
    step = pl.program_id(0)
    hidden = active_ref.shape[2]
    depth = gradffn_ref.shape[1]
    _, blocks, width, size = context_refs[0].shape
    result_ref[0, 0:hidden] = dot(active_ref[0], gradffn_ref[...], 0, 0).astype(bf16)
    for position, slot in enumerate(order):

        @pl.when(step == position)
        def _():
            context = context_refs[slot // turns].at[slot % turns]
            total = dot(context[0], gradattn_ref[0:size], 1, 0)
            for block in range(1, blocks):
                total += dot(context[block], gradattn_ref[block * size : (block + 1) * size], 1, 0)
            result_ref[0, hidden : hidden + width] = total.astype(bf16)

    row = lax.broadcasted_iota(jnp.int32, (HIDDEN_EXTRA, depth), 0)
    extra = jnp.zeros((HIDDEN_EXTRA, depth), f32)
    for index in range(3):
        extra = jnp.where(row == index, small_ref[index : index + 1], extra)
        extra = jnp.where(row == 3 + index, smalltwo_ref[index : index + 1], extra)
    result_ref[0, hidden + width :] = extra.astype(bf16)


def ffn(place, frames, cotangent, ids, vectors, contexts, weights, up, down):
    group = len(up)
    count, depth = frames.shape[1:]
    hidden = down[0].shape[0]
    width = contexts[0].shape[2]
    own = pl.BlockSpec((1, count, depth), lambda s, place: (place[2], 0, 0))
    per_slot = pl.BlockSpec((1, count, hidden), lambda s, place: (s, 0, 0))
    spec = pltpu.PrefetchScalarGridSpec(
        num_scalar_prefetch=1,
        grid=(group,),
        in_specs=[own, own, whole(ids.shape), whole(vectors.shape)]
        + [whole(contexts[0].shape)] * len(contexts)
        + [ANYWHERE] * (3 * group),
        out_specs=[
            whole((count, depth)), whole((count, depth)), whole((count, depth)), whole((count, 1)),
            whole((count, depth)), whole((8, depth)), per_slot, per_slot,
        ],
        scratch_shapes=[
            pltpu.VMEM((2, hidden, depth), bf16),
            pltpu.VMEM((2, hidden, depth), bf16),
            pltpu.VMEM((group, width, depth), bf16),
            pltpu.VMEM((group, BIAS_ROWS, depth), bf16),
            pltpu.VMEM((count, depth), f32),
            pltpu.SemaphoreType.DMA((2, 2)),
            pltpu.SemaphoreType.DMA((2, group)),
        ],
    )
    shape = jax.ShapeDtypeStruct
    return pl.pallas_call(
        functools.partial(ffn_kernel, group),
        grid_spec=spec,
        out_shape=[
            shape((count, depth), bf16), shape((count, depth), bf16), shape((count, depth), bf16),
            shape((count, 1), f32), shape((count, depth), bf16), shape((8, depth), f32), shape((group, count, hidden), bf16),
            shape((group, count, hidden), bf16),
        ],
        cost_estimate=cost(2**34),
        compiler_params=limit(28),
        name="ffn",
    )(
        place, far_away(frames), far_away(cotangent), ids, vectors, *map(far_away, contexts), *map(far_away, weights),
        *up, *down,
    )


def in_order(order):
    def slot_of(s):
        result = jnp.int32(order[-1])
        for position in reversed(range(len(order) - 1)):
            result = jnp.where(s == position, order[position], result)
        return result

    return slot_of


def everything(shape):
    return pl.BlockSpec(shape, lambda s: (0,) * len(shape))


def up_back(order, last, low, normal, inverse, before, gradffn, slope, gain, up, down):
    group = len(up)
    count, depth = low.shape
    hidden = slope.shape[2]
    slot_of = in_order(order)
    per_slot = pl.BlockSpec((1, count, hidden), lambda s: (slot_of(s), 0, 0))
    rows = hidden + HIDDEN_EXTRA
    shape = jax.ShapeDtypeStruct
    wide = shape((count, depth), f32)
    tail = [shape((8, depth), f32), wide, shape((count, depth), bf16)] if last else [wide]
    return pl.pallas_call(
        functools.partial(up_back_kernel, order, last, group),
        grid=(len(order),),
        in_specs=[
            everything(v.shape) for v in (low, normal, inverse, before, gradffn)
        ]
        + [per_slot, everything(gain.shape)]
        + [ANYWHERE] * (2 * group),
        out_specs=[pl.BlockSpec((1, rows, depth), lambda s: (s, 0, 0))]
        + [everything(t.shape) for t in tail],
        out_shape=[shape((len(order), rows, depth), bf16)] + tail,
        scratch_shapes=[
            pltpu.VMEM((2, hidden, depth), bf16),
            pltpu.VMEM((2, hidden, depth), bf16),
            pltpu.VMEM((count, hidden), bf16),
            pltpu.SemaphoreType.DMA((2, 2)),
        ]
        + ([pltpu.VMEM((count, depth), f32)] if last else []),
        cost_estimate=cost(2**33),
        compiler_params=limit(26),
        name="up_back",
    )(low, normal, inverse, before, gradffn, slope, gain, *up, *down)


def down_back(order, active, gradffn, gradattn, smalls, contexts):
    count, hidden = active.shape[1:]
    depth = gradffn.shape[1]
    width = contexts[0].shape[2]
    slot_of = in_order(order)
    rows = hidden + width + HIDDEN_EXTRA
    return pl.pallas_call(
        functools.partial(down_back_kernel, order, active.shape[0]),
        grid=(len(order),),
        in_specs=[pl.BlockSpec((1, count, hidden), lambda s: (slot_of(s), 0, 0))]
        + [everything(v.shape) for v in (gradffn, gradattn, *smalls, *contexts)],
        out_specs=pl.BlockSpec((1, rows, depth), lambda s: (s, 0, 0)),
        out_shape=jax.ShapeDtypeStruct((len(order), rows, depth), bf16),
        cost_estimate=cost(2**32),
        compiler_params=limit(20),
        name="down_back",
    )(active, gradffn, gradattn, *smalls, *contexts)


def swap(value, axis, distance):
    size = lax.axis_size(axis)
    return lax.ppermute(value, axis, [(i, i ^ distance) for i in range(size)])


def add_low(a, b):
    return (a.astype(f32) + b.astype(f32)).astype(bf16)


def add_three(a, b, c):
    return (a.astype(f32) + b.astype(f32) + c.astype(f32)).astype(bf16)


def hold(value, *others):
    return lax.optimization_barrier((value,) + tuple(others))[0]


def row_distances(size):
    distance, result = 1, []
    while distance < size:
        result.append(distance)
        distance *= 2
    return result


def join_rows(value, arrived, distance):
    upper = (lax.axis_index("rows") // distance) % 2 == 1
    return jnp.concatenate(
        [jnp.where(upper, arrived, value), jnp.where(upper, value, arrived)], axis=0
    )


def far_swap(value, far):
    return swap(value, "rows", (far & 1) * 2 + (far >> 1))


def own_quarter():
    here = lax.axis_index("rows")
    return here % 2 * 2 + here // 2 % 2


def quarters_of(value, axis=0):
    rows = value.shape[axis] // QUARTERS
    return [
        lax.dynamic_slice_in_dim(value, (own_quarter() ^ far) * rows, rows, axis)
        for far in range(QUARTERS)
    ]


def send_quarters(quarters):
    return [far_swap(quarters[far], far) for far in range(1, QUARTERS)]


def add_quarters(quarters, came):
    total = quarters[0].astype(f32)
    for value in came:
        total = total + value.astype(f32)
    return total.astype(bf16)


def join_pieces(pieces):
    near = [join_rows(pieces[i], pieces[i + 1], 2) for i in (0, 2)]
    return join_rows(near[0], near[1], 1)


def across(value, came, distances):
    value = add_low(value, came)
    for distance in distances:
        value = add_low(value, swap(value, "rows", distance))
    return value


def gather_slots(value):
    slots = {0: value}
    distance = lax.axis_size("heads") // 2
    while distance >= 1:
        for slot in list(slots):
            slots[slot ^ distance] = swap(slots[slot], "heads", distance)
        distance //= 2
    return [slots[slot] for slot in range(len(slots))]


def per_device(
    frames, segment_ids, cotangent, query_weight, query_bias, key_weight, value_weight, value_bias,
    output_weight, output_bias, first_gain, first_shift, inner_weight, inner_bias, outer_weight,
    outer_bias, second_gain, second_shift,
):
    group = lax.axis_size("heads")
    position = lax.axis_index("heads")
    row_count, row_length, depth = frames.shape
    own_len = row_count * row_length // group
    size = math.gcd(row_length, own_len)
    steps = own_len // size
    per_row = row_length // size
    width = query_weight.shape[1]
    heads_here = width // HEAD_DIM
    per_head = FF_LIVE // HEADS_LIVE
    hidden_slots = inner_weight.shape[1]
    hidden_cap = min(hidden_slots, (HEADS_LIVE + group - 1) // group * per_head)

    def live_of(index):
        return HEADS_LIVE // group + (index < HEADS_LIVE % group).astype(jnp.int32)

    rest = row_distances(lax.axis_size("rows"))[2:]
    piece_rows = hidden_cap // QUARTERS
    place = jnp.stack(
        [position * steps, jnp.int32(per_row), position]
        + [live_of(position ^ slot) for slot in range(group)]
        + [own_quarter() * piece_rows, own_quarter()]
    )
    blocks = frames.reshape(row_count * per_row, size, depth)
    weight_own, piece = prepare(
        place, query_weight.T, key_weight.T, value_weight.T, query_bias, value_bias,
        inner_bias, output_weight, outer_weight, piece_rows,
    )
    weight = {0: weight_own, 1: swap(weight_own, "heads", 1), 2: swap(weight_own, "heads", 2)}
    piece = swap(piece, "heads", 2)
    up_own, down_own, keyf, queryf = prepare_wide(
        place, inner_weight, outer_weight, segment_ids,
        segment_ids.reshape(row_count * per_row, 1, size), hidden_cap,
    )
    up = {0: up_own, 1: swap(up_own, "heads", 1)}
    down = {0: down_own, 1: swap(down_own, "heads", 1)}
    half = group // 2

    def forward(first, *waits):
        return attend(
            first, place, hold(blocks, *waits), frames,
            [weight[slot] for slot in range(first, first + half)], keyf, queryf, steps, width,
        )

    saved = [forward(0)]
    done = saved[0][0]
    weight[2], piece, done = lax.optimization_barrier((weight[2], piece, done))
    weight[3] = swap(weight[2], "heads", 1)
    up[2] = swap(hold(up_own, weight[2]), "heads", 2)
    piece = hold(piece, weight[2])
    pieces = [piece] + send_quarters([piece] * QUARTERS)
    saved.append(forward(half, done))
    down[2] = join_pieces(hold(pieces, saved[1][0]))
    up[3] = swap(up[2], "heads", 1)
    down[3] = swap(down[2], "heads", 1)
    up = [up[slot] for slot in range(group)]
    down = [down[slot] for slot in range(group)]
    contexts = [kept[3] for kept in saved]

    vectors = jnp.stack(
        [output_bias, first_gain, first_shift, outer_bias, second_gain, second_shift]
    )
    whole_frames = frames.reshape(group, own_len, depth)
    whole_cot = cotangent.reshape(group, own_len, depth)
    flat_ids = segment_ids.reshape(row_count * row_length)
    ids_own = lax.dynamic_slice_in_dim(flat_ids, position * own_len, own_len)[:, None]
    layer_own, normed_low, normal_one, inverse_one, grad_ffn, small_two, actives, slopes = ffn(
        place, whole_frames, whole_cot, ids_own, vectors, contexts,
        [weight[slot] for slot in range(group)], up, down,
    )
    layer = {0: layer_own, 1: swap(layer_own, "heads", 1), 2: swap(layer_own, "heads", 2)}
    known = (normed_low, normal_one, inverse_one)
    gain = first_gain[None]
    up_send, grad_part = up_back((1, 3), False, *known, inverse_one, grad_ffn, slopes, gain, up, down)
    up_came = swap(up_send, "heads", 1)
    layer[1] = hold(layer[1], grad_part)
    up_keep, small_one, grad_hidden_one, grad_attn = up_back(
        (0, 2), True, *known, grad_part, grad_ffn, slopes, gain, up, down
    )
    barrier = lax.optimization_barrier
    up_quarters = quarters_of(add_low(up_keep, up_came), 1)
    up_came = send_quarters(up_quarters)

    smalls = (small_one, small_two)
    down_send = down_back((1, 3), actives, hold(grad_ffn, up_quarters), grad_attn, smalls, contexts)
    down_came = swap(down_send, "heads", 1)
    down_keep = down_back((0, 2), actives, hold(grad_ffn, down_send), grad_attn, smalls, contexts)
    down_came = hold(down_came, down_keep)
    grad_attn = grad_attn.reshape(steps, size, depth)
    block_sum = grad_hidden_one.reshape(steps, size, depth)
    row_sum = jnp.zeros((8, 128), f32)
    grads = {}

    def back(slot, first, block_sum, row_sum, *waits):
        return attend_back(
            slot, first, place, blocks, frames, weight[slot], saved[slot // half], grad_attn,
            hold(block_sum, *waits), row_sum,
        )

    layer[2] = hold(layer[2], down_keep)
    layer[3] = swap(layer[2], "heads", 1)
    down_two = add_low(down_keep[1], down_came[1])
    cut = down_two.shape[0] // 2
    down_first = swap(hold(down_two[:cut], layer[2]), "heads", 2)
    grads[3], block_sum, row_sum = back(3, True, block_sum, row_sum, layer[2], down_two)

    block_sum, up_came, down_first, layer[3], grads[3] = barrier(
        (block_sum, up_came, down_first, layer[3], grads[3])
    )
    down_second = swap(hold(down_two[cut:], down_first), "heads", 2)
    grads_came = swap(grads[3], "heads", 1)
    up_pair = add_quarters(up_quarters, up_came)
    up_came = swap(up_pair[1], "heads", 2)
    grads[2], block_sum, row_sum = back(2, False, block_sum, row_sum, up_pair)

    block_sum, up_came, down_second, grads_came, grads[2] = barrier(
        (block_sum, up_came, down_second, grads_came, grads[2])
    )
    attn_two = add_low(grads[2], grads_came)
    attn_rows = attn_two.shape[0] // 2
    attn_first = swap(attn_two[:attn_rows], "heads", 2)
    up_piece = add_low(up_pair[0], up_came)
    up_came = swap(up_piece, "rows", rest[0])
    down_far = jnp.concatenate([down_first, down_second])
    down_quarters = quarters_of(add_three(down_keep[0], down_came[0], down_far))
    down_came = send_quarters(down_quarters)
    grads[1], block_sum, row_sum = back(
        1, False, block_sum, row_sum, attn_two, up_piece, down_quarters
    )

    block_sum, up_came, down_came, attn_first, grads[1] = barrier(
        (block_sum, up_came, down_came, attn_first, grads[1])
    )
    grads_came = swap(grads[1], "heads", 1)
    up_piece = across(up_piece, up_came, rest[1:])
    attn_second = swap(hold(attn_two[attn_rows:], attn_first), "heads", 2)
    up_came = swap(up_piece, "rows", 2)
    down_piece = add_quarters(down_quarters, down_came)
    down_came = swap(down_piece, "rows", rest[0])
    grads[0], block_sum, row_sum = back(0, False, block_sum, row_sum, up_piece, down_piece)
    block_sum, up_came, down_came, attn_second, grads_came, grads[0] = barrier(
        (block_sum, up_came, down_came, attn_second, grads_came, grads[0])
    )

    reach, pairs = [0], {}
    for distance in range(1, group):
        pairs[distance] = []
        for i in range(group):
            j = i ^ distance
            rows_i = range(i * steps // per_row, ((i + 1) * steps - 1) // per_row + 1)
            rows_j = range(j * steps // per_row, ((j + 1) * steps - 1) // per_row + 1)
            if set(rows_i) & set(rows_j):
                pairs[distance].append((i, j))
        if pairs[distance]:
            reach.append(distance)
    own_grad, *owed = shares(place, row_sum, block_sum, tuple(reach))
    attn_two = jnp.concatenate([attn_first, attn_second])
    attn_quarters = quarters_of(add_three(hold(grads[0], owed), grads_came, attn_two))
    owed = [
        lax.ppermute(sent, "heads", pairs[distance]) for distance, sent in zip(reach[1:], owed)
    ]
    attn_came = send_quarters(attn_quarters)
    up_half = join_rows(up_piece, hold(up_came, own_grad), 2)
    down_piece = across(down_piece, hold(down_came, own_grad), rest[1:])
    layer[0] = hold(layer[0], own_grad)
    layer_out = assemble(
        place, [(slot, 0, layer[slot]) for slot in range(group)], own_len, row_count * row_length
    ).reshape(frames.shape)
    attn_came, owed, layer_out, up_half, down_piece = barrier(
        (attn_came, owed, layer_out, up_half, down_piece)
    )

    attn_piece = add_quarters(attn_quarters, attn_came)
    attn_came = swap(attn_piece, "rows", rest[0])
    up_came = swap(hold(up_half, attn_piece), "rows", 1)
    down_came = swap(hold(down_piece, attn_piece), "rows", 2)
    for came in owed:
        own_grad = own_grad + hold(came, attn_piece).astype(f32)
    own_grad = own_grad.astype(bf16).reshape(own_len, depth)
    cut = own_len // 2 // 8 * 8
    first_cut = swap(own_grad[:cut], "heads", 2)
    mate = swap(own_grad, "heads", 1)
    attn_came, first_cut, mate, up_came, down_came = barrier(
        (attn_came, first_cut, mate, up_came, down_came)
    )

    attn_piece = across(attn_piece, attn_came, rest[1:])
    attn_came = send_quarters([attn_piece] * QUARTERS)
    second_cut = swap(hold(own_grad[cut:], attn_piece), "heads", 2)
    down_half = join_rows(down_piece, down_came, 2)
    down_came = swap(down_half, "rows", 1)
    up_done = finish(
        finish_up_kernel, place, [hold(up_half, attn_piece), up_came],
        [(depth, hidden_slots), (8, depth)], "finish_up",
    )
    second_cut, up_done, attn_came = barrier((second_cut, up_done, attn_came))
    second_mate = swap(second_cut, "heads", 1)
    first_mate = swap(hold(first_cut, second_cut), "heads", 1)
    attn_done = finish(
        finish_attn_kernel, place, [attn_piece, *attn_came],
        [(width, depth)] * 3 + [(8, depth)], "finish_attn",
    )
    frames_grad = assemble(
        place,
        [
            (0, 0, own_grad), (1, 0, mate), (2, 0, first_cut), (2, cut, second_cut),
            (3, 0, first_mate), (3, cut, second_mate),
        ],
        own_len, row_count * row_length,
    ).reshape(frames.shape)
    down_done = finish(
        functools.partial(finish_down_kernel, per_head), place,
        [down_half, hold(down_came, frames_grad)],
        [(hidden_slots, depth), (width, depth), (8, depth)], "finish_down",
    )

    innerbias = jnp.concatenate([up_done[1][0], up_done[1][1, : hidden_cap - depth]])
    innerbias_full = jnp.pad(innerbias, ((0, hidden_slots - hidden_cap),))
    extra = attn_done[3]
    small = down_done[2]
    return (
        layer_out,
        frames_grad,
        attn_done[0].T,
        extra[0, :width],
        attn_done[1].T,
        attn_done[2].T,
        extra[1, :width],
        down_done[1],
        small[2],
        small[0],
        small[1],
        up_done[0],
        innerbias_full,
        down_done[0],
        small[5],
        small[3],
        small[4],
    )


def solution(mesh):
    in_specs = (
        P("rows", None, None), P("rows", None), P("rows", None, None), P(None, "heads"), P("heads"),
        P(None, "heads"), P(None, "heads"), P("heads"), P("heads", None), P(), P(), P(),
        P(None, "heads"), P("heads"), P("heads", None), P(), P(), P(),
    )
    out_specs = (
        P("rows", None, None), P("rows", None, None), P(None, "heads"), P("heads"), P(None, "heads"),
        P(None, "heads"), P("heads"), P("heads", None), P(), P(), P(), P(None, "heads"), P("heads"),
        P("heads", None), P(), P(), P(),
    )
    return jax.shard_map(
        per_device, mesh=mesh, in_specs=in_specs, out_specs=out_specs, check_vma=False
    )
```

```python
import functools
import math

import jax
import jax.numpy as jnp
from jax import lax
from jax.experimental import pallas as pl
from jax.experimental.pallas import tpu as pltpu
from jax.sharding import PartitionSpec as P

HEADS_LIVE = 10
HEAD_SLOTS = 12
HEAD_DIM = 64
FF_LIVE = 2240
PAD_HEAD = 128
SEGMENTS = 5
MASK_STEP = -(2.0**30)
norm_eps = 1e-05
f32 = jnp.float32
bf16 = jnp.bfloat16


def dot(a, b, ca, cb):
    return lax.dot_general(a, b, (((ca,), (cb,)), ((), ())), preferred_element_type=f32)


def three_parts(value):
    high = value.astype(bf16).astype(f32)
    middle = (value - high).astype(bf16).astype(f32)
    return high, middle, value - high - middle


def live_heads(live, heads, one_head):
    least = HEADS_LIVE * heads // HEAD_SLOTS
    for head in range(least):
        one_head(head)
    for head in range(least, heads):

        @pl.when(head < live)
        def _():
            one_head(head)


def feature_rows(base, value):
    high, middle, low = three_parts(-value)
    row = lax.broadcasted_iota(jnp.int32, base.shape, 0)
    base = jnp.where(row == SEGMENTS, high, base)
    base = jnp.where(row == SEGMENTS + 1, middle, base)
    return jnp.where(row == SEGMENTS + 2, low, base).astype(bf16)


def bias_row(rows, index):
    first = 3 * index
    return rows[first : first + 1] + rows[first + 1 : first + 2] + rows[first + 2 : first + 3]


def attend_kernel(
    first, place, block_ref, row_ref, keyf_ref, queryf_ref, *refs,
):
    pair = len(refs) - 5
    weight_refs, (query_ref, key_ref, value_ref, context_ref, weight_ref) = refs[:pair], refs[pair:]
    turn = pl.program_id(0)
    step = pl.program_id(1)
    per_row, live = place[1], place[3 + first + turn]
    row_now = (place[0] + step) // per_row
    row_before = (place[0] + step - 1) // per_row
    length = row_ref.shape[1]
    width = context_ref.shape[2]
    heads = width // HEAD_DIM

    for index, ref in enumerate(weight_refs):

        @pl.when(jnp.logical_and(step == 0, turn == index))
        def _():
            weight_ref[...] = ref[...]

    biases = weight_ref[3 * width :].astype(f32)

    @pl.when(jnp.logical_or(step == 0, row_now != row_before))
    def _():
        frames = row_ref[0]
        keys = dot(frames, weight_ref[width : 2 * width], 1, 1).astype(bf16)
        values = dot(frames, weight_ref[2 * width : 3 * width], 1, 1)
        values = (values + bias_row(biases, 1)[:, 0:width]).astype(bf16)
        features = keyf_ref[0]
        for head in range(heads):
            cut = slice(head * HEAD_DIM, (head + 1) * HEAD_DIM)
            key_ref[0, 0, head * length : (head + 1) * length] = jnp.concatenate(
                [keys[:, cut], features], axis=1
            )
            value_ref[0, 0, head * length : (head + 1) * length] = jnp.concatenate(
                [values[:, cut], features], axis=1
            )

    qbias = jnp.broadcast_to(bias_row(biases, 0)[:, 0:width], (8, width)).T[:, 0:1]
    queries = (dot(weight_ref[0:width], block_ref[0], 1, 1) + qbias).astype(bf16)
    queries = queries * jnp.asarray(HEAD_DIM**-0.5, bf16)
    for head in range(heads):
        query_ref[0, 0, head * PAD_HEAD : head * PAD_HEAD + HEAD_DIM] = queries[
            head * HEAD_DIM : (head + 1) * HEAD_DIM
        ]
        query_ref[0, 0, head * PAD_HEAD + HEAD_DIM : (head + 1) * PAD_HEAD] = queryf_ref[0]
    context_ref[...] = jnp.zeros_like(context_ref)

    def one_head(head):
        keys = key_ref[0, 0, pl.ds(head * length, length)]
        values = value_ref[0, 0, pl.ds(head * length, length)]
        start = head * PAD_HEAD
        scores = dot(keys, query_ref[0, 0, pl.ds(start, PAD_HEAD)], 1, 0)
        highest = jnp.max(scores, axis=0, keepdims=True)
        probs = jnp.exp(scores - highest).astype(bf16)
        mixed = dot(values, probs, 0, 0)
        total = mixed[HEAD_DIM + SEGMENTS : HEAD_DIM + SEGMENTS + 1]
        context = mixed[0:HEAD_DIM] / total
        context_ref[0, 0, pl.ds(head * HEAD_DIM, HEAD_DIM)] = context.astype(bf16)
        base = queryf_ref[0, 0:16].astype(f32)
        query_ref[0, 0, pl.ds(start + HEAD_DIM, 16)] = feature_rows(base, highest + jnp.log(total))

    live_heads(live, heads, one_head)


def attend_back_kernel(
    slot, first, place, block_ref, row_ref, weight_ref, query_ref, key_ref, value_ref,
    context_ref, grad_ref, blocksum_ref, rowsum_ref,
    gradw_ref, blockout_ref, rowout_ref,
    weight_acc, dkey, dvalue, picked, dcontext, dquery, bias_acc,
):
    step = pl.program_id(0)
    steps = pl.num_programs(0)
    per_row, live = place[1], place[3 + slot]
    row_now = (place[0] + step) // per_row
    row_before = (place[0] + step - 1) // per_row
    row_after = (place[0] + step + 1) // per_row
    length, depth = row_ref.shape[1:]
    width = context_ref.shape[2]
    heads = width // HEAD_DIM
    ones = jnp.ones((8, length), bf16)

    @pl.when(step == 0)
    def _():
        weight_acc[...] = jnp.zeros_like(weight_acc)
        bias_acc[...] = jnp.zeros_like(bias_acc)
        picked[...] = jnp.zeros_like(picked)

    @pl.when(jnp.logical_or(step == 0, row_now != row_before))
    def _():
        dkey[...] = jnp.zeros_like(dkey)
        dvalue[...] = jnp.zeros_like(dvalue)

    dcontext[...] = dot(weight_ref[3 * width + BIAS_ROWS :], grad_ref[0], 1, 1).astype(bf16)
    dquery[...] = jnp.zeros_like(dquery)

    def one_head(head):
        own = pl.ds(head * HEAD_DIM, HEAD_DIM)
        keys = key_ref[0, 0, pl.ds(head * length, length)]
        values = value_ref[0, 0, pl.ds(head * length, length)]
        queries = query_ref[0, 0, pl.ds(head * PAD_HEAD, PAD_HEAD)]
        grad = dcontext[own]
        inner = jnp.sum(grad.astype(f32) * context_ref[0, 0, own].astype(f32), axis=0, keepdims=True)
        extra = feature_rows(jnp.zeros((PAD_HEAD - HEAD_DIM, grad.shape[1]), f32), inner)
        probs = jnp.exp(dot(keys, queries, 1, 0))
        dprobs = dot(values, jnp.concatenate([grad, extra], axis=0), 1, 0)
        dscores = (probs * dprobs).astype(bf16)
        picked[0, pl.ds(head * width + head * HEAD_DIM, HEAD_DIM)] = grad
        picked[1, pl.ds(head * width + head * HEAD_DIM, HEAD_DIM)] = queries[0:HEAD_DIM]
        place_head = pl.ds(head * width, width)
        dvalue[...] += dot(probs.astype(bf16), picked[0, place_head], 1, 1)
        dkey[...] += dot(dscores, picked[1, place_head], 1, 1)
        dquery[own] = (dot(keys, dscores, 0, 0)[0:HEAD_DIM] * HEAD_DIM**-0.5).astype(bf16)

    live_heads(live, heads, one_head)
    weight_acc[0:width] += dot(dquery[...], block_ref[0], 1, 0)
    blockout_ref[0] = blocksum_ref[0] + dot(dquery[...], weight_ref[0:width], 0, 0)
    bias_acc[0:8] += dot(ones[:, 0 : dquery.shape[1]], dquery[...], 1, 1)

    @pl.when(jnp.logical_or(step == steps - 1, row_now != row_after))
    def _():
        keys_low = dkey[...].astype(bf16)
        values_low = dvalue[...].astype(bf16)
        weight_acc[width : 2 * width] += dot(keys_low, row_ref[0], 0, 0)
        weight_acc[2 * width : 3 * width] += dot(values_low, row_ref[0], 0, 0)
        back = dot(keys_low, weight_ref[width : 2 * width], 1, 0) + dot(
            values_low, weight_ref[2 * width : 3 * width], 1, 0
        )
        if first:
            rowout_ref[0] = back.astype(bf16)
        else:
            rowout_ref[0] = (rowsum_ref[0].astype(f32) + back).astype(bf16)
        bias_acc[8:16] += dot(ones, values_low, 1, 0)

    @pl.when(step == steps - 1)
    def _():
        gradw_ref[0 : 3 * width] = weight_acc[...].astype(bf16)
        row = lax.broadcasted_iota(jnp.int32, (gradw_ref.shape[0] - 3 * width, depth), 0)
        lanes = depth - width
        extra = jnp.where(row == 0, jnp.pad(bias_acc[0:1], ((0, 0), (0, lanes))), 0.0)
        extra = jnp.where(row == 1, jnp.pad(bias_acc[8:9], ((0, 0), (0, lanes))), extra)
        gradw_ref[3 * width :] = extra.astype(bf16)


def whole(shape):
    return pl.BlockSpec(shape, lambda b, place: (0,) * len(shape))


def limit(mib):
    return pltpu.CompilerParams(vmem_limit_bytes=mib * 2**20)


def cost(flops):
    return pl.CostEstimate(flops=2**40, bytes_accessed=2**33, transcendentals=0)


ANYWHERE = pl.BlockSpec(memory_space=pltpu.HBM)


def far_away(value):
    return pltpu.with_memory_space_constraint(value, pltpu.HBM)
BIAS_ROWS = 16
EXTRA_ROWS = 32
HIDDEN_EXTRA = 32


def row_of(b, place):
    return (place[0] + b) // place[1], 0, 0


def rel_row(b, place):
    return (place[0] + b) // place[1] - place[0] // place[1], 0, 0


def block_of(b, place):
    return place[0] + b, 0, 0


def local(b, place):
    return b, 0, 0


def attend(first, place, blocks, rows, weights, keyf, queryf, steps, width):
    size, depth = blocks.shape[1:]
    count, length, _ = rows.shape
    weight_shape = (3 * width + BIAS_ROWS, depth)
    heads = width // HEAD_DIM
    window = min(2, count)
    pair = len(weights)
    fixed = lambda shape: pl.BlockSpec(shape, lambda s, b, place: (0,) * len(shape))
    per_row = lambda shape: pl.BlockSpec((1,) + shape, lambda s, b, place: row_of(b, place))
    per_block = lambda shape: pl.BlockSpec((1,) + shape, lambda s, b, place: block_of(b, place))
    out_row = pl.BlockSpec(
        (1, 1, heads * length, PAD_HEAD), lambda s, b, place: (s,) + rel_row(b, place)
    )
    out_block = lambda rows: pl.BlockSpec((1, 1, rows, size), lambda s, b, place: (s, b, 0, 0))
    spec = pltpu.PrefetchScalarGridSpec(
        num_scalar_prefetch=1,
        grid=(pair, steps),
        in_specs=[
            per_block((size, depth)), per_row((length, depth)), per_row(keyf.shape[1:]),
            per_block(queryf.shape[1:]),
        ]
        + [fixed(weight_shape)] * pair,
        out_specs=[out_block(heads * PAD_HEAD), out_row, out_row, out_block(width)],
        scratch_shapes=[pltpu.VMEM(weight_shape, bf16)],
    )
    return pl.pallas_call(
        functools.partial(attend_kernel, first),
        grid_spec=spec,
        out_shape=[
            jax.ShapeDtypeStruct((pair, steps, heads * PAD_HEAD, size), bf16),
            jax.ShapeDtypeStruct((pair, window, heads * length, PAD_HEAD), bf16),
            jax.ShapeDtypeStruct((pair, window, heads * length, PAD_HEAD), bf16),
            jax.ShapeDtypeStruct((pair, steps, width, size), bf16),
        ],
        cost_estimate=cost(2**33),
        compiler_params=limit(FORWARD_LIMIT),
        name="attend",
    )(place, blocks, rows, keyf, queryf, *map(far_away, weights))


FORWARD_LIMIT = 60


def attend_back(slot, first, place, blocks, rows, weight, saved, grad, blocksum, rowsum):
    query, key, value, context = saved
    steps, size, depth = blocksum.shape
    count, length, _ = rows.shape
    width = context.shape[2]
    heads = width // HEAD_DIM
    turn = slot % query.shape[0]
    pinned = query.shape[0]
    saved_block = lambda v: pl.BlockSpec(
        (1, 1) + v.shape[2:], lambda b, place: (turn,) + local(b, place)
    )
    saved_row = lambda v: pl.BlockSpec(
        (1, 1) + v.shape[2:], lambda b, place: (turn,) + rel_row(b, place)
    )
    row_spec = pl.BlockSpec((1, length, depth), rel_row)
    near = far_away if slot >= pinned else lambda value: value
    spec = pltpu.PrefetchScalarGridSpec(
        num_scalar_prefetch=1,
        grid=(steps,),
        in_specs=[
            pl.BlockSpec((1, size, depth), block_of),
            pl.BlockSpec((1, length, depth), row_of),
            whole((4 * width + BIAS_ROWS, depth)),
            saved_block(query), saved_row(key), saved_row(value), saved_block(context),
            pl.BlockSpec((1, size, depth), local),
            pl.BlockSpec((1, size, depth), local),
            ANYWHERE if first else row_spec,
        ],
        out_specs=[
            whole((3 * width + EXTRA_ROWS, depth)),
            pl.BlockSpec((1, size, depth), local),
            row_spec,
        ],
        scratch_shapes=[
            pltpu.VMEM((3 * width, depth), f32),
            pltpu.VMEM((length, width), f32),
            pltpu.VMEM((length, width), f32),
            pltpu.VMEM((2, heads * width, size), bf16),
            pltpu.VMEM((width, size), bf16),
            pltpu.VMEM((width, size), bf16),
            pltpu.VMEM((16, width), f32),
        ],
    )
    return pl.pallas_call(
        functools.partial(attend_back_kernel, slot, first),
        grid_spec=spec,
        out_shape=[
            jax.ShapeDtypeStruct((3 * width + EXTRA_ROWS, depth), bf16),
            jax.ShapeDtypeStruct(blocksum.shape, f32),
            jax.ShapeDtypeStruct((min(2, count), length, depth), bf16),
        ],
        input_output_aliases={} if first else {10: 2},
        cost_estimate=cost(2**34),
        compiler_params=limit(26),
        name="attend_back",
    )(
        place, near(blocks), near(rows), near(weight), query, near(key), near(value), context, grad,
        blocksum, rowsum,
    )


def prepare_kernel(
    per_head, place, query_ref, key_ref, value_ref, qbias_ref, vbias_ref, ubias_ref, out_ref, down_ref,
    weight_ref, piece_ref,
):
    width, depth = query_ref.shape
    weight_ref[0:width] = query_ref[...]
    weight_ref[width : 2 * width] = key_ref[...]
    weight_ref[2 * width : 3 * width] = value_ref[...]
    lanes = ubias_ref.shape[0]
    row = lax.broadcasted_iota(jnp.int32, (BIAS_ROWS, depth), 0)
    result = jnp.zeros((BIAS_ROWS, depth), f32)
    qbias, vbias, ubias = qbias_ref[...][None], vbias_ref[...][None], ubias_ref[...][None]
    vectors = [
        jnp.pad(qbias, ((0, 0), (0, depth - width))),
        jnp.pad(vbias, ((0, 0), (0, depth - width))),
        ubias[:, 0:depth],
        jnp.pad(ubias[:, depth:lanes], ((0, 0), (0, 2 * depth - lanes))),
    ]
    for index, vector in enumerate(vectors):
        for offset, part in enumerate(three_parts(vector)):
            result = jnp.where(row == 3 * index + offset, part, result)
    first = 3 * width + BIAS_ROWS
    weight_ref[3 * width : first] = result.astype(bf16)
    row = lax.broadcasted_iota(jnp.int32, out_ref.shape, 0)
    kept = jnp.where(row < place[3] * HEAD_DIM, out_ref[...].astype(f32), 0.0)
    weight_ref[first : first + width] = kept.astype(bf16)
    piece = piece_ref.shape[0]
    start = place[3 + SLOT_COUNT]
    row = start + lax.broadcasted_iota(jnp.int32, (piece, depth), 0)
    kept = down_ref[pl.ds(pl.multiple_of(start, 8), piece)].astype(f32)
    piece_ref[...] = jnp.where(row < place[3] * per_head, kept, 0.0).astype(bf16)


SLOT_COUNT = 4


def prepare(place, query, key, value, qbias, vbias, ubias, out, down, piece):
    width, depth = query.shape
    shapes = [(4 * width + BIAS_ROWS, depth), (piece, depth)]
    args = (query, key, value, qbias, vbias, ubias, out, down)
    return pl.pallas_call(
        functools.partial(prepare_kernel, FF_LIVE // HEADS_LIVE),
        grid_spec=pltpu.PrefetchScalarGridSpec(
            num_scalar_prefetch=1,
            grid=(1,),
            in_specs=[whole(v.shape) for v in args],
            out_specs=[whole(shape) for shape in shapes],
        ),
        out_shape=[jax.ShapeDtypeStruct(shape, bf16) for shape in shapes],
        compiler_params=limit(60),
        name="prepare",
    )(place, *args)


def prepare_wide_kernel(
    per_head, place, up_ref, down_ref, ids_ref, blocks_ref,
    upout_ref, downout_ref, keyf_ref, queryf_ref,
):
    hidden = downout_ref.shape[0]
    upout_ref[...] = up_ref[...].T[0:hidden]
    row = lax.broadcasted_iota(jnp.int32, downout_ref.shape, 0)
    kept = jnp.where(row < place[3] * per_head, down_ref[0:hidden].astype(f32), 0.0)
    downout_ref[...] = kept.astype(bf16)
    rows, length = ids_ref.shape
    feature = lax.broadcasted_iota(jnp.int32, (HEAD_DIM, length), 0)
    for r in range(rows):
        same = jnp.where(feature == ids_ref[r : r + 1] + 1, 1.0, 0.0)
        ones = jnp.where(jnp.logical_and(feature >= SEGMENTS, feature < SEGMENTS + 3), 1.0, same)
        keyf_ref[r] = ones.T.astype(bf16)
    size = blocks_ref.shape[2]
    feature = lax.broadcasted_iota(jnp.int32, (HEAD_DIM, size), 0)
    for b in range(blocks_ref.shape[0]):
        other = jnp.logical_and(feature < SEGMENTS, feature != blocks_ref[b] + 1)
        queryf_ref[b] = jnp.where(other, MASK_STEP, 0.0).astype(bf16)


def prepare_wide(place, up, down, ids, id_blocks, hidden):
    depth = up.shape[0]
    rows, length = ids.shape
    shapes = [
        (hidden, depth), (hidden, depth), (rows, length, HEAD_DIM),
        (id_blocks.shape[0], HEAD_DIM, id_blocks.shape[2]),
    ]
    return pl.pallas_call(
        functools.partial(prepare_wide_kernel, FF_LIVE // HEADS_LIVE),
        grid_spec=pltpu.PrefetchScalarGridSpec(
            num_scalar_prefetch=1,
            grid=(1,),
            in_specs=[whole(v.shape) for v in (up, down, ids, id_blocks)],
            out_specs=[whole(shape) for shape in shapes],
        ),
        out_shape=[jax.ShapeDtypeStruct(shape, bf16) for shape in shapes],
        compiler_params=limit(60),
        name="prepare_wide",
    )(place, up, down, ids, id_blocks)


def assemble_kernel(parts, share, place, *refs):
    sources, (out_ref, *rest) = refs[: len(parts)], refs[len(parts) :]
    buffers, sems = rest[:-1], rest[-1]
    inward, outward = [], []
    for index, (slot, first) in enumerate(parts):
        rows = buffers[index].shape[0]
        start = pl.multiple_of((place[2] ^ slot) * share + first, 8)
        inward.append(pltpu.make_async_copy(sources[index], buffers[index], sems.at[0, index]))
        outward.append(
            pltpu.make_async_copy(buffers[index], out_ref.at[pl.ds(start, rows)], sems.at[1, index])
        )
    for copy in inward:
        copy.start()
    for into, out in zip(inward, outward):
        into.wait()
        out.start()
    for copy in outward:
        copy.wait()


def assemble(place, pieces, share, total):
    depth = pieces[0][2].shape[1]
    arrays = [piece[2] for piece in pieces]
    parts = tuple(piece[:2] for piece in pieces)
    return pl.pallas_call(
        functools.partial(assemble_kernel, parts, share),
        grid_spec=pltpu.PrefetchScalarGridSpec(
            num_scalar_prefetch=1,
            grid=(1,),
            in_specs=[ANYWHERE] * len(arrays),
            out_specs=ANYWHERE,
            scratch_shapes=[pltpu.VMEM(v.shape, v.dtype) for v in arrays]
            + [pltpu.SemaphoreType.DMA((2, len(arrays)))],
        ),
        out_shape=jax.ShapeDtypeStruct((total, depth), arrays[0].dtype),
        cost_estimate=cost(0),
        compiler_params=limit(12),
        name="assemble",
    )(place, *arrays)


QUARTERS = 4


def collect(place, refs, buffer):
    share = refs[0].shape[0]
    number = place[4 + SLOT_COUNT] * len(refs) // QUARTERS
    for far, ref in enumerate(refs):
        start = (number ^ far) * share
        buffer[pl.ds(pl.multiple_of(start, 8), share)] = ref[...].astype(f32)


def finish_up_kernel(place, *refs):
    pieces, (grad_ref, bias_ref, buffer) = refs[:-3], refs[-3:]
    collect(place, pieces, buffer)
    depth, slots = grad_ref.shape
    hidden = buffer.shape[0] - HIDDEN_EXTRA
    grad_ref[:, 0:hidden] = buffer[0:hidden].T
    if slots > hidden:
        grad_ref[:, hidden:] = jnp.zeros((depth, slots - hidden), f32)
    bias_ref[...] = buffer[hidden : hidden + 8]


def finish_down_kernel(per_head, place, *refs):
    pieces, (grad_ref, out_ref, extra_ref, buffer) = refs[:-4], refs[-4:]
    collect(place, pieces, buffer)
    width = out_ref.shape[0]
    hidden = buffer.shape[0] - HIDDEN_EXTRA - width
    row = lax.broadcasted_iota(jnp.int32, (hidden, buffer.shape[1]), 0)
    grad_ref[0:hidden] = jnp.where(row < place[3] * per_head, buffer[0:hidden], 0.0)
    if grad_ref.shape[0] > hidden:
        grad_ref[hidden:] = jnp.zeros((grad_ref.shape[0] - hidden, buffer.shape[1]), f32)
    out_ref[...] = buffer[hidden : hidden + width]
    extra_ref[...] = buffer[hidden + width : hidden + width + 8]


def finish_attn_kernel(place, *refs):
    pieces, (query_ref, key_ref, value_ref, extra_ref, buffer) = refs[:QUARTERS], refs[QUARTERS:]
    collect(place, pieces, buffer)
    width = query_ref.shape[0]
    for index, ref in enumerate((query_ref, key_ref, value_ref)):
        ref[...] = buffer[index * width : (index + 1) * width]
    extra_ref[...] = buffer[3 * width : 3 * width + 8]


def finish(kernel, place, pieces, shapes, name):
    rows, depth = pieces[0].shape[0] * len(pieces), pieces[0].shape[1]
    return pl.pallas_call(
        kernel,
        grid_spec=pltpu.PrefetchScalarGridSpec(
            num_scalar_prefetch=1,
            grid=(1,),
            in_specs=[whole(v.shape) for v in pieces],
            out_specs=[whole(shape) for shape in shapes],
            scratch_shapes=[pltpu.VMEM((rows, depth), f32)],
        ),
        out_shape=[jax.ShapeDtypeStruct(shape, f32) for shape in shapes],
        cost_estimate=cost(0),
        compiler_params=limit(20),
        name=name,
    )(place, *pieces)


def shares_kernel(distances, group, place, *refs):
    step = pl.program_id(0)
    steps = pl.num_programs(0)
    count = len(distances)
    sources, blocksum_ref, (own_ref, *sent_refs) = refs[:count], refs[count], refs[count + 1 :]
    rows_touched = (place[0] + steps - 1) // place[1] - place[0] // place[1] + 1
    for distance, source, target in zip(distances, sources, (own_ref, *sent_refs)):
        block = (place[2] ^ distance) * steps + step - place[0] // place[1] * place[1]
        inside = jnp.logical_and(block >= 0, block < rows_touched * place[1])
        value = jnp.where(inside, source[0].astype(f32), 0.0)
        if distance == 0:
            target[0] = blocksum_ref[0] + value
        else:
            target[0] = value.astype(bf16)


def shares(place, rowsum, blocksum, distances):
    steps, size, depth = blocksum.shape
    group = None
    window = rowsum.reshape(-1, size, depth)

    def source(distance):
        def index(b, place):
            block = (place[2] ^ distance) * steps + b - place[0] // place[1] * place[1]
            return jnp.clip(block, 0, window.shape[0] - 1), 0, 0

        return pl.BlockSpec((1, size, depth), index)

    block = pl.BlockSpec((1, size, depth), local)
    return pl.pallas_call(
        functools.partial(shares_kernel, distances, group),
        grid_spec=pltpu.PrefetchScalarGridSpec(
            num_scalar_prefetch=1,
            grid=(steps,),
            in_specs=[source(d) for d in distances] + [block],
            out_specs=[block for _ in distances],
        ),
        out_shape=[
            jax.ShapeDtypeStruct(blocksum.shape, bf16 if d else f32) for d in distances
        ],
        compiler_params=limit(12),
        name="shares",
    )(place, *[window for _ in distances], blocksum)


def row_chunks(count, body):
    chunk = 200 if count % 200 == 0 else 16

    @pl.loop(0, count // chunk)
    def _(i):
        body(pl.ds(pl.multiple_of(i * chunk, 8), chunk))

    if count % chunk:
        body(pl.ds(count // chunk * chunk, count % chunk))


def phi_parts(value):
    bell = jnp.exp2(value * value * (-0.5 / math.log(2.0)))
    t = 1.0 / (1.0 + jnp.abs(value) * (0.3275911 * 0.5**0.5))
    poly = t * (
        0.127414796
        + t * (-0.142248368 + t * (0.7107068705 + t * (-0.7265760135 + t * 0.5307027145)))
    )
    half = poly * bell
    return jnp.where(value >= 0, 1.0 - half, half), bell * (2.0 * math.pi) ** -0.5


def chunk_stats(value):
    centre = value - jnp.mean(value, axis=-1, keepdims=True)
    inverse = lax.rsqrt(jnp.mean(centre * centre, axis=-1, keepdims=True) + norm_eps)
    return centre * inverse, inverse


def fetch_slot(order, step, sources, buffers, sems):
    for which, (refs, buffer) in enumerate(zip(sources, buffers)):
        for position, slot in enumerate(order):

            @pl.when(step == position)
            def _():
                pltpu.make_async_copy(refs[slot], buffer.at[step % 2], sems.at[which, step % 2]).start()


def await_slot(step, sources, buffers, sems):
    for which, (refs, buffer) in enumerate(zip(sources, buffers)):
        pltpu.make_async_copy(refs[0], buffer.at[step % 2], sems.at[which, step % 2]).wait()


def stream_slots(order, sources, buffers, sems):
    step = pl.program_id(0)

    @pl.when(step == 0)
    def _():
        fetch_slot(order, step, sources, buffers, sems)

    @pl.when(step + 1 < pl.num_programs(0))
    def _():
        fetch_slot(order, step + 1, sources, buffers, sems)

    await_slot(step, sources, buffers, sems)


def fetch_slot(order, step, sources, buffers, sems, firsts):
    for which, (refs, buffer, first) in enumerate(zip(sources, buffers, firsts)):
        for position, slot in enumerate(order):

            @pl.when(step == position)
            def _():
                pltpu.make_async_copy(
                    refs[slot].at[pl.ds(first, buffer.shape[1])],
                    buffer.at[step % 2],
                    sems.at[which, step % 2],
                ).start()


def stream_slots(order, sources, buffers, sems, firsts):
    step = pl.program_id(0)

    @pl.when(step == 0)
    def _():
        fetch_slot(order, step, sources, buffers, sems, firsts)

    @pl.when(step + 1 < pl.num_programs(0))
    def _():
        fetch_slot(order, step + 1, sources, buffers, sems, firsts)

    for which, (refs, buffer, first) in enumerate(zip(sources, buffers, firsts)):
        pltpu.make_async_copy(
            refs[0].at[pl.ds(first, buffer.shape[1])], buffer.at[step % 2], sems.at[which, step % 2]
        ).wait()


def ffn_kernel(
    group, place, frames_ref, cot_ref, ids_ref, vec_ref, *refs,
):
    held = len(refs) - 15 - 3 * group
    context_refs, refs = refs[:held], refs[held:]
    weight_refs, refs = refs[:group], refs[group:]
    up_refs, down_refs = refs[:group], refs[group : 2 * group]
    (
        layer_ref, low_ref, normal_ref, inverse_ref, gradffn_ref, small_ref,
        active_ref, slope_ref, up_buf, down_buf, out_buf, bias_buf, mixed, sems, out_sems,
    ) = refs[2 * group :]
    turns = group // held
    step = pl.program_id(0)
    count, depth = mixed.shape
    hidden = active_ref.shape[2]
    width = out_buf.shape[1]
    out_bias, gain_one, shift_one = vec_ref[0:1], vec_ref[1:2], vec_ref[2:3]
    outer_bias, gain_two, shift_two = vec_ref[3:4], vec_ref[4:5], vec_ref[5:6]

    def out_copies(slot):
        return [
            pltpu.make_async_copy(
                weight_refs[slot].at[pl.ds(first, target.shape[1])], target.at[slot], out_sems.at[which, slot]
            )
            for which, (target, first) in enumerate(
                ((out_buf, 3 * width + BIAS_ROWS), (bias_buf, 3 * width))
            )
        ]

    @pl.when(step == 0)
    def _():
        for slot in range(group):
            for copy in out_copies(slot):
                copy.start()

    stream_slots(tuple(range(group)), (up_refs, down_refs), (up_buf, down_buf), sems, (0, 0))

    @pl.when(step == 0)
    def _():
        for slot in range(group):
            for copy in out_copies(slot):
                copy.wait()
        _, blocks, _, size = context_refs[0].shape
        for block in range(blocks):
            total = dot(context_refs[0][0, block], out_buf[0], 0, 0)
            for slot in range(1, group):
                total += dot(context_refs[slot // turns][slot % turns, block], out_buf[slot], 0, 0)
            mixed[block * size : (block + 1) * size] = total

        def first(rows):
            hidden_one = frames_ref[0, rows].astype(f32) + mixed[rows] + out_bias
            normal, inverse = chunk_stats(hidden_one)
            normal_ref[rows] = normal.astype(bf16)
            inverse_ref[rows] = inverse
            normed = normal * gain_one + shift_one
            low_ref[rows] = normed.astype(bf16)
            mixed[rows] = normed + outer_bias

        row_chunks(count, first)

    biases = bias_buf[step].astype(f32)
    bias = jnp.concatenate([bias_row(biases, 2), bias_row(biases, 3)[:, 0 : hidden - depth]], axis=1)
    up_now, down_now = up_buf[step % 2], down_buf[step % 2]

    def gelu(rows):
        value = dot(low_ref[rows], up_now, 1, 1) + bias
        whole_part, bell = phi_parts(value)
        active = (value * whole_part).astype(bf16)
        active_ref[0, rows] = active
        slope_ref[0, rows] = (whole_part + value * bell).astype(bf16)
        mixed[rows] += dot(active, down_now, 1, 0)

    gelu(slice(None))

    @pl.when(step == pl.num_programs(0) - 1)
    def _():
        small_ref[...] = jnp.zeros_like(small_ref)

        def last(rows):
            normal, inverse = chunk_stats(mixed[rows])
            live = (ids_ref[rows] >= 0).astype(f32)
            layer_ref[rows] = ((normal * gain_two + shift_two) * live).astype(bf16)
            grad = cot_ref[0, rows].astype(f32) * live
            small_ref[0:1] += jnp.sum(grad * normal, axis=0, keepdims=True)
            small_ref[1:2] += jnp.sum(grad, axis=0, keepdims=True)
            scaled = grad * gain_two
            back = inverse * (
                scaled
                - jnp.mean(scaled, axis=-1, keepdims=True)
                - normal * jnp.mean(scaled * normal, axis=-1, keepdims=True)
            )
            small_ref[2:3] += jnp.sum(back, axis=0, keepdims=True)
            gradffn_ref[rows] = back.astype(bf16)

        row_chunks(count, last)


def up_back_kernel(
    order, last, group, low_ref, normal_ref, inverse_ref, before_ref, gradffn_ref, slope_ref,
    gain_ref, *refs,
):
    up_refs, down_refs, rest = refs[:group], refs[group : 2 * group], refs[2 * group :]
    if last:
        upgrad_ref, small_ref, gradone_ref, gradattn_ref, *rest = rest
    else:
        upgrad_ref, normed_grad, *rest = rest
    up_buf, down_buf, inner, sems, *rest = rest
    if last:
        normed_grad = rest[0]
    step = pl.program_id(0)
    count, hidden = inner.shape
    depth = low_ref.shape[1]
    stream_slots(order, (up_refs, down_refs), (up_buf, down_buf), sems, (0, 0))

    @pl.when(step == 0)
    def _():
        normed_grad[...] = before_ref[...] if last else gradffn_ref[...].astype(f32)

    grad_active = dot(gradffn_ref[...], down_buf[step % 2], 1, 1)
    inner[...] = (grad_active * slope_ref[0].astype(f32)).astype(bf16)
    upgrad_ref[0, 0:hidden] = dot(inner[...], low_ref[...], 0, 0).astype(bf16)
    ones = jnp.ones((8, count), bf16)
    bias = dot(ones, inner[...], 1, 0)
    row = lax.broadcasted_iota(jnp.int32, (upgrad_ref.shape[1] - hidden, depth), 0)
    extra = jnp.where(row == 0, bias[0:1, 0:depth], 0.0)
    rest_lanes = jnp.pad(bias[0:1, depth:hidden], ((0, 0), (0, 2 * depth - hidden)))
    upgrad_ref[0, hidden:] = jnp.where(row == 1, rest_lanes, extra).astype(bf16)
    normed_grad[...] += dot(inner[...], up_buf[step % 2], 1, 0)

    if last:

        @pl.when(step == pl.num_programs(0) - 1)
        def _():
            small_ref[...] = jnp.zeros_like(small_ref)
            gain = gain_ref[...]

            def last_rows(rows):
                grad, normal = normed_grad[rows], normal_ref[rows].astype(f32)
                small_ref[0:1] += jnp.sum(grad * normal, axis=0, keepdims=True)
                small_ref[1:2] += jnp.sum(grad, axis=0, keepdims=True)
                scaled = grad * gain
                back = inverse_ref[rows] * (
                    scaled
                    - jnp.mean(scaled, axis=-1, keepdims=True)
                    - normal * jnp.mean(scaled * normal, axis=-1, keepdims=True)
                )
                small_ref[2:3] += jnp.sum(back, axis=0, keepdims=True)
                gradone_ref[rows] = back
                gradattn_ref[rows] = back.astype(bf16)

            row_chunks(count, last_rows)


def down_back_kernel(
    order, group, active_ref, gradffn_ref, gradattn_ref, small_ref, smalltwo_ref, *refs
):
    context_refs, result_ref = refs[:-1], refs[-1]
    turns = group // len(context_refs)
    step = pl.program_id(0)
    hidden = active_ref.shape[2]
    depth = gradffn_ref.shape[1]
    _, blocks, width, size = context_refs[0].shape
    result_ref[0, 0:hidden] = dot(active_ref[0], gradffn_ref[...], 0, 0).astype(bf16)
    for position, slot in enumerate(order):

        @pl.when(step == position)
        def _():
            context = context_refs[slot // turns].at[slot % turns]
            total = dot(context[0], gradattn_ref[0:size], 1, 0)
            for block in range(1, blocks):
                total += dot(context[block], gradattn_ref[block * size : (block + 1) * size], 1, 0)
            result_ref[0, hidden : hidden + width] = total.astype(bf16)

    row = lax.broadcasted_iota(jnp.int32, (HIDDEN_EXTRA, depth), 0)
    extra = jnp.zeros((HIDDEN_EXTRA, depth), f32)
    for index in range(3):
        extra = jnp.where(row == index, small_ref[index : index + 1], extra)
        extra = jnp.where(row == 3 + index, smalltwo_ref[index : index + 1], extra)
    result_ref[0, hidden + width :] = extra.astype(bf16)


def ffn(place, frames, cotangent, ids, vectors, contexts, weights, up, down):
    group = len(up)
    count, depth = frames.shape[1:]
    hidden = down[0].shape[0]
    width = contexts[0].shape[2]
    own = pl.BlockSpec((1, count, depth), lambda s, place: (place[2], 0, 0))
    per_slot = pl.BlockSpec((1, count, hidden), lambda s, place: (s, 0, 0))
    spec = pltpu.PrefetchScalarGridSpec(
        num_scalar_prefetch=1,
        grid=(group,),
        in_specs=[own, own, whole(ids.shape), whole(vectors.shape)]
        + [whole(contexts[0].shape)] * len(contexts)
        + [ANYWHERE] * (3 * group),
        out_specs=[
            whole((count, depth)), whole((count, depth)), whole((count, depth)), whole((count, 1)),
            whole((count, depth)), whole((8, depth)), per_slot, per_slot,
        ],
        scratch_shapes=[
            pltpu.VMEM((2, hidden, depth), bf16),
            pltpu.VMEM((2, hidden, depth), bf16),
            pltpu.VMEM((group, width, depth), bf16),
            pltpu.VMEM((group, BIAS_ROWS, depth), bf16),
            pltpu.VMEM((count, depth), f32),
            pltpu.SemaphoreType.DMA((2, 2)),
            pltpu.SemaphoreType.DMA((2, group)),
        ],
    )
    shape = jax.ShapeDtypeStruct
    return pl.pallas_call(
        functools.partial(ffn_kernel, group),
        grid_spec=spec,
        out_shape=[
            shape((count, depth), bf16), shape((count, depth), bf16), shape((count, depth), bf16),
            shape((count, 1), f32), shape((count, depth), bf16), shape((8, depth), f32), shape((group, count, hidden), bf16),
            shape((group, count, hidden), bf16),
        ],
        cost_estimate=cost(2**34),
        compiler_params=limit(28),
        name="ffn",
    )(
        place, far_away(frames), far_away(cotangent), ids, vectors, *map(far_away, contexts), *map(far_away, weights),
        *up, *down,
    )


def in_order(order):
    def slot_of(s):
        result = jnp.int32(order[-1])
        for position in reversed(range(len(order) - 1)):
            result = jnp.where(s == position, order[position], result)
        return result

    return slot_of


def everything(shape):
    return pl.BlockSpec(shape, lambda s: (0,) * len(shape))


def up_back(order, last, low, normal, inverse, before, gradffn, slope, gain, up, down):
    group = len(up)
    count, depth = low.shape
    hidden = slope.shape[2]
    slot_of = in_order(order)
    per_slot = pl.BlockSpec((1, count, hidden), lambda s: (slot_of(s), 0, 0))
    rows = hidden + HIDDEN_EXTRA
    shape = jax.ShapeDtypeStruct
    wide = shape((count, depth), f32)
    tail = [shape((8, depth), f32), wide, shape((count, depth), bf16)] if last else [wide]
    return pl.pallas_call(
        functools.partial(up_back_kernel, order, last, group),
        grid=(len(order),),
        in_specs=[
            everything(v.shape) for v in (low, normal, inverse, before, gradffn)
        ]
        + [per_slot, everything(gain.shape)]
        + [ANYWHERE] * (2 * group),
        out_specs=[pl.BlockSpec((1, rows, depth), lambda s: (s, 0, 0))]
        + [everything(t.shape) for t in tail],
        out_shape=[shape((len(order), rows, depth), bf16)] + tail,
        scratch_shapes=[
            pltpu.VMEM((2, hidden, depth), bf16),
            pltpu.VMEM((2, hidden, depth), bf16),
            pltpu.VMEM((count, hidden), bf16),
            pltpu.SemaphoreType.DMA((2, 2)),
        ]
        + ([pltpu.VMEM((count, depth), f32)] if last else []),
        cost_estimate=cost(2**33),
        compiler_params=limit(26),
        name="up_back",
    )(low, normal, inverse, before, gradffn, slope, gain, *up, *down)


def down_back(order, active, gradffn, gradattn, smalls, contexts):
    count, hidden = active.shape[1:]
    depth = gradffn.shape[1]
    width = contexts[0].shape[2]
    slot_of = in_order(order)
    rows = hidden + width + HIDDEN_EXTRA
    return pl.pallas_call(
        functools.partial(down_back_kernel, order, active.shape[0]),
        grid=(len(order),),
        in_specs=[pl.BlockSpec((1, count, hidden), lambda s: (slot_of(s), 0, 0))]
        + [everything(v.shape) for v in (gradffn, gradattn, *smalls, *contexts)],
        out_specs=pl.BlockSpec((1, rows, depth), lambda s: (s, 0, 0)),
        out_shape=jax.ShapeDtypeStruct((len(order), rows, depth), bf16),
        cost_estimate=cost(2**32),
        compiler_params=limit(20),
        name="down_back",
    )(active, gradffn, gradattn, *smalls, *contexts)


def swap(value, axis, distance):
    size = lax.axis_size(axis)
    return lax.ppermute(value, axis, [(i, i ^ distance) for i in range(size)])


def add_low(a, b):
    return (a.astype(f32) + b.astype(f32)).astype(bf16)


def add_three(a, b, c):
    return (a.astype(f32) + b.astype(f32) + c.astype(f32)).astype(bf16)


def hold(value, *others):
    return lax.optimization_barrier((value,) + tuple(others))[0]


def row_distances(size):
    distance, result = 1, []
    while distance < size:
        result.append(distance)
        distance *= 2
    return result


def join_rows(value, arrived, distance):
    upper = (lax.axis_index("rows") // distance) % 2 == 1
    return jnp.concatenate(
        [jnp.where(upper, arrived, value), jnp.where(upper, value, arrived)], axis=0
    )


def far_swap(value, far):
    return swap(value, "rows", (far & 1) * 2 + (far >> 1))


def own_quarter():
    here = lax.axis_index("rows")
    return here % 2 * 2 + here // 2 % 2


def quarters_of(value, axis=0):
    rows = value.shape[axis] // QUARTERS
    return [
        lax.dynamic_slice_in_dim(value, (own_quarter() ^ far) * rows, rows, axis)
        for far in range(QUARTERS)
    ]


def send_quarters(quarters):
    return [far_swap(quarters[far], far) for far in range(1, QUARTERS)]


def add_quarters(quarters, came):
    total = quarters[0].astype(f32)
    for value in came:
        total = total + value.astype(f32)
    return total.astype(bf16)


def join_pieces(pieces):
    near = [join_rows(pieces[i], pieces[i + 1], 2) for i in (0, 2)]
    return join_rows(near[0], near[1], 1)


def across(value, came, distances):
    value = add_low(value, came)
    for distance in distances:
        value = add_low(value, swap(value, "rows", distance))
    return value


def gather_slots(value):
    slots = {0: value}
    distance = lax.axis_size("heads") // 2
    while distance >= 1:
        for slot in list(slots):
            slots[slot ^ distance] = swap(slots[slot], "heads", distance)
        distance //= 2
    return [slots[slot] for slot in range(len(slots))]


def per_device(
    frames, segment_ids, cotangent, query_weight, query_bias, key_weight, value_weight, value_bias,
    output_weight, output_bias, first_gain, first_shift, inner_weight, inner_bias, outer_weight,
    outer_bias, second_gain, second_shift,
):
    group = lax.axis_size("heads")
    position = lax.axis_index("heads")
    row_count, row_length, depth = frames.shape
    own_len = row_count * row_length // group
    size = math.gcd(row_length, own_len)
    steps = own_len // size
    per_row = row_length // size
    width = query_weight.shape[1]
    heads_here = width // HEAD_DIM
    per_head = FF_LIVE // HEADS_LIVE
    hidden_slots = inner_weight.shape[1]
    hidden_cap = min(hidden_slots, (HEADS_LIVE + group - 1) // group * per_head)

    def live_of(index):
        return HEADS_LIVE // group + (index < HEADS_LIVE % group).astype(jnp.int32)

    rest = row_distances(lax.axis_size("rows"))[2:]
    piece_rows = hidden_cap // QUARTERS
    place = jnp.stack(
        [position * steps, jnp.int32(per_row), position]
        + [live_of(position ^ slot) for slot in range(group)]
        + [own_quarter() * piece_rows, own_quarter()]
    )
    blocks = frames.reshape(row_count * per_row, size, depth)
    weight_own, piece = prepare(
        place, query_weight.T, key_weight.T, value_weight.T, query_bias, value_bias,
        inner_bias, output_weight, outer_weight, piece_rows,
    )
    weight = {0: weight_own, 1: swap(weight_own, "heads", 1), 2: swap(weight_own, "heads", 2)}
    piece = swap(piece, "heads", 2)
    up_own, down_own, keyf, queryf = prepare_wide(
        place, inner_weight, outer_weight, segment_ids,
        segment_ids.reshape(row_count * per_row, 1, size), hidden_cap,
    )
    up = {0: up_own, 1: swap(up_own, "heads", 1)}
    down = {0: down_own, 1: swap(down_own, "heads", 1)}
    half = group // 2

    def forward(first, *waits):
        return attend(
            first, place, hold(blocks, *waits), frames,
            [weight[slot] for slot in range(first, first + half)], keyf, queryf, steps, width,
        )

    saved = [forward(0)]
    done = saved[0][0]
    weight[2], piece, done = lax.optimization_barrier((weight[2], piece, done))
    weight[3] = swap(weight[2], "heads", 1)
    up[2] = swap(hold(up_own, weight[2]), "heads", 2)
    piece = hold(piece, weight[2])
    pieces = [piece] + send_quarters([piece] * QUARTERS)
    saved.append(forward(half, done))
    down[2] = join_pieces(hold(pieces, saved[1][0]))
    up[3] = swap(up[2], "heads", 1)
    down[3] = swap(down[2], "heads", 1)
    up = [up[slot] for slot in range(group)]
    down = [down[slot] for slot in range(group)]
    contexts = [kept[3] for kept in saved]

    vectors = jnp.stack(
        [output_bias, first_gain, first_shift, outer_bias, second_gain, second_shift]
    )
    whole_frames = frames.reshape(group, own_len, depth)
    whole_cot = cotangent.reshape(group, own_len, depth)
    flat_ids = segment_ids.reshape(row_count * row_length)
    ids_own = lax.dynamic_slice_in_dim(flat_ids, position * own_len, own_len)[:, None]
    layer_own, normed_low, normal_one, inverse_one, grad_ffn, small_two, actives, slopes = ffn(
        place, whole_frames, whole_cot, ids_own, vectors, contexts,
        [weight[slot] for slot in range(group)], up, down,
    )
    layer = {0: layer_own, 1: swap(layer_own, "heads", 1), 2: swap(layer_own, "heads", 2)}
    known = (normed_low, normal_one, inverse_one)
    gain = first_gain[None]
    up_send, grad_part = up_back((1, 3), False, *known, inverse_one, grad_ffn, slopes, gain, up, down)
    up_came = swap(up_send, "heads", 1)
    layer[1] = hold(layer[1], grad_part)
    up_keep, small_one, grad_hidden_one, grad_attn = up_back(
        (0, 2), True, *known, grad_part, grad_ffn, slopes, gain, up, down
    )
    barrier = lax.optimization_barrier
    up_quarters = quarters_of(add_low(up_keep, up_came), 1)
    up_came = send_quarters(up_quarters)

    smalls = (small_one, small_two)
    down_send = down_back((1, 3), actives, hold(grad_ffn, up_quarters), grad_attn, smalls, contexts)
    down_came = swap(down_send, "heads", 1)
    down_keep = down_back((0, 2), actives, hold(grad_ffn, down_send), grad_attn, smalls, contexts)
    down_came = hold(down_came, down_keep)
    grad_attn = grad_attn.reshape(steps, size, depth)
    block_sum = grad_hidden_one.reshape(steps, size, depth)
    row_sum = jnp.zeros((8, 128), bf16)
    grads = {}

    def back(slot, first, block_sum, row_sum, *waits):
        return attend_back(
            slot, first, place, blocks, frames, weight[slot], saved[slot // half], grad_attn,
            hold(block_sum, *waits), row_sum,
        )

    layer[2] = hold(layer[2], down_keep)
    layer[3] = swap(layer[2], "heads", 1)
    down_two = add_low(down_keep[1], down_came[1])
    cut = down_two.shape[0] * 9 // 16 // 8 * 8
    down_first = swap(hold(down_two[:cut], layer[2]), "heads", 2)
    grads[3], block_sum, row_sum = back(3, True, block_sum, row_sum, layer[2], down_two)

    block_sum, up_came, down_first, layer[3], grads[3] = barrier(
        (block_sum, up_came, down_first, layer[3], grads[3])
    )
    down_second = swap(hold(down_two[cut:], down_first), "heads", 2)
    grads_came = swap(grads[3], "heads", 1)
    up_pair = add_quarters(up_quarters, up_came)
    up_came = swap(up_pair[1], "heads", 2)
    grads[2], block_sum, row_sum = back(2, False, block_sum, row_sum, up_pair)

    block_sum, up_came, down_second, grads_came, grads[2] = barrier(
        (block_sum, up_came, down_second, grads_came, grads[2])
    )
    attn_two = add_low(grads[2], grads_came)
    attn_rows = attn_two.shape[0] // 2
    attn_first = swap(attn_two[:attn_rows], "heads", 2)
    up_piece = add_low(up_pair[0], up_came)
    up_came = swap(up_piece, "rows", rest[0])
    down_far = jnp.concatenate([down_first, down_second])
    down_quarters = quarters_of(add_three(down_keep[0], down_came[0], down_far))
    down_came = send_quarters(down_quarters)
    grads[1], block_sum, row_sum = back(
        1, False, block_sum, row_sum, attn_two, up_piece, down_quarters
    )

    block_sum, up_came, down_came, attn_first, grads[1] = barrier(
        (block_sum, up_came, down_came, attn_first, grads[1])
    )
    grads_came = swap(grads[1], "heads", 1)
    up_piece = across(up_piece, up_came, rest[1:])
    attn_second = swap(hold(attn_two[attn_rows:], attn_first), "heads", 2)
    up_came = swap(up_piece, "rows", 2)
    down_piece = add_quarters(down_quarters, down_came)
    down_came = swap(down_piece, "rows", rest[0])
    grads[0], block_sum, row_sum = back(0, False, block_sum, row_sum, up_piece, down_piece)
    block_sum, up_came, down_came, attn_second, grads_came, grads[0] = barrier(
        (block_sum, up_came, down_came, attn_second, grads_came, grads[0])
    )

    reach, pairs = [0], {}
    for distance in range(1, group):
        pairs[distance] = []
        for i in range(group):
            j = i ^ distance
            rows_i = range(i * steps // per_row, ((i + 1) * steps - 1) // per_row + 1)
            rows_j = range(j * steps // per_row, ((j + 1) * steps - 1) // per_row + 1)
            if set(rows_i) & set(rows_j):
                pairs[distance].append((i, j))
        if pairs[distance]:
            reach.append(distance)
    own_grad, *owed = shares(place, row_sum, block_sum, tuple(reach))
    attn_two = jnp.concatenate([attn_first, attn_second])
    attn_quarters = quarters_of(add_three(hold(grads[0], owed), grads_came, attn_two))
    owed = [
        lax.ppermute(sent, "heads", pairs[distance]) for distance, sent in zip(reach[1:], owed)
    ]
    attn_came = send_quarters(attn_quarters)
    up_half = join_rows(up_piece, hold(up_came, own_grad), 2)
    down_piece = across(down_piece, hold(down_came, own_grad), rest[1:])
    layer[0] = hold(layer[0], own_grad)
    layer_out = assemble(
        place, [(slot, 0, layer[slot]) for slot in range(group)], own_len, row_count * row_length
    ).reshape(frames.shape)
    attn_came, owed, layer_out, up_half, down_piece = barrier(
        (attn_came, owed, layer_out, up_half, down_piece)
    )

    attn_piece = add_quarters(attn_quarters, attn_came)
    attn_came = swap(attn_piece, "rows", rest[0])
    up_came = swap(hold(up_half, attn_piece), "rows", 1)
    for came in owed:
        own_grad = own_grad + hold(came, attn_piece).astype(f32)
    own_grad = own_grad.astype(bf16).reshape(own_len, depth)
    cut = own_len // 2 // 8 * 8
    first_cut = swap(own_grad[:cut], "heads", 2)
    mate = swap(own_grad, "heads", 1)
    attn_came, first_cut, mate, up_came = barrier((attn_came, first_cut, mate, up_came))

    attn_piece = across(attn_piece, attn_came, rest[1:])
    attn_came = send_quarters([attn_piece] * QUARTERS)
    second_cut = swap(hold(own_grad[cut:], attn_piece), "heads", 2)
    down_came = send_quarters([hold(down_piece, attn_piece)] * QUARTERS)
    up_done = finish(
        finish_up_kernel, place, [hold(up_half, attn_piece), up_came],
        [(depth, hidden_slots), (8, depth)], "finish_up",
    )
    second_cut, up_done, attn_came = barrier((second_cut, up_done, attn_came))
    second_mate = swap(second_cut, "heads", 1)
    first_mate = swap(hold(first_cut, second_cut), "heads", 1)
    attn_done = finish(
        finish_attn_kernel, place, [attn_piece, *attn_came],
        [(width, depth)] * 3 + [(8, depth)], "finish_attn",
    )
    frames_grad = assemble(
        place,
        [
            (0, 0, own_grad), (1, 0, mate), (2, 0, first_cut), (2, cut, second_cut),
            (3, 0, first_mate), (3, cut, second_mate),
        ],
        own_len, row_count * row_length,
    ).reshape(frames.shape)
    down_done = finish(
        functools.partial(finish_down_kernel, per_head), place,
        [down_piece, *hold(down_came, frames_grad)],
        [(hidden_slots, depth), (width, depth), (8, depth)], "finish_down",
    )

    innerbias = jnp.concatenate([up_done[1][0], up_done[1][1, : hidden_cap - depth]])
    innerbias_full = jnp.pad(innerbias, ((0, hidden_slots - hidden_cap),))
    extra = attn_done[3]
    small = down_done[2]
    return (
        layer_out,
        frames_grad,
        attn_done[0].T,
        extra[0, :width],
        attn_done[1].T,
        attn_done[2].T,
        extra[1, :width],
        down_done[1],
        small[2],
        small[0],
        small[1],
        up_done[0],
        innerbias_full,
        down_done[0],
        small[5],
        small[3],
        small[4],
    )


def solution(mesh):
    in_specs = (
        P("rows", None, None), P("rows", None), P("rows", None, None), P(None, "heads"), P("heads"),
        P(None, "heads"), P(None, "heads"), P("heads"), P("heads", None), P(), P(), P(),
        P(None, "heads"), P("heads"), P("heads", None), P(), P(), P(),
    )
    out_specs = (
        P("rows", None, None), P("rows", None, None), P(None, "heads"), P("heads"), P(None, "heads"),
        P(None, "heads"), P("heads"), P("heads", None), P(), P(), P(), P(None, "heads"), P("heads"),
        P("heads", None), P(), P(), P(),
    )
    return jax.shard_map(
        per_device, mesh=mesh, in_specs=in_specs, out_specs=out_specs, check_vma=False
    )
```

```python
import functools
import math

import jax
import jax.numpy as jnp
from jax import lax
from jax.experimental import pallas as pl
from jax.experimental.pallas import tpu as pltpu
from jax.sharding import PartitionSpec as P

HEADS_LIVE = 10
HEAD_SLOTS = 12
HEAD_DIM = 64
FF_LIVE = 2240
PAD_HEAD = 128
SEGMENTS = 5
MASK_STEP = -(2.0**30)
norm_eps = 1e-05
f32 = jnp.float32
bf16 = jnp.bfloat16


def dot(a, b, ca, cb):
    return lax.dot_general(a, b, (((ca,), (cb,)), ((), ())), preferred_element_type=f32)


def three_parts(value):
    high = value.astype(bf16).astype(f32)
    middle = (value - high).astype(bf16).astype(f32)
    return high, middle, value - high - middle


def live_heads(live, heads, one_head):
    least = HEADS_LIVE * heads // HEAD_SLOTS
    for head in range(least):
        one_head(head)
    for head in range(least, heads):

        @pl.when(head < live)
        def _():
            one_head(head)


def feature_rows(base, value):
    high, middle, low = three_parts(-value)
    row = lax.broadcasted_iota(jnp.int32, base.shape, 0)
    base = jnp.where(row == SEGMENTS, high, base)
    base = jnp.where(row == SEGMENTS + 1, middle, base)
    return jnp.where(row == SEGMENTS + 2, low, base).astype(bf16)


def bias_row(rows, index):
    first = 3 * index
    return rows[first : first + 1] + rows[first + 1 : first + 2] + rows[first + 2 : first + 3]


def attend_kernel(
    first, place, block_ref, row_ref, keyf_ref, queryf_ref, *refs,
):
    pair = len(refs) - 5
    weight_refs, (query_ref, key_ref, value_ref, context_ref, weight_ref) = refs[:pair], refs[pair:]
    turn = pl.program_id(0)
    step = pl.program_id(1)
    per_row, live = place[1], place[3 + first + turn]
    row_now = (place[0] + step) // per_row
    row_before = (place[0] + step - 1) // per_row
    length = row_ref.shape[1]
    width = context_ref.shape[2]
    heads = width // HEAD_DIM

    for index, ref in enumerate(weight_refs):

        @pl.when(jnp.logical_and(step == 0, turn == index))
        def _():
            weight_ref[...] = ref[...]

    biases = weight_ref[3 * width :].astype(f32)

    @pl.when(jnp.logical_or(step == 0, row_now != row_before))
    def _():
        frames = row_ref[0]
        keys = dot(frames, weight_ref[width : 2 * width], 1, 1).astype(bf16)
        values = dot(frames, weight_ref[2 * width : 3 * width], 1, 1)
        values = (values + bias_row(biases, 1)[:, 0:width]).astype(bf16)
        features = keyf_ref[0]
        for head in range(heads):
            cut = slice(head * HEAD_DIM, (head + 1) * HEAD_DIM)
            key_ref[0, 0, head * length : (head + 1) * length] = jnp.concatenate(
                [keys[:, cut], features], axis=1
            )
            value_ref[0, 0, head * length : (head + 1) * length] = jnp.concatenate(
                [values[:, cut], features], axis=1
            )

    qbias = jnp.broadcast_to(bias_row(biases, 0)[:, 0:width], (8, width)).T[:, 0:1]
    queries = (dot(weight_ref[0:width], block_ref[0], 1, 1) + qbias).astype(bf16)
    queries = queries * jnp.asarray(HEAD_DIM**-0.5, bf16)
    for head in range(heads):
        query_ref[0, 0, head * PAD_HEAD : head * PAD_HEAD + HEAD_DIM] = queries[
            head * HEAD_DIM : (head + 1) * HEAD_DIM
        ]
        query_ref[0, 0, head * PAD_HEAD + HEAD_DIM : (head + 1) * PAD_HEAD] = queryf_ref[0]
    context_ref[...] = jnp.zeros_like(context_ref)

    def one_head(head):
        keys = key_ref[0, 0, pl.ds(head * length, length)]
        values = value_ref[0, 0, pl.ds(head * length, length)]
        start = head * PAD_HEAD
        scores = dot(keys, query_ref[0, 0, pl.ds(start, PAD_HEAD)], 1, 0)
        highest = jnp.max(scores, axis=0, keepdims=True)
        probs = jnp.exp(scores - highest).astype(bf16)
        mixed = dot(values, probs, 0, 0)
        total = mixed[HEAD_DIM + SEGMENTS : HEAD_DIM + SEGMENTS + 1]
        context = mixed[0:HEAD_DIM] / total
        context_ref[0, 0, pl.ds(head * HEAD_DIM, HEAD_DIM)] = context.astype(bf16)
        base = queryf_ref[0, 0:16].astype(f32)
        query_ref[0, 0, pl.ds(start + HEAD_DIM, 16)] = feature_rows(base, highest + jnp.log(total))

    live_heads(live, heads, one_head)


def attend_back_kernel(
    slot, first, place, block_ref, row_ref, weight_ref, query_ref, key_ref, value_ref,
    context_ref, grad_ref, blocksum_ref, rowsum_ref,
    gradw_ref, blockout_ref, rowout_ref,
    weight_acc, dkey, dvalue, picked, dcontext, dquery, bias_acc,
):
    step = pl.program_id(0)
    steps = pl.num_programs(0)
    per_row, live = place[1], place[3 + slot]
    row_now = (place[0] + step) // per_row
    row_before = (place[0] + step - 1) // per_row
    row_after = (place[0] + step + 1) // per_row
    length, depth = row_ref.shape[1:]
    width = context_ref.shape[2]
    heads = width // HEAD_DIM
    ones = jnp.ones((8, length), bf16)

    @pl.when(step == 0)
    def _():
        weight_acc[...] = jnp.zeros_like(weight_acc)
        bias_acc[...] = jnp.zeros_like(bias_acc)
        picked[...] = jnp.zeros_like(picked)

    @pl.when(jnp.logical_or(step == 0, row_now != row_before))
    def _():
        dkey[...] = jnp.zeros_like(dkey)
        dvalue[...] = jnp.zeros_like(dvalue)

    dcontext[...] = dot(weight_ref[3 * width + BIAS_ROWS :], grad_ref[0], 1, 1).astype(bf16)
    dquery[...] = jnp.zeros_like(dquery)

    def one_head(head):
        own = pl.ds(head * HEAD_DIM, HEAD_DIM)
        keys = key_ref[0, 0, pl.ds(head * length, length)]
        values = value_ref[0, 0, pl.ds(head * length, length)]
        queries = query_ref[0, 0, pl.ds(head * PAD_HEAD, PAD_HEAD)]
        grad = dcontext[own]
        inner = jnp.sum(grad.astype(f32) * context_ref[0, 0, own].astype(f32), axis=0, keepdims=True)
        extra = feature_rows(jnp.zeros((PAD_HEAD - HEAD_DIM, grad.shape[1]), f32), inner)
        probs = jnp.exp(dot(keys, queries, 1, 0))
        dprobs = dot(values, jnp.concatenate([grad, extra], axis=0), 1, 0)
        dscores = (probs * dprobs).astype(bf16)
        picked[0, pl.ds(head * width + head * HEAD_DIM, HEAD_DIM)] = grad
        picked[1, pl.ds(head * width + head * HEAD_DIM, HEAD_DIM)] = queries[0:HEAD_DIM]
        place_head = pl.ds(head * width, width)
        dvalue[...] += dot(probs.astype(bf16), picked[0, place_head], 1, 1)
        dkey[...] += dot(dscores, picked[1, place_head], 1, 1)
        dquery[own] = (dot(keys, dscores, 0, 0)[0:HEAD_DIM] * HEAD_DIM**-0.5).astype(bf16)

    live_heads(live, heads, one_head)
    weight_acc[0:width] += dot(dquery[...], block_ref[0], 1, 0)
    blockout_ref[0] = blocksum_ref[0] + dot(dquery[...], weight_ref[0:width], 0, 0)
    bias_acc[0:8] += dot(ones[:, 0 : dquery.shape[1]], dquery[...], 1, 1)

    @pl.when(jnp.logical_or(step == steps - 1, row_now != row_after))
    def _():
        keys_low = dkey[...].astype(bf16)
        values_low = dvalue[...].astype(bf16)
        weight_acc[width : 2 * width] += dot(keys_low, row_ref[0], 0, 0)
        weight_acc[2 * width : 3 * width] += dot(values_low, row_ref[0], 0, 0)
        back = dot(keys_low, weight_ref[width : 2 * width], 1, 0) + dot(
            values_low, weight_ref[2 * width : 3 * width], 1, 0
        )
        if first:
            rowout_ref[0] = back.astype(bf16)
        else:
            rowout_ref[0] = (rowsum_ref[0].astype(f32) + back).astype(bf16)
        bias_acc[8:16] += dot(ones, values_low, 1, 0)

    @pl.when(step == steps - 1)
    def _():
        gradw_ref[0 : 3 * width] = weight_acc[...].astype(bf16)
        row = lax.broadcasted_iota(jnp.int32, (gradw_ref.shape[0] - 3 * width, depth), 0)
        lanes = depth - width
        extra = jnp.where(row == 0, jnp.pad(bias_acc[0:1], ((0, 0), (0, lanes))), 0.0)
        extra = jnp.where(row == 1, jnp.pad(bias_acc[8:9], ((0, 0), (0, lanes))), extra)
        gradw_ref[3 * width :] = extra.astype(bf16)


def whole(shape):
    return pl.BlockSpec(shape, lambda b, place: (0,) * len(shape))


def limit(mib):
    return pltpu.CompilerParams(vmem_limit_bytes=mib * 2**20)


def cost(flops):
    return pl.CostEstimate(flops=2**40, bytes_accessed=2**33, transcendentals=0)


ANYWHERE = pl.BlockSpec(memory_space=pltpu.HBM)


def far_away(value):
    return pltpu.with_memory_space_constraint(value, pltpu.HBM)
BIAS_ROWS = 16
EXTRA_ROWS = 32
HIDDEN_EXTRA = 32


def row_of(b, place):
    return (place[0] + b) // place[1], 0, 0


def rel_row(b, place):
    return (place[0] + b) // place[1] - place[0] // place[1], 0, 0


def block_of(b, place):
    return place[0] + b, 0, 0


def local(b, place):
    return b, 0, 0


def attend(first, place, blocks, rows, weights, keyf, queryf, steps, width):
    size, depth = blocks.shape[1:]
    count, length, _ = rows.shape
    weight_shape = (3 * width + BIAS_ROWS, depth)
    heads = width // HEAD_DIM
    window = min(2, count)
    pair = len(weights)
    fixed = lambda shape: pl.BlockSpec(shape, lambda s, b, place: (0,) * len(shape))
    per_row = lambda shape: pl.BlockSpec((1,) + shape, lambda s, b, place: row_of(b, place))
    per_block = lambda shape: pl.BlockSpec((1,) + shape, lambda s, b, place: block_of(b, place))
    out_row = pl.BlockSpec(
        (1, 1, heads * length, PAD_HEAD), lambda s, b, place: (s,) + rel_row(b, place)
    )
    out_block = lambda rows: pl.BlockSpec((1, 1, rows, size), lambda s, b, place: (s, b, 0, 0))
    spec = pltpu.PrefetchScalarGridSpec(
        num_scalar_prefetch=1,
        grid=(pair, steps),
        in_specs=[
            per_block((size, depth)), per_row((length, depth)), per_row(keyf.shape[1:]),
            per_block(queryf.shape[1:]),
        ]
        + [fixed(weight_shape)] * pair,
        out_specs=[out_block(heads * PAD_HEAD), out_row, out_row, out_block(width)],
        scratch_shapes=[pltpu.VMEM(weight_shape, bf16)],
    )
    return pl.pallas_call(
        functools.partial(attend_kernel, first),
        grid_spec=spec,
        out_shape=[
            jax.ShapeDtypeStruct((pair, steps, heads * PAD_HEAD, size), bf16),
            jax.ShapeDtypeStruct((pair, window, heads * length, PAD_HEAD), bf16),
            jax.ShapeDtypeStruct((pair, window, heads * length, PAD_HEAD), bf16),
            jax.ShapeDtypeStruct((pair, steps, width, size), bf16),
        ],
        cost_estimate=cost(2**33),
        compiler_params=limit(FORWARD_LIMIT),
        name="attend",
    )(place, blocks, rows, keyf, queryf, *map(far_away, weights))


FORWARD_LIMIT = 60


def attend_back(slot, first, place, blocks, rows, weight, saved, grad, blocksum, rowsum):
    query, key, value, context = saved
    steps, size, depth = blocksum.shape
    count, length, _ = rows.shape
    width = context.shape[2]
    heads = width // HEAD_DIM
    turn = slot % query.shape[0]
    pinned = query.shape[0]
    saved_block = lambda v: pl.BlockSpec(
        (1, 1) + v.shape[2:], lambda b, place: (turn,) + local(b, place)
    )
    saved_row = lambda v: pl.BlockSpec(
        (1, 1) + v.shape[2:], lambda b, place: (turn,) + rel_row(b, place)
    )
    row_spec = pl.BlockSpec((1, length, depth), rel_row)
    near = far_away if slot >= pinned else lambda value: value
    spec = pltpu.PrefetchScalarGridSpec(
        num_scalar_prefetch=1,
        grid=(steps,),
        in_specs=[
            pl.BlockSpec((1, size, depth), block_of),
            pl.BlockSpec((1, length, depth), row_of),
            whole((4 * width + BIAS_ROWS, depth)),
            saved_block(query), saved_row(key), saved_row(value), saved_block(context),
            pl.BlockSpec((1, size, depth), local),
            pl.BlockSpec((1, size, depth), local),
            ANYWHERE if first else row_spec,
        ],
        out_specs=[
            whole((3 * width + EXTRA_ROWS, depth)),
            pl.BlockSpec((1, size, depth), local),
            row_spec,
        ],
        scratch_shapes=[
            pltpu.VMEM((3 * width, depth), f32),
            pltpu.VMEM((length, width), f32),
            pltpu.VMEM((length, width), f32),
            pltpu.VMEM((2, heads * width, size), bf16),
            pltpu.VMEM((width, size), bf16),
            pltpu.VMEM((width, size), bf16),
            pltpu.VMEM((16, width), f32),
        ],
    )
    return pl.pallas_call(
        functools.partial(attend_back_kernel, slot, first),
        grid_spec=spec,
        out_shape=[
            jax.ShapeDtypeStruct((3 * width + EXTRA_ROWS, depth), bf16),
            jax.ShapeDtypeStruct(blocksum.shape, f32),
            jax.ShapeDtypeStruct((min(2, count), length, depth), bf16),
        ],
        input_output_aliases={} if first else {10: 2},
        cost_estimate=cost(2**34),
        compiler_params=limit(26),
        name="attend_back",
    )(
        place, near(blocks), near(rows), near(weight), query, near(key), near(value), context, grad,
        blocksum, rowsum,
    )


def zero_tail(ref, first, rows, unit, live):
    for count in range(rows // unit):

        @pl.when(live == count)
        def _():
            ref[first + count * unit : first + rows] = jnp.zeros((rows - count * unit, ref.shape[1]), ref.dtype)


def prepare_kernel(
    per_head, place, query_ref, key_ref, value_ref, qbias_ref, vbias_ref, ubias_ref, out_ref, down_ref,
    weight_ref, piece_ref,
):
    width, depth = query_ref.shape
    weight_ref[0:width] = query_ref[...]
    weight_ref[width : 2 * width] = key_ref[...]
    weight_ref[2 * width : 3 * width] = value_ref[...]
    lanes = ubias_ref.shape[0]
    row = lax.broadcasted_iota(jnp.int32, (BIAS_ROWS, depth), 0)
    result = jnp.zeros((BIAS_ROWS, depth), f32)
    qbias, vbias, ubias = qbias_ref[...][None], vbias_ref[...][None], ubias_ref[...][None]
    vectors = [
        jnp.pad(qbias, ((0, 0), (0, depth - width))),
        jnp.pad(vbias, ((0, 0), (0, depth - width))),
        ubias[:, 0:depth],
        jnp.pad(ubias[:, depth:lanes], ((0, 0), (0, 2 * depth - lanes))),
    ]
    for index, vector in enumerate(vectors):
        for offset, part in enumerate(three_parts(vector)):
            result = jnp.where(row == 3 * index + offset, part, result)
    first = 3 * width + BIAS_ROWS
    weight_ref[3 * width : first] = result.astype(bf16)
    weight_ref[first : first + width] = out_ref[...]
    zero_tail(weight_ref, first, width, HEAD_DIM, place[3])
    piece = piece_ref.shape[0]
    start = place[3 + SLOT_COUNT]
    row = start + lax.broadcasted_iota(jnp.int32, (piece, depth), 0)
    kept = down_ref[pl.ds(pl.multiple_of(start, 8), piece)].astype(f32)
    piece_ref[...] = jnp.where(row < place[3] * per_head, kept, 0.0).astype(bf16)


SLOT_COUNT = 4


def prepare(place, query, key, value, qbias, vbias, ubias, out, down, piece):
    width, depth = query.shape
    shapes = [(4 * width + BIAS_ROWS, depth), (piece, depth)]
    args = (query, key, value, qbias, vbias, ubias, out, down)
    return pl.pallas_call(
        functools.partial(prepare_kernel, FF_LIVE // HEADS_LIVE),
        grid_spec=pltpu.PrefetchScalarGridSpec(
            num_scalar_prefetch=1,
            grid=(1,),
            in_specs=[whole(v.shape) for v in args],
            out_specs=[whole(shape) for shape in shapes],
        ),
        out_shape=[jax.ShapeDtypeStruct(shape, bf16) for shape in shapes],
        compiler_params=limit(60),
        name="prepare",
    )(place, *args)


def prepare_wide_kernel(
    per_head, place, up_ref, down_ref, ids_ref, blocks_ref,
    upout_ref, downout_ref, keyf_ref, queryf_ref,
):
    hidden = downout_ref.shape[0]
    upout_ref[...] = up_ref[...].T[0:hidden]
    downout_ref[...] = down_ref[0:hidden]
    zero_tail(downout_ref, 0, hidden, per_head, place[3])
    rows, length = ids_ref.shape
    feature = lax.broadcasted_iota(jnp.int32, (HEAD_DIM, length), 0)
    for r in range(rows):
        same = jnp.where(feature == ids_ref[r : r + 1] + 1, 1.0, 0.0)
        ones = jnp.where(jnp.logical_and(feature >= SEGMENTS, feature < SEGMENTS + 3), 1.0, same)
        keyf_ref[r] = ones.T.astype(bf16)
    size = blocks_ref.shape[2]
    feature = lax.broadcasted_iota(jnp.int32, (HEAD_DIM, size), 0)
    for b in range(blocks_ref.shape[0]):
        other = jnp.logical_and(feature < SEGMENTS, feature != blocks_ref[b] + 1)
        queryf_ref[b] = jnp.where(other, MASK_STEP, 0.0).astype(bf16)


def prepare_wide(place, up, down, ids, id_blocks, hidden):
    depth = up.shape[0]
    rows, length = ids.shape
    shapes = [
        (hidden, depth), (hidden, depth), (rows, length, HEAD_DIM),
        (id_blocks.shape[0], HEAD_DIM, id_blocks.shape[2]),
    ]
    return pl.pallas_call(
        functools.partial(prepare_wide_kernel, FF_LIVE // HEADS_LIVE),
        grid_spec=pltpu.PrefetchScalarGridSpec(
            num_scalar_prefetch=1,
            grid=(1,),
            in_specs=[whole(v.shape) for v in (up, down, ids, id_blocks)],
            out_specs=[whole(shape) for shape in shapes],
        ),
        out_shape=[jax.ShapeDtypeStruct(shape, bf16) for shape in shapes],
        compiler_params=limit(60),
        name="prepare_wide",
    )(place, up, down, ids, id_blocks)


def assemble_kernel(parts, share, place, *refs):
    sources, (out_ref, *rest) = refs[: len(parts)], refs[len(parts) :]
    buffers, sems = rest[:-1], rest[-1]
    inward, outward = [], []
    for index, (slot, first) in enumerate(parts):
        rows = buffers[index].shape[0]
        start = pl.multiple_of((place[2] ^ slot) * share + first, 8)
        inward.append(pltpu.make_async_copy(sources[index], buffers[index], sems.at[0, index]))
        outward.append(
            pltpu.make_async_copy(buffers[index], out_ref.at[pl.ds(start, rows)], sems.at[1, index])
        )
    for copy in inward:
        copy.start()
    for into, out in zip(inward, outward):
        into.wait()
        out.start()
    for copy in outward:
        copy.wait()


def assemble(place, pieces, share, total):
    depth = pieces[0][2].shape[1]
    arrays = [piece[2] for piece in pieces]
    parts = tuple(piece[:2] for piece in pieces)
    return pl.pallas_call(
        functools.partial(assemble_kernel, parts, share),
        grid_spec=pltpu.PrefetchScalarGridSpec(
            num_scalar_prefetch=1,
            grid=(1,),
            in_specs=[ANYWHERE] * len(arrays),
            out_specs=ANYWHERE,
            scratch_shapes=[pltpu.VMEM(v.shape, v.dtype) for v in arrays]
            + [pltpu.SemaphoreType.DMA((2, len(arrays)))],
        ),
        out_shape=jax.ShapeDtypeStruct((total, depth), arrays[0].dtype),
        cost_estimate=cost(0),
        compiler_params=limit(12),
        name="assemble",
    )(place, *arrays)


QUARTERS = 4


def collect(place, refs, buffer):
    share = refs[0].shape[0]
    number = place[4 + SLOT_COUNT] * len(refs) // QUARTERS
    for far, ref in enumerate(refs):
        start = (number ^ far) * share
        buffer[pl.ds(pl.multiple_of(start, 8), share)] = ref[...].astype(f32)


def finish_up_kernel(place, *refs):
    pieces, (grad_ref, bias_ref, buffer) = refs[:-3], refs[-3:]
    collect(place, pieces, buffer)
    depth, slots = grad_ref.shape
    hidden = buffer.shape[0] - HIDDEN_EXTRA
    grad_ref[:, 0:hidden] = buffer[0:hidden].T
    if slots > hidden:
        grad_ref[:, hidden:] = jnp.zeros((depth, slots - hidden), f32)
    bias_ref[...] = buffer[hidden : hidden + 8]


def finish_down_kernel(per_head, place, *refs):
    pieces, (grad_ref, out_ref, extra_ref, buffer) = refs[:-4], refs[-4:]
    collect(place, pieces, buffer)
    width = out_ref.shape[0]
    hidden = buffer.shape[0] - HIDDEN_EXTRA - width
    row = lax.broadcasted_iota(jnp.int32, (hidden, buffer.shape[1]), 0)
    grad_ref[0:hidden] = jnp.where(row < place[3] * per_head, buffer[0:hidden], 0.0)
    if grad_ref.shape[0] > hidden:
        grad_ref[hidden:] = jnp.zeros((grad_ref.shape[0] - hidden, buffer.shape[1]), f32)
    out_ref[...] = buffer[hidden : hidden + width]
    extra_ref[...] = buffer[hidden + width : hidden + width + 8]


def finish_attn_kernel(place, *refs):
    pieces, (query_ref, key_ref, value_ref, extra_ref, buffer) = refs[:QUARTERS], refs[QUARTERS:]
    collect(place, pieces, buffer)
    width = query_ref.shape[0]
    for index, ref in enumerate((query_ref, key_ref, value_ref)):
        ref[...] = buffer[index * width : (index + 1) * width]
    extra_ref[...] = buffer[3 * width : 3 * width + 8]


def finish(kernel, place, pieces, shapes, name):
    rows, depth = pieces[0].shape[0] * len(pieces), pieces[0].shape[1]
    return pl.pallas_call(
        kernel,
        grid_spec=pltpu.PrefetchScalarGridSpec(
            num_scalar_prefetch=1,
            grid=(1,),
            in_specs=[whole(v.shape) for v in pieces],
            out_specs=[whole(shape) for shape in shapes],
            scratch_shapes=[pltpu.VMEM((rows, depth), f32)],
        ),
        out_shape=[jax.ShapeDtypeStruct(shape, f32) for shape in shapes],
        cost_estimate=cost(0),
        compiler_params=limit(20),
        name=name,
    )(place, *pieces)


def shares_kernel(distances, group, place, *refs):
    step = pl.program_id(0)
    steps = pl.num_programs(0)
    count = len(distances)
    sources, blocksum_ref, (own_ref, *sent_refs) = refs[:count], refs[count], refs[count + 1 :]
    rows_touched = (place[0] + steps - 1) // place[1] - place[0] // place[1] + 1
    for distance, source, target in zip(distances, sources, (own_ref, *sent_refs)):
        block = (place[2] ^ distance) * steps + step - place[0] // place[1] * place[1]
        inside = jnp.logical_and(block >= 0, block < rows_touched * place[1])
        value = jnp.where(inside, source[0].astype(f32), 0.0)
        if distance == 0:
            target[0] = blocksum_ref[0] + value
        else:
            target[0] = value.astype(bf16)


def shares(place, rowsum, blocksum, distances):
    steps, size, depth = blocksum.shape
    group = None
    window = rowsum.reshape(-1, size, depth)

    def source(distance):
        def index(b, place):
            block = (place[2] ^ distance) * steps + b - place[0] // place[1] * place[1]
            return jnp.clip(block, 0, window.shape[0] - 1), 0, 0

        return pl.BlockSpec((1, size, depth), index)

    block = pl.BlockSpec((1, size, depth), local)
    return pl.pallas_call(
        functools.partial(shares_kernel, distances, group),
        grid_spec=pltpu.PrefetchScalarGridSpec(
            num_scalar_prefetch=1,
            grid=(steps,),
            in_specs=[source(d) for d in distances] + [block],
            out_specs=[block for _ in distances],
        ),
        out_shape=[
            jax.ShapeDtypeStruct(blocksum.shape, bf16 if d else f32) for d in distances
        ],
        compiler_params=limit(12),
        name="shares",
    )(place, *[window for _ in distances], blocksum)


def row_chunks(count, body):
    chunk = 200 if count % 200 == 0 else 16

    @pl.loop(0, count // chunk)
    def _(i):
        body(pl.ds(pl.multiple_of(i * chunk, 8), chunk))

    if count % chunk:
        body(pl.ds(count // chunk * chunk, count % chunk))


def phi_parts(value):
    bell = jnp.exp2(value * value * (-0.5 / math.log(2.0)))
    t = 1.0 / (1.0 + jnp.abs(value) * (0.3275911 * 0.5**0.5))
    poly = t * (
        0.127414796
        + t * (-0.142248368 + t * (0.7107068705 + t * (-0.7265760135 + t * 0.5307027145)))
    )
    half = poly * bell
    return jnp.where(value >= 0, 1.0 - half, half), bell * (2.0 * math.pi) ** -0.5


def chunk_stats(value):
    centre = value - jnp.mean(value, axis=-1, keepdims=True)
    inverse = lax.rsqrt(jnp.mean(centre * centre, axis=-1, keepdims=True) + norm_eps)
    return centre * inverse, inverse


def fetch_slot(order, step, sources, buffers, sems):
    for which, (refs, buffer) in enumerate(zip(sources, buffers)):
        for position, slot in enumerate(order):

            @pl.when(step == position)
            def _():
                pltpu.make_async_copy(refs[slot], buffer.at[step % 2], sems.at[which, step % 2]).start()


def await_slot(step, sources, buffers, sems):
    for which, (refs, buffer) in enumerate(zip(sources, buffers)):
        pltpu.make_async_copy(refs[0], buffer.at[step % 2], sems.at[which, step % 2]).wait()


def stream_slots(order, sources, buffers, sems):
    step = pl.program_id(0)

    @pl.when(step == 0)
    def _():
        fetch_slot(order, step, sources, buffers, sems)

    @pl.when(step + 1 < pl.num_programs(0))
    def _():
        fetch_slot(order, step + 1, sources, buffers, sems)

    await_slot(step, sources, buffers, sems)


def fetch_slot(order, step, sources, buffers, sems, firsts):
    for which, (refs, buffer, first) in enumerate(zip(sources, buffers, firsts)):
        for position, slot in enumerate(order):

            @pl.when(step == position)
            def _():
                pltpu.make_async_copy(
                    refs[slot].at[pl.ds(first, buffer.shape[1])],
                    buffer.at[step % 2],
                    sems.at[which, step % 2],
                ).start()


def stream_slots(order, sources, buffers, sems, firsts):
    step = pl.program_id(0)

    @pl.when(step == 0)
    def _():
        fetch_slot(order, step, sources, buffers, sems, firsts)

    @pl.when(step + 1 < pl.num_programs(0))
    def _():
        fetch_slot(order, step + 1, sources, buffers, sems, firsts)

    for which, (refs, buffer, first) in enumerate(zip(sources, buffers, firsts)):
        pltpu.make_async_copy(
            refs[0].at[pl.ds(first, buffer.shape[1])], buffer.at[step % 2], sems.at[which, step % 2]
        ).wait()


def ffn_kernel(
    group, place, frames_ref, cot_ref, ids_ref, vec_ref, *refs,
):
    held = len(refs) - 15 - 3 * group
    context_refs, refs = refs[:held], refs[held:]
    weight_refs, refs = refs[:group], refs[group:]
    up_refs, down_refs = refs[:group], refs[group : 2 * group]
    (
        layer_ref, low_ref, normal_ref, inverse_ref, gradffn_ref, small_ref,
        active_ref, slope_ref, up_buf, down_buf, out_buf, bias_buf, mixed, sems, out_sems,
    ) = refs[2 * group :]
    turns = group // held
    step = pl.program_id(0)
    count, depth = mixed.shape
    hidden = active_ref.shape[2]
    width = out_buf.shape[1]
    out_bias, gain_one, shift_one = vec_ref[0:1], vec_ref[1:2], vec_ref[2:3]
    outer_bias, gain_two, shift_two = vec_ref[3:4], vec_ref[4:5], vec_ref[5:6]

    def out_copies(slot):
        return [
            pltpu.make_async_copy(
                weight_refs[slot].at[pl.ds(first, target.shape[1])], target.at[slot], out_sems.at[which, slot]
            )
            for which, (target, first) in enumerate(
                ((out_buf, 3 * width + BIAS_ROWS), (bias_buf, 3 * width))
            )
        ]

    @pl.when(step == 0)
    def _():
        for slot in range(group):
            for copy in out_copies(slot):
                copy.start()

    stream_slots(tuple(range(group)), (up_refs, down_refs), (up_buf, down_buf), sems, (0, 0))

    @pl.when(step == 0)
    def _():
        for slot in range(group):
            for copy in out_copies(slot):
                copy.wait()
        _, blocks, _, size = context_refs[0].shape
        for block in range(blocks):
            total = dot(context_refs[0][0, block], out_buf[0], 0, 0)
            for slot in range(1, group):
                total += dot(context_refs[slot // turns][slot % turns, block], out_buf[slot], 0, 0)
            mixed[block * size : (block + 1) * size] = total

        def first(rows):
            hidden_one = frames_ref[0, rows].astype(f32) + mixed[rows] + out_bias
            normal, inverse = chunk_stats(hidden_one)
            normal_ref[rows] = normal.astype(bf16)
            inverse_ref[rows] = inverse
            normed = normal * gain_one + shift_one
            low_ref[rows] = normed.astype(bf16)
            mixed[rows] = normed + outer_bias

        row_chunks(count, first)

    biases = bias_buf[step].astype(f32)
    bias = jnp.concatenate([bias_row(biases, 2), bias_row(biases, 3)[:, 0 : hidden - depth]], axis=1)
    up_now, down_now = up_buf[step % 2], down_buf[step % 2]

    def gelu(rows):
        value = dot(low_ref[rows], up_now, 1, 1) + bias
        whole_part, bell = phi_parts(value)
        active = (value * whole_part).astype(bf16)
        active_ref[0, rows] = active
        slope_ref[0, rows] = (whole_part + value * bell).astype(bf16)
        mixed[rows] += dot(active, down_now, 1, 0)

    gelu(slice(None))

    @pl.when(step == pl.num_programs(0) - 1)
    def _():
        small_ref[...] = jnp.zeros_like(small_ref)

        def last(rows):
            normal, inverse = chunk_stats(mixed[rows])
            live = (ids_ref[rows] >= 0).astype(f32)
            layer_ref[rows] = ((normal * gain_two + shift_two) * live).astype(bf16)
            grad = cot_ref[0, rows].astype(f32) * live
            small_ref[0:1] += jnp.sum(grad * normal, axis=0, keepdims=True)
            small_ref[1:2] += jnp.sum(grad, axis=0, keepdims=True)
            scaled = grad * gain_two
            back = inverse * (
                scaled
                - jnp.mean(scaled, axis=-1, keepdims=True)
                - normal * jnp.mean(scaled * normal, axis=-1, keepdims=True)
            )
            small_ref[2:3] += jnp.sum(back, axis=0, keepdims=True)
            gradffn_ref[rows] = back.astype(bf16)

        row_chunks(count, last)


def up_back_kernel(
    order, last, group, low_ref, normal_ref, inverse_ref, before_ref, gradffn_ref, slope_ref,
    gain_ref, *refs,
):
    up_refs, down_refs, rest = refs[:group], refs[group : 2 * group], refs[2 * group :]
    if last:
        upgrad_ref, small_ref, gradone_ref, gradattn_ref, *rest = rest
    else:
        upgrad_ref, normed_grad, *rest = rest
    up_buf, down_buf, inner, sems, *rest = rest
    if last:
        normed_grad = rest[0]
    step = pl.program_id(0)
    count, hidden = inner.shape
    depth = low_ref.shape[1]
    stream_slots(order, (up_refs, down_refs), (up_buf, down_buf), sems, (0, 0))

    @pl.when(step == 0)
    def _():
        normed_grad[...] = before_ref[...] if last else gradffn_ref[...].astype(f32)

    grad_active = dot(gradffn_ref[...], down_buf[step % 2], 1, 1)
    inner[...] = (grad_active * slope_ref[0].astype(f32)).astype(bf16)
    upgrad_ref[0, 0:hidden] = dot(inner[...], low_ref[...], 0, 0).astype(bf16)
    ones = jnp.ones((8, count), bf16)
    bias = dot(ones, inner[...], 1, 0)
    row = lax.broadcasted_iota(jnp.int32, (upgrad_ref.shape[1] - hidden, depth), 0)
    extra = jnp.where(row == 0, bias[0:1, 0:depth], 0.0)
    rest_lanes = jnp.pad(bias[0:1, depth:hidden], ((0, 0), (0, 2 * depth - hidden)))
    upgrad_ref[0, hidden:] = jnp.where(row == 1, rest_lanes, extra).astype(bf16)
    normed_grad[...] += dot(inner[...], up_buf[step % 2], 1, 0)

    if last:

        @pl.when(step == pl.num_programs(0) - 1)
        def _():
            small_ref[...] = jnp.zeros_like(small_ref)
            gain = gain_ref[...]

            def last_rows(rows):
                grad, normal = normed_grad[rows], normal_ref[rows].astype(f32)
                small_ref[0:1] += jnp.sum(grad * normal, axis=0, keepdims=True)
                small_ref[1:2] += jnp.sum(grad, axis=0, keepdims=True)
                scaled = grad * gain
                back = inverse_ref[rows] * (
                    scaled
                    - jnp.mean(scaled, axis=-1, keepdims=True)
                    - normal * jnp.mean(scaled * normal, axis=-1, keepdims=True)
                )
                small_ref[2:3] += jnp.sum(back, axis=0, keepdims=True)
                gradone_ref[rows] = back
                gradattn_ref[rows] = back.astype(bf16)

            row_chunks(count, last_rows)


def down_back_kernel(
    order, group, active_ref, gradffn_ref, gradattn_ref, small_ref, smalltwo_ref, *refs
):
    context_refs, result_ref = refs[:-1], refs[-1]
    turns = group // len(context_refs)
    step = pl.program_id(0)
    hidden = active_ref.shape[2]
    depth = gradffn_ref.shape[1]
    _, blocks, width, size = context_refs[0].shape
    result_ref[0, 0:hidden] = dot(active_ref[0], gradffn_ref[...], 0, 0).astype(bf16)
    for position, slot in enumerate(order):

        @pl.when(step == position)
        def _():
            context = context_refs[slot // turns].at[slot % turns]
            total = dot(context[0], gradattn_ref[0:size], 1, 0)
            for block in range(1, blocks):
                total += dot(context[block], gradattn_ref[block * size : (block + 1) * size], 1, 0)
            result_ref[0, hidden : hidden + width] = total.astype(bf16)

    row = lax.broadcasted_iota(jnp.int32, (HIDDEN_EXTRA, depth), 0)
    extra = jnp.zeros((HIDDEN_EXTRA, depth), f32)
    for index in range(3):
        extra = jnp.where(row == index, small_ref[index : index + 1], extra)
        extra = jnp.where(row == 3 + index, smalltwo_ref[index : index + 1], extra)
    result_ref[0, hidden + width :] = extra.astype(bf16)


def ffn(place, frames, cotangent, ids, vectors, contexts, weights, up, down):
    group = len(up)
    count, depth = frames.shape[1:]
    hidden = down[0].shape[0]
    width = contexts[0].shape[2]
    own = pl.BlockSpec((1, count, depth), lambda s, place: (place[2], 0, 0))
    per_slot = pl.BlockSpec((1, count, hidden), lambda s, place: (s, 0, 0))
    spec = pltpu.PrefetchScalarGridSpec(
        num_scalar_prefetch=1,
        grid=(group,),
        in_specs=[own, own, whole(ids.shape), whole(vectors.shape)]
        + [whole(contexts[0].shape)] * len(contexts)
        + [ANYWHERE] * (3 * group),
        out_specs=[
            whole((count, depth)), whole((count, depth)), whole((count, depth)), whole((count, 1)),
            whole((count, depth)), whole((8, depth)), per_slot, per_slot,
        ],
        scratch_shapes=[
            pltpu.VMEM((2, hidden, depth), bf16),
            pltpu.VMEM((2, hidden, depth), bf16),
            pltpu.VMEM((group, width, depth), bf16),
            pltpu.VMEM((group, BIAS_ROWS, depth), bf16),
            pltpu.VMEM((count, depth), f32),
            pltpu.SemaphoreType.DMA((2, 2)),
            pltpu.SemaphoreType.DMA((2, group)),
        ],
    )
    shape = jax.ShapeDtypeStruct
    return pl.pallas_call(
        functools.partial(ffn_kernel, group),
        grid_spec=spec,
        out_shape=[
            shape((count, depth), bf16), shape((count, depth), bf16), shape((count, depth), bf16),
            shape((count, 1), f32), shape((count, depth), bf16), shape((8, depth), f32), shape((group, count, hidden), bf16),
            shape((group, count, hidden), bf16),
        ],
        cost_estimate=cost(2**34),
        compiler_params=limit(28),
        name="ffn",
    )(
        place, far_away(frames), far_away(cotangent), ids, vectors, *map(far_away, contexts), *map(far_away, weights),
        *up, *down,
    )


def in_order(order):
    def slot_of(s):
        result = jnp.int32(order[-1])
        for position in reversed(range(len(order) - 1)):
            result = jnp.where(s == position, order[position], result)
        return result

    return slot_of


def everything(shape):
    return pl.BlockSpec(shape, lambda s: (0,) * len(shape))


def up_back(order, last, low, normal, inverse, before, gradffn, slope, gain, up, down):
    group = len(up)
    count, depth = low.shape
    hidden = slope.shape[2]
    slot_of = in_order(order)
    per_slot = pl.BlockSpec((1, count, hidden), lambda s: (slot_of(s), 0, 0))
    rows = hidden + HIDDEN_EXTRA
    shape = jax.ShapeDtypeStruct
    wide = shape((count, depth), f32)
    tail = [shape((8, depth), f32), wide, shape((count, depth), bf16)] if last else [wide]
    return pl.pallas_call(
        functools.partial(up_back_kernel, order, last, group),
        grid=(len(order),),
        in_specs=[
            everything(v.shape) for v in (low, normal, inverse, before, gradffn)
        ]
        + [per_slot, everything(gain.shape)]
        + [ANYWHERE] * (2 * group),
        out_specs=[pl.BlockSpec((1, rows, depth), lambda s: (s, 0, 0))]
        + [everything(t.shape) for t in tail],
        out_shape=[shape((len(order), rows, depth), bf16)] + tail,
        scratch_shapes=[
            pltpu.VMEM((2, hidden, depth), bf16),
            pltpu.VMEM((2, hidden, depth), bf16),
            pltpu.VMEM((count, hidden), bf16),
            pltpu.SemaphoreType.DMA((2, 2)),
        ]
        + ([pltpu.VMEM((count, depth), f32)] if last else []),
        cost_estimate=cost(2**33),
        compiler_params=limit(26),
        name="up_back",
    )(low, normal, inverse, before, gradffn, slope, gain, *up, *down)


def down_back(order, active, gradffn, gradattn, smalls, contexts):
    count, hidden = active.shape[1:]
    depth = gradffn.shape[1]
    width = contexts[0].shape[2]
    slot_of = in_order(order)
    rows = hidden + width + HIDDEN_EXTRA
    return pl.pallas_call(
        functools.partial(down_back_kernel, order, active.shape[0]),
        grid=(len(order),),
        in_specs=[pl.BlockSpec((1, count, hidden), lambda s: (slot_of(s), 0, 0))]
        + [everything(v.shape) for v in (gradffn, gradattn, *smalls, *contexts)],
        out_specs=pl.BlockSpec((1, rows, depth), lambda s: (s, 0, 0)),
        out_shape=jax.ShapeDtypeStruct((len(order), rows, depth), bf16),
        cost_estimate=cost(2**32),
        compiler_params=limit(20),
        name="down_back",
    )(active, gradffn, gradattn, *smalls, *contexts)


def swap(value, axis, distance):
    size = lax.axis_size(axis)
    return lax.ppermute(value, axis, [(i, i ^ distance) for i in range(size)])


def add_low(a, b):
    return (a.astype(f32) + b.astype(f32)).astype(bf16)


def add_three(a, b, c):
    return (a.astype(f32) + b.astype(f32) + c.astype(f32)).astype(bf16)


def hold(value, *others):
    return lax.optimization_barrier((value,) + tuple(others))[0]


def row_distances(size):
    distance, result = 1, []
    while distance < size:
        result.append(distance)
        distance *= 2
    return result


def join_rows(value, arrived, distance):
    upper = (lax.axis_index("rows") // distance) % 2 == 1
    return jnp.concatenate(
        [jnp.where(upper, arrived, value), jnp.where(upper, value, arrived)], axis=0
    )


def far_swap(value, far):
    return swap(value, "rows", (far & 1) * 2 + (far >> 1))


def own_quarter():
    here = lax.axis_index("rows")
    return here % 2 * 2 + here // 2 % 2


def quarters_of(value, axis=0):
    rows = value.shape[axis] // QUARTERS
    return [
        lax.dynamic_slice_in_dim(value, (own_quarter() ^ far) * rows, rows, axis)
        for far in range(QUARTERS)
    ]


def send_quarters(quarters):
    return [far_swap(quarters[far], far) for far in range(1, QUARTERS)]


def add_quarters(quarters, came):
    total = quarters[0].astype(f32)
    for value in came:
        total = total + value.astype(f32)
    return total.astype(bf16)


def join_pieces(pieces):
    near = [join_rows(pieces[i], pieces[i + 1], 2) for i in (0, 2)]
    return join_rows(near[0], near[1], 1)


def across(value, came, distances):
    value = add_low(value, came)
    for distance in distances:
        value = add_low(value, swap(value, "rows", distance))
    return value


def gather_slots(value):
    slots = {0: value}
    distance = lax.axis_size("heads") // 2
    while distance >= 1:
        for slot in list(slots):
            slots[slot ^ distance] = swap(slots[slot], "heads", distance)
        distance //= 2
    return [slots[slot] for slot in range(len(slots))]


def per_device(
    frames, segment_ids, cotangent, query_weight, query_bias, key_weight, value_weight, value_bias,
    output_weight, output_bias, first_gain, first_shift, inner_weight, inner_bias, outer_weight,
    outer_bias, second_gain, second_shift,
):
    group = lax.axis_size("heads")
    position = lax.axis_index("heads")
    row_count, row_length, depth = frames.shape
    own_len = row_count * row_length // group
    size = math.gcd(row_length, own_len)
    steps = own_len // size
    per_row = row_length // size
    width = query_weight.shape[1]
    heads_here = width // HEAD_DIM
    per_head = FF_LIVE // HEADS_LIVE
    hidden_slots = inner_weight.shape[1]
    hidden_cap = min(hidden_slots, (HEADS_LIVE + group - 1) // group * per_head)

    def live_of(index):
        return HEADS_LIVE // group + (index < HEADS_LIVE % group).astype(jnp.int32)

    rest = row_distances(lax.axis_size("rows"))[2:]
    piece_rows = hidden_cap // QUARTERS
    place = jnp.stack(
        [position * steps, jnp.int32(per_row), position]
        + [live_of(position ^ slot) for slot in range(group)]
        + [own_quarter() * piece_rows, own_quarter()]
    )
    blocks = frames.reshape(row_count * per_row, size, depth)
    weight_own, piece = prepare(
        place, query_weight.T, key_weight.T, value_weight.T, query_bias, value_bias,
        inner_bias, output_weight, outer_weight, piece_rows,
    )
    weight = {0: weight_own, 1: swap(weight_own, "heads", 1), 2: swap(weight_own, "heads", 2)}
    piece = swap(piece, "heads", 2)
    up_own, down_own, keyf, queryf = prepare_wide(
        place, inner_weight, outer_weight, segment_ids,
        segment_ids.reshape(row_count * per_row, 1, size), hidden_cap,
    )
    up = {0: up_own, 1: swap(up_own, "heads", 1)}
    down = {0: down_own, 1: swap(down_own, "heads", 1)}
    half = group // 2

    def forward(first, *waits):
        return attend(
            first, place, hold(blocks, *waits), frames,
            [weight[slot] for slot in range(first, first + half)], keyf, queryf, steps, width,
        )

    saved = [forward(0)]
    done = saved[0][0]
    weight[2], piece, done = lax.optimization_barrier((weight[2], piece, done))
    weight[3] = swap(weight[2], "heads", 1)
    up[2] = swap(hold(up_own, weight[2]), "heads", 2)
    piece = hold(piece, weight[2])
    pieces = [piece] + send_quarters([piece] * QUARTERS)
    saved.append(forward(half, done))
    down[2] = join_pieces(hold(pieces, saved[1][0]))
    up[3] = swap(up[2], "heads", 1)
    down[3] = swap(down[2], "heads", 1)
    up = [up[slot] for slot in range(group)]
    down = [down[slot] for slot in range(group)]
    contexts = [kept[3] for kept in saved]

    vectors = jnp.stack(
        [output_bias, first_gain, first_shift, outer_bias, second_gain, second_shift]
    )
    whole_frames = frames.reshape(group, own_len, depth)
    whole_cot = cotangent.reshape(group, own_len, depth)
    flat_ids = segment_ids.reshape(row_count * row_length)
    ids_own = lax.dynamic_slice_in_dim(flat_ids, position * own_len, own_len)[:, None]
    layer_own, normed_low, normal_one, inverse_one, grad_ffn, small_two, actives, slopes = ffn(
        place, whole_frames, whole_cot, ids_own, vectors, contexts,
        [weight[slot] for slot in range(group)], up, down,
    )
    layer = {0: layer_own, 1: swap(layer_own, "heads", 1), 2: swap(layer_own, "heads", 2)}
    known = (normed_low, normal_one, inverse_one)
    gain = first_gain[None]
    up_send, grad_part = up_back((1, 3), False, *known, inverse_one, grad_ffn, slopes, gain, up, down)
    up_came = swap(up_send, "heads", 1)
    layer[1] = hold(layer[1], grad_part)
    up_keep, small_one, grad_hidden_one, grad_attn = up_back(
        (0, 2), True, *known, grad_part, grad_ffn, slopes, gain, up, down
    )
    barrier = lax.optimization_barrier
    up_quarters = quarters_of(add_low(up_keep, up_came), 1)
    up_came = send_quarters(up_quarters)

    smalls = (small_one, small_two)
    down_send = down_back((1, 3), actives, hold(grad_ffn, up_quarters), grad_attn, smalls, contexts)
    down_came = swap(down_send, "heads", 1)
    down_keep = down_back((0, 2), actives, hold(grad_ffn, down_send), grad_attn, smalls, contexts)
    down_came = hold(down_came, down_keep)
    grad_attn = grad_attn.reshape(steps, size, depth)
    block_sum = grad_hidden_one.reshape(steps, size, depth)
    row_sum = jnp.zeros((8, 128), bf16)
    grads = {}

    def back(slot, first, block_sum, row_sum, *waits):
        return attend_back(
            slot, first, place, blocks, frames, weight[slot], saved[slot // half], grad_attn,
            hold(block_sum, *waits), row_sum,
        )

    layer[2] = hold(layer[2], down_keep)
    layer[3] = swap(layer[2], "heads", 1)
    down_two = add_low(down_keep[1], down_came[1])
    cut = down_two.shape[0] * 9 // 16 // 8 * 8
    down_first = swap(hold(down_two[:cut], layer[2]), "heads", 2)
    grads[3], block_sum, row_sum = back(3, True, block_sum, row_sum, layer[2], down_two)

    block_sum, up_came, down_first, layer[3], grads[3] = barrier(
        (block_sum, up_came, down_first, layer[3], grads[3])
    )
    down_second = swap(hold(down_two[cut:], down_first), "heads", 2)
    grads_came = swap(grads[3], "heads", 1)
    up_pair = add_quarters(up_quarters, up_came)
    up_came = swap(up_pair[1], "heads", 2)
    grads[2], block_sum, row_sum = back(2, False, block_sum, row_sum, up_pair)

    block_sum, up_came, down_second, grads_came, grads[2] = barrier(
        (block_sum, up_came, down_second, grads_came, grads[2])
    )
    attn_two = add_low(grads[2], grads_came)
    attn_rows = attn_two.shape[0] // 2
    attn_first = swap(attn_two[:attn_rows], "heads", 2)
    up_piece = add_low(up_pair[0], up_came)
    up_came = swap(up_piece, "rows", rest[0])
    down_far = jnp.concatenate([down_first, down_second])
    down_quarters = quarters_of(add_three(down_keep[0], down_came[0], down_far))
    down_came = send_quarters(down_quarters)
    grads[1], block_sum, row_sum = back(
        1, False, block_sum, row_sum, attn_two, up_piece, down_quarters
    )

    block_sum, up_came, down_came, attn_first, grads[1] = barrier(
        (block_sum, up_came, down_came, attn_first, grads[1])
    )
    grads_came = swap(grads[1], "heads", 1)
    up_piece = across(up_piece, up_came, rest[1:])
    attn_second = swap(hold(attn_two[attn_rows:], attn_first), "heads", 2)
    up_came = swap(up_piece, "rows", 2)
    down_piece = add_quarters(down_quarters, down_came)
    down_came = swap(down_piece, "rows", rest[0])
    grads[0], block_sum, row_sum = back(0, False, block_sum, row_sum, up_piece, down_piece)
    block_sum, up_came, down_came, attn_second, grads_came, grads[0] = barrier(
        (block_sum, up_came, down_came, attn_second, grads_came, grads[0])
    )

    reach, pairs = [0], {}
    for distance in range(1, group):
        pairs[distance] = []
        for i in range(group):
            j = i ^ distance
            rows_i = range(i * steps // per_row, ((i + 1) * steps - 1) // per_row + 1)
            rows_j = range(j * steps // per_row, ((j + 1) * steps - 1) // per_row + 1)
            if set(rows_i) & set(rows_j):
                pairs[distance].append((i, j))
        if pairs[distance]:
            reach.append(distance)
    own_grad, *owed = shares(place, row_sum, block_sum, tuple(reach))
    attn_two = jnp.concatenate([attn_first, attn_second])
    attn_quarters = quarters_of(add_three(hold(grads[0], owed), grads_came, attn_two))
    owed = [
        lax.ppermute(sent, "heads", pairs[distance]) for distance, sent in zip(reach[1:], owed)
    ]
    attn_came = send_quarters(attn_quarters)
    up_half = join_rows(up_piece, hold(up_came, own_grad), 2)
    down_piece = across(down_piece, hold(down_came, own_grad), rest[1:])
    layer[0] = hold(layer[0], own_grad)
    layer_out = assemble(
        place, [(slot, 0, layer[slot]) for slot in range(group)], own_len, row_count * row_length
    ).reshape(frames.shape)
    attn_came, owed, layer_out, up_half, down_piece = barrier(
        (attn_came, owed, layer_out, up_half, down_piece)
    )

    attn_piece = add_quarters(attn_quarters, attn_came)
    attn_came = swap(attn_piece, "rows", rest[0])
    up_came = swap(hold(up_half, attn_piece), "rows", 1)
    for came in owed:
        own_grad = own_grad + hold(came, attn_piece).astype(f32)
    own_grad = own_grad.astype(bf16).reshape(own_len, depth)
    cut = own_len // 2 // 8 * 8
    first_cut = swap(own_grad[:cut], "heads", 2)
    mate = swap(own_grad, "heads", 1)
    attn_came, first_cut, mate, up_came = barrier((attn_came, first_cut, mate, up_came))

    attn_piece = across(attn_piece, attn_came, rest[1:])
    attn_came = send_quarters([attn_piece] * QUARTERS)
    second_cut = swap(hold(own_grad[cut:], attn_piece), "heads", 2)
    down_came = send_quarters([hold(down_piece, attn_piece)] * QUARTERS)
    up_done = finish(
        finish_up_kernel, place, [hold(up_half, attn_piece), up_came],
        [(depth, hidden_slots), (8, depth)], "finish_up",
    )
    second_cut, up_done, attn_came = barrier((second_cut, up_done, attn_came))
    second_mate = swap(second_cut, "heads", 1)
    first_mate = swap(hold(first_cut, second_cut), "heads", 1)
    attn_done = finish(
        finish_attn_kernel, place, [attn_piece, *attn_came],
        [(width, depth)] * 3 + [(8, depth)], "finish_attn",
    )
    frames_grad = assemble(
        place,
        [
            (0, 0, own_grad), (1, 0, mate), (2, 0, first_cut), (2, cut, second_cut),
            (3, 0, first_mate), (3, cut, second_mate),
        ],
        own_len, row_count * row_length,
    ).reshape(frames.shape)
    down_done = finish(
        functools.partial(finish_down_kernel, per_head), place,
        [down_piece, *hold(down_came, frames_grad)],
        [(hidden_slots, depth), (width, depth), (8, depth)], "finish_down",
    )

    innerbias = jnp.concatenate([up_done[1][0], up_done[1][1, : hidden_cap - depth]])
    innerbias_full = jnp.pad(innerbias, ((0, hidden_slots - hidden_cap),))
    extra = attn_done[3]
    small = down_done[2]
    return (
        layer_out,
        frames_grad,
        attn_done[0].T,
        extra[0, :width],
        attn_done[1].T,
        attn_done[2].T,
        extra[1, :width],
        down_done[1],
        small[2],
        small[0],
        small[1],
        up_done[0],
        innerbias_full,
        down_done[0],
        small[5],
        small[3],
        small[4],
    )


def solution(mesh):
    in_specs = (
        P("rows", None, None), P("rows", None), P("rows", None, None), P(None, "heads"), P("heads"),
        P(None, "heads"), P(None, "heads"), P("heads"), P("heads", None), P(), P(), P(),
        P(None, "heads"), P("heads"), P("heads", None), P(), P(), P(),
    )
    out_specs = (
        P("rows", None, None), P("rows", None, None), P(None, "heads"), P("heads"), P(None, "heads"),
        P(None, "heads"), P("heads"), P("heads", None), P(), P(), P(), P(None, "heads"), P("heads"),
        P("heads", None), P(), P(), P(),
    )
    return jax.shard_map(
        per_device, mesh=mesh, in_specs=in_specs, out_specs=out_specs, check_vma=False
    )
```
